32 devices in a mesh: rep: 4 (over x, core), fsdp: 8 (over z, y).
Axes of the slice: x: 2, y: 2, z: 4, core: 2. Of those that a mesh axis runs over, the one named last changes fastest.
Arguments:
- tokens: bfloat16 [64, 512, 1024], P('rep', 'fsdp'), may hold values from -6 to 6
- cotangent: bfloat16 [64, 512, 1024], P('rep', 'fsdp'), may hold values from -6 to 6
- lengths: int32 [4, 16], P('rep'), may hold values from 1 to 512, as said below
- deal: int32 [4, 16], P('rep'), may hold values from 0 to 15, each once within a row
- norm_gain: bfloat16 [1024], P('fsdp'), may hold values from 0.099609375 to 1.8984375
- in_weight: bfloat16 [1024, 3072], P('fsdp'), may hold values from -0.1875 to 0.1875
- conv_weight: bfloat16 [1024, 3], P('fsdp'), may hold values from -3 to 3
- out_weight: bfloat16 [1024, 1024], P('fsdp'), may hold values from -0.1875 to 0.1875
- ffn_gain: bfloat16 [1024], P('fsdp'), may hold values from 0.099609375 to 1.8984375
- gate_weight: bfloat16 [1024, 4608], P('fsdp'), may hold values from -0.1875 to 0.1875
- up_weight: bfloat16 [1024, 4608], P('fsdp'), may hold values from -0.1875 to 0.1875
- down_weight: bfloat16 [4608, 1024], P('fsdp'), may hold values from -0.1875 to 0.1875
Outputs:
- block_out: bfloat16 [64, 512, 1024], P('rep', 'fsdp')
- block_grad: bfloat16 [64, 512, 1024], P('rep', 'fsdp')
- norm_gain_grad: float32 [1024], P('fsdp')
- in_grad: float32 [1024, 3072], P('fsdp')
- conv_grad: float32 [1024, 3], P('fsdp')
- out_grad: float32 [1024, 1024], P('fsdp')
- ffn_gain_grad: float32 [1024], P('fsdp')
- gate_grad: float32 [1024, 4608], P('fsdp')
- up_grad: float32 [1024, 4608], P('fsdp')
- down_grad: float32 [4608, 1024], P('fsdp')
The draws below stay inside these ranges and needn't reach their ends.
Inputs may be any that keep to these rules, and one draw needn't show every extreme that they name: In each row, the 2 lengths of slots 2 i to 2 i + 1 sum to at most 768; in each row one such set sums to exactly 768 and holds a length of exactly 512. `deal`: each row is a permutation of the group's sequence numbers.
All inputs are finite; a program needn't handle non-finite values.
Results may differ from the reference program's by a relative error of at most 0.018.
Values may be sent and summed in bfloat16 or wider, within the bound.
A program may use at most 256 MiB of HBM per device.

```python
import math
import jax
import jax.numpy as jnp
from jax import lax

D = 1024
FF = 4608
KER = 3
SLOT = 512
CAP_DEV = 768
GROUPS = 4
SEQS_G = 16
SEQS = 64


def draw_lengths(key, part):

    def one_group(group_index):
        group_key = jax.random.fold_in(key, group_index)
        key_full, key_total, key_first, key_swap = jax.random.split(group_key, 4)
        devices = SEQS_G // 2
        device_ids = jnp.arange(devices, dtype=jnp.int32)
        full_slot = jax.random.randint(key_full, (), 0, devices)
        totals = jax.random.randint(key_total, (devices,), CAP_DEV // 3, CAP_DEV + 1)
        totals = jnp.where(device_ids == full_slot, CAP_DEV, totals)
        low_end = jnp.maximum(1, totals - SLOT)
        high_end = jnp.minimum(SLOT, totals - 1)
        first_len = jax.random.randint(key_first, (devices,), low_end, high_end + 1)
        first_len = jnp.where(device_ids == full_slot, SLOT, first_len)
        second_len = totals - first_len
        swap_bit = jax.random.randint(key_swap, (devices,), 0, 2)
        left_len = jnp.where(swap_bit == 1, second_len, first_len)
        right_len = jnp.where(swap_bit == 1, first_len, second_len)
        return jnp.stack([left_len, right_len], axis=1).reshape(SEQS_G)
    return jax.vmap(one_group)(jnp.arange(GROUPS, dtype=jnp.int32)).astype(jnp.int32)


def steps_of(key, extent, shards, least, top_value):
    level = 1.0
    for axis_at, parts in shards:
        draws = jax.random.uniform(jax.random.fold_in(jax.random.fold_in(key, 6), axis_at), (parts,), jnp.float32, least / len(shards), top_value / len(shards))
        level = level * jnp.repeat(jnp.exp(draws), extent[axis_at] // parts).reshape((-1,) + (1,) * (len(extent) - 1 - axis_at))
    return level


def scatter_about(own_key, dims, spread, most, pieces=(), kind=jnp.bfloat16):
    entries = jax.random.normal(own_key, dims, jnp.float32) * spread
    if len(pieces) > 0:
        entries = steps_of(own_key, dims, pieces, -0.22, 0.18) * entries
    return jnp.clip(entries, min=-most, max=most).astype(kind)


def setup_inputs(seed: int = 0) -> dict:
    key_list = jax.random.split(jax.random.key(seed), 13)
    return {
        "tokens": scatter_about(key_list[0], (SEQS, SLOT, D), 1.0, 6.0, ((0, 4), (1, 8))),
        "cotangent": scatter_about(key_list[1], (SEQS, SLOT, D), 1.0, 6.0, ((0, 4), (1, 8))),
        "lengths": draw_lengths(jax.random.fold_in(key_list[12], 71), 0),
        "deal": jax.vmap(lambda own: jax.random.permutation(own, SEQS_G))(jax.random.split(key_list[3], GROUPS)).reshape((GROUPS, SEQS_G)).astype(jnp.int32),
        "norm_gain": jnp.clip(1.0 + 0.18 * jax.random.normal(key_list[4], (D,), jnp.float32), 0.099609375, 1.8984375).astype(jnp.bfloat16),
        "in_weight": scatter_about(key_list[5], (D, 3 * D), D ** -0.5, 0.1875, ((0, 8),)),
        "conv_weight": scatter_about(key_list[6], (D, KER), 0.6, 3.0, ((0, 8),)),
        "out_weight": scatter_about(key_list[7], (D, D), D ** -0.5, 0.1875, ((0, 8),)),
        "ffn_gain": jnp.clip(1.0 + 0.18 * jax.random.normal(key_list[8], (D,), jnp.float32), 0.099609375, 1.8984375).astype(jnp.bfloat16),
        "gate_weight": scatter_about(key_list[9], (D, FF), D ** -0.5, 0.1875, ((0, 8),)),
        "up_weight": scatter_about(key_list[10], (D, FF), D ** -0.5, 0.1875, ((0, 8),)),
        "down_weight": scatter_about(key_list[11], (FF, D), (FF // 4) ** -0.5, 0.1875, ((0, 8),)),
    }


EPS = 1e-05
HIGH = lax.Precision.HIGHEST

@jax.custom_vjp
def low(v):
    return lax.optimization_barrier(v.astype(jnp.bfloat16)).astype(jnp.float32)

@jax.custom_vjp
def low_back(v):
    return v

def low_keep(v):
    return (low(v), None)

def low_pass(kept, grad):
    return (grad,)

def back_keep(v):
    return (v, None)

def back_low(kept, grad):
    return (low(grad),)
low.defvjp(low_keep, low_pass)
low_back.defvjp(back_keep, back_low)

def rms_scaled(values, gain):
    return values * lax.rsqrt(lax.optimization_barrier(jnp.mean(values * values, axis=-1, keepdims=True)) + EPS) * gain

def project(values, matrix):
    return jnp.einsum('bsd,de->bse', values, matrix, precision=HIGH)

def block_forward(tokens_in, norm_gain, in_weight, conv_weight, out_weight, ffn_gain, gate_weight, up_weight, down_weight):
    normed_one = low(rms_scaled(tokens_in, norm_gain))
    projected = low_back(project(normed_one, in_weight))
    b_gate = projected[..., :D]
    c_gate = projected[..., D:2 * D]
    x_value = projected[..., 2 * D:]
    product = b_gate * x_value
    padded = jnp.pad(product, ((0, 0), (2, 0), (0, 0)))
    convolved = conv_weight[:, 0] * padded[:, :SLOT] + conv_weight[:, 1] * padded[:, 1:SLOT + 1] + conv_weight[:, 2] * padded[:, 2:]
    gated = low(c_gate * convolved)
    mixed = low_back(project(gated, out_weight))
    middle = tokens_in + mixed
    normed_two = low(rms_scaled(middle, ffn_gain))
    gate_lin = low_back(project(normed_two, gate_weight))
    up_lin = low_back(project(normed_two, up_weight))
    hidden = low(jax.nn.silu(gate_lin) * up_lin)
    ffn_out = low_back(project(hidden, down_weight))
    return middle + ffn_out

def reference(tokens, cotangent, lengths, deal, norm_gain, in_weight, conv_weight, out_weight, ffn_gain, gate_weight, up_weight, down_weight):

    def source_lengths(deal_row, length_row):
        return jnp.zeros((SEQS_G,), jnp.int32).at[deal_row].set(length_row)
    source_len = jax.vmap(source_lengths)(deal, lengths).reshape(SEQS)
    live = (jnp.arange(SLOT, dtype=jnp.int32)[None, :] < source_len[:, None]).astype(jnp.float32)[..., None]
    weights = tuple((matrix.astype(jnp.float32) for matrix in (norm_gain, in_weight, conv_weight, out_weight, ffn_gain, gate_weight, up_weight, down_weight)))
    group_size = math.gcd(SEQS, max(1, 4096 // SLOT))
    block_count = SEQS // group_size
    token_blocks = tokens.astype(jnp.float32).reshape(block_count, group_size, SLOT, D)
    cot_blocks = cotangent.astype(jnp.float32).reshape(block_count, group_size, SLOT, D)
    live_blocks = live.reshape(block_count, group_size, SLOT, 1)

    def visit(totals, block_data):
        tokens_block, cot_block, live_block = block_data
        output_block, pullback = jax.vjp(block_forward, tokens_block, *weights)
        grads = pullback(cot_block * live_block)
        new_totals = tuple((total_part + grad_part for total_part, grad_part in zip(totals, grads[1:])))
        return (new_totals, ((output_block * live_block).astype(jnp.bfloat16), (grads[0] * live_block).astype(jnp.bfloat16)))
    zeros = tuple((jnp.zeros(matrix.shape, jnp.float32) for matrix in weights))
    totals, (outputs, input_grads) = lax.scan(visit, zeros, (token_blocks, cot_blocks, live_blocks))
    block_out = outputs.reshape(SEQS, SLOT, D)
    block_grad = input_grads.reshape(SEQS, SLOT, D)
    return (block_out, block_grad, totals[0], totals[1], totals[2], totals[3], totals[4], totals[5], totals[6], totals[7])
```

```python
import jax
import jax.numpy as jnp
from jax import lax
from jax.sharding import PartitionSpec as P

EPS = 1e-05
F32 = jnp.float32
BF16 = jnp.bfloat16


def row_scale(values):
    return lax.rsqrt(jnp.mean(values * values, axis=-1, keepdims=True) + EPS)


def norm_back(grad_unit, unit_rows, scale_rows):
    return scale_rows * (
        grad_unit - unit_rows * jnp.mean(grad_unit * unit_rows, axis=-1, keepdims=True)
    )


def over_rows(left_side, right_side):
    return lax.dot_general(
        left_side, right_side, (((0,), (0,)), ((), ())), preferred_element_type=F32
    )


def over_cols(left_side, right_side):
    return lax.dot_general(
        left_side, right_side, (((1,), (1,)), ((), ())), preferred_element_type=F32
    )


def dot(left_side, right_side):
    return jnp.dot(left_side, right_side, preferred_element_type=F32)


def live_mask(lengths, deal, span):
    slots = jnp.arange(deal.shape[1], dtype=jnp.int32)
    picked = deal[0][:, None] == slots[None, :]
    source_len = jnp.sum(jnp.where(picked, lengths[0][:, None], 0), axis=0)
    position = lax.axis_index("fsdp") * span + jnp.arange(span, dtype=jnp.int32)
    return (position[None, :] < source_len[:, None]).astype(F32)[..., None]


def shift(values, amount):
    size = lax.axis_size("fsdp")
    pairs = [(i, i + amount) for i in range(size) if 0 <= i + amount < size]
    return lax.ppermute(values, "fsdp", pairs)


def body(
    tokens,
    cotangent,
    lengths,
    deal,
    norm_gain,
    in_weight,
    conv_weight,
    out_weight,
    ffn_gain,
    gate_weight,
    up_weight,
    down_weight,
):
    seqs, span, width = tokens.shape
    live = live_mask(lengths, deal, span)
    halo = shift(tokens[:, span - 2 :], 1)

    def gather(values):
        return lax.all_gather(values, "fsdp", axis=0, tiled=True)

    norm_gain, in_weight, conv_weight, out_weight = map(
        gather, (norm_gain, in_weight, conv_weight, out_weight)
    )
    ffn_gain, gate_weight, up_weight, down_weight = map(
        gather, (ffn_gain, gate_weight, up_weight, down_weight)
    )
    gain_one = norm_gain.astype(F32)
    gain_two = ffn_gain.astype(F32)
    taps = conv_weight.astype(F32)
    extended = jnp.concatenate([halo, tokens], axis=1).astype(F32)
    scale_ext = row_scale(extended)
    unit_ext = extended * scale_ext
    normed_ext = (unit_ext * gain_one).astype(BF16)
    projected = dot(normed_ext.reshape(-1, width), in_weight).reshape(seqs, span + 2, 3 * width)
    b_gate = projected[:, :, :width]
    c_gate = projected[:, 2:, width : 2 * width]
    x_value = projected[:, :, 2 * width :]
    product = b_gate * x_value
    lags = (product[:, :span], product[:, 1 : span + 1], product[:, 2:])
    convolved = taps[:, 0] * lags[0] + taps[:, 1] * lags[1] + taps[:, 2] * lags[2]
    gated = (c_gate * convolved).astype(BF16).reshape(-1, width)
    token_rows = tokens.astype(F32).reshape(-1, width)
    middle = token_rows + dot(gated, out_weight)
    scale_two = row_scale(middle)
    unit_two = middle * scale_two
    normed_two = (unit_two * gain_two).astype(BF16)
    grad_out = (cotangent.astype(F32) * live).reshape(-1, width)
    grad_ffn = grad_out.astype(BF16)
    gate_lin = dot(normed_two, gate_weight)
    up_lin = dot(normed_two, up_weight)
    sigma = jax.nn.sigmoid(gate_lin)
    hidden = (gate_lin * sigma * up_lin).astype(BF16)
    output = middle + dot(hidden, down_weight)
    down_grad = over_rows(hidden, grad_ffn)
    grad_hidden = over_cols(grad_ffn, down_weight)
    grad_gate = (grad_hidden * up_lin * sigma * (1.0 + gate_lin * (1.0 - sigma))).astype(BF16)
    grad_up = (grad_hidden * gate_lin * sigma).astype(BF16)
    gate_grad = over_rows(normed_two, grad_gate)
    up_grad = over_rows(normed_two, grad_up)
    grad_normed_two = over_cols(grad_gate, gate_weight) + over_cols(grad_up, up_weight)
    ffn_gain_grad = jnp.sum(grad_normed_two * unit_two, axis=0)
    grad_middle = grad_out + norm_back(grad_normed_two * gain_two, unit_two, scale_two)
    grad_mixed = grad_middle.astype(BF16)
    out_grad = over_rows(gated, grad_mixed)
    grad_gated = over_cols(grad_mixed, out_weight).reshape(seqs, span, width)
    grad_c = grad_gated * convolved
    grad_conv = grad_gated * c_gate
    conv_grad = jnp.stack([jnp.sum(grad_conv * lag, axis=(0, 1)) for lag in lags], axis=1)
    ahead = jnp.concatenate([grad_conv, shift(grad_conv[:, :2], -1)], axis=1)
    grad_product = (
        taps[:, 2] * ahead[:, :span]
        + taps[:, 1] * ahead[:, 1 : span + 1]
        + taps[:, 0] * ahead[:, 2:]
    )
    grad_projected = (
        jnp.concatenate(
            [grad_product * x_value[:, 2:], grad_c, grad_product * b_gate[:, 2:]], axis=2
        )
        .astype(BF16)
        .reshape(-1, 3 * width)
    )
    normed_one = normed_ext[:, 2:].reshape(-1, width)
    unit_one = unit_ext[:, 2:].reshape(-1, width)
    scale_one = scale_ext[:, 2:].reshape(-1, 1)
    in_grad = over_rows(normed_one, grad_projected)
    grad_normed_one = over_cols(grad_projected, in_weight)
    norm_gain_grad = jnp.sum(grad_normed_one * unit_one, axis=0)
    grad_tokens = grad_middle + norm_back(grad_normed_one * gain_one, unit_one, scale_one)

    def to_slots(rows):
        return (rows.reshape(seqs, span, width) * live).astype(BF16)

    def reduced(values):
        share = lax.psum_scatter(values.astype(BF16), "fsdp", scatter_dimension=0, tiled=True)
        return lax.psum(share, "rep").astype(F32)

    return (
        to_slots(output),
        to_slots(grad_tokens),
        *map(
            reduced,
            (
                norm_gain_grad,
                in_grad,
                conv_grad,
                out_grad,
                ffn_gain_grad,
                gate_grad,
                up_grad,
                down_grad,
            ),
        ),
    )


def solution(mesh):
    rows = P("rep", "fsdp", None)
    lists = P("rep", None)
    vector = P("fsdp")
    matrix = P("fsdp", None)
    return jax.shard_map(
        body,
        mesh=mesh,
        in_specs=(
            rows,
            rows,
            lists,
            lists,
            vector,
            matrix,
            matrix,
            matrix,
            vector,
            matrix,
            matrix,
            matrix,
        ),
        out_specs=(rows, rows, vector, matrix, matrix, matrix, vector, matrix, matrix, matrix),
        check_vma=False,
    )
```

```python
import functools
import jax
import jax.numpy as jnp
from jax import lax
from jax.experimental import pallas as pl
from jax.experimental.pallas import tpu as pltpu
from jax.sharding import Mesh, PartitionSpec as P

EPS = 1e-05
F32 = jnp.float32
BF16 = jnp.bfloat16
NT = (((1,), (1,)), ((), ()))
TN = (((0,), (0,)), ((), ()))
MESH = pl.DeviceIdType.MESH
CHUNK = 256
BLOCK = 128
GROUP = ("z", "y")


def ffn_kernel(
    sizes,
    n2_in, ef_in, gate_in, up_in, down_in,
    ffn_out, dn2_out, gu_out, down_out, all_gu, all_down,
    n2v, efv, n2t, wgu, wd, outv, dnv, qs, ggs, gvs,
    ggu, gd, rxg, rxd, s1g, s1d, ryg, ryd, s2g, s2d, rzg, rzd, fing, find, give, take,
    sem_in, sem_load, sem_own, sem_pair,
    ag_z, ag_y, ag_dz, ag_dy, ag_send, ag_relay, ag_dsend, ag_drelay,
    rx_g, rx_d, ry_g, ry_d, rz_g, rz_d, sx_g, sx_d, sy_g, sy_d, sz_g, sz_d, sem_fin,
):
    nx, nz, ny, rows, width, hidden = sizes
    n = nz * ny
    dn = width // n
    half = hidden // 2
    steps = half // CHUNK
    per_half = half // BLOCK // 2
    own_rows = hidden // n
    gp = min(BLOCK, own_rows & -own_rows)
    pieces = CHUNK // gp
    slots = ggu.shape[0]
    lag = slots // 2
    x, c = lax.axis_index("x"), lax.axis_index("core")
    z, y = lax.axis_index("z"), lax.axis_index("y")
    me = z * ny + y

    def at(x=x, c=c, z=z, y=y):
        return (x, c, z, y)

    def zp(d):
        return lax.rem(z + d, nz)

    def yp(d):
        return lax.rem(y + d, ny)

    def xp(d):
        return lax.rem(x + d, nx)

    def blocks(m):
        h, i = m % 2, m // 2
        return per_half * h + i, per_half * h + per_half - 1 - i + per_half * (m // (2 * (per_half // 2)))

    def column(b):
        return pl.multiple_of(c * half + b * BLOCK, BLOCK)

    def owner(m, q):
        b = blocks(m)[q * gp // BLOCK]
        row = c * half + b * BLOCK + (q * gp) % BLOCK
        j = row // own_rows
        return j // ny, j % ny, pl.multiple_of(row - j * own_rows, gp)

    def remote(src, dst, ssem, rsem, dev):
        return pltpu.make_async_remote_copy(
            src_ref=src, dst_ref=dst, send_sem=ssem, recv_sem=rsem, device_id=dev, device_id_type=MESH
        )

    def landed(ref, sem):
        pltpu.make_async_copy(ref, ref, sem).wait()

    barrier = pltpu.get_barrier_semaphore()
    peers = [at(z=zp(d)) for d in range(1, nz)] + [at(y=yp(d)) for d in range(1, ny)]
    peers += [at(x=xp(d)) for d in range(1, nx)] + [at(c=1 - c)]
    for dev in peers:
        pl.semaphore_signal(barrier, inc=1, device_id=dev, device_id_type=MESH)
    pl.semaphore_wait(barrier, len(peers))

    mine = pl.ds(pl.multiple_of(c * rows, rows), rows)
    other = pl.ds(pl.multiple_of((1 - c) * rows, rows), rows)
    pair = []
    for i, (src, dst) in enumerate(((n2_in, n2v), (ef_in, efv))):
        pltpu.make_async_copy(src, dst.at[mine], sem_in.at[i]).start()
        pair.append(remote(src, dst.at[mine], sem_pair.at[0, i], sem_pair.at[1, i], at(c=1 - c)))
        pair[i].start()

    ag_peers = [(0, d) for d in range(1, nz)] + [(1, d) for d in range(1, ny)]

    def first_hop(m):
        b = blocks(m)
        for k in range(2):
            src_cols = pl.ds(column(b[k]), BLOCK)
            dst_cols = pl.ds(k * BLOCK, BLOCK)
            for w, src in enumerate((gate_in, up_in)):
                here = src.at[:, src_cols]
                there = all_gu.at[m, w, z, y, :, dst_cols]
                pltpu.make_async_copy(here, there, sem_own.at[0]).start()
                for p, (ax, d) in enumerate(ag_peers):
                    if ax == 0:
                        remote(here, there, ag_send.at[p], ag_z.at[m, d - 1], at(z=zp(d))).start()
                    else:
                        remote(here, there, ag_send.at[p], ag_y.at[m, d - 1], at(y=yp(d))).start()
        for q in range(pieces):
            zo, yo, row = owner(m, q)

            @pl.when(jnp.logical_and(zo == z, yo == y))
            def _():
                here = down_in.at[pl.ds(row, gp)]
                there = all_down.at[m, pl.ds(q * gp, gp)]
                pltpu.make_async_copy(here, there, sem_own.at[1]).start()
                for p, (ax, d) in enumerate(ag_peers):
                    if ax == 0:
                        remote(here, there, ag_dsend.at[p], ag_dz.at[m, q], at(z=zp(d))).start()
                    else:
                        remote(here, there, ag_dsend.at[p], ag_dy.at[m, q], at(y=yp(d))).start()

    def second_hop(m):
        for d in range(1, nz):
            zs = lax.rem(z - d + nz, nz)
            block = all_gu.at[m, :, zs, y]
            landed(block, ag_z.at[m, d - 1])
            for e in range(1, ny):
                remote(block, block, ag_relay.at[d - 1, e - 1], ag_y.at[m, e - 1], at(y=yp(e))).start()
        for q in range(pieces):
            zo, yo, _ = owner(m, q)

            @pl.when(jnp.logical_and(zo != z, yo == y))
            def _():
                block = all_down.at[m, pl.ds(q * gp, gp)]
                landed(block, ag_dz.at[m, q])
                for e in range(1, ny):
                    remote(block, block, ag_drelay.at[zo % 2, e - 1], ag_dy.at[m, q], at(y=yp(e))).start()

    def load(m):
        for e in range(1, ny):
            ys = lax.rem(y - e + ny, ny)
            landed(all_gu.at[m, :, :, ys], ag_y.at[m, e - 1])
        for q in range(pieces):
            _, yo, _ = owner(m, q)

            @pl.when(yo != y)
            def _():
                landed(all_down.at[m, pl.ds(q * gp, gp)], ag_dy.at[m, q])
        a = pltpu.make_async_copy(all_gu.at[m], wgu, sem_load.at[0])
        b = pltpu.make_async_copy(all_down.at[m], wd, sem_load.at[1])
        a.start()
        b.start()
        a.wait()
        b.wait()

    in_half = me // (n // 2) == c
    relay = 2

    @pl.loop(0, steps)
    def _(m):
        first_hop(m)

    for i, (src, dst) in enumerate(((n2_in, n2v), (ef_in, efv))):
        pltpu.make_async_copy(src, dst.at[mine], sem_in.at[i]).wait()
        pair[i].wait_send()
        landed(dst.at[other], sem_pair.at[1, i])

    @pl.loop(0, 2 * rows // 256)
    def _(r):
        rs = pl.ds(pl.multiple_of(r * 256, 256), 256)
        n2t[:, rs] = n2v[rs, :].T
        outv[rs, :] = jnp.zeros((256, width), F32)
        dnv[rs, :] = jnp.zeros((256, width), F32)

    landed(all_gu.at[:, :, 0, 0], sem_own.at[0])

    @pl.when(in_half)
    def _():
        landed(all_down.at[:, pl.ds(0, gp)], sem_own.at[1])

    for m in range(relay):
        second_hop(m)
    load(0)

    tile = 512

    def compute(m):
        slot = m % slots

        @pl.loop(0, 2 * rows // tile)
        def _(r):
            rs = pl.ds(pl.multiple_of(r * tile, tile), tile)
            gate = wgu[0].reshape(width, CHUNK)
            up = wgu[1].reshape(width, CHUNK)
            n2r = n2v[rs, :]
            g = jnp.dot(n2r, gate, preferred_element_type=F32)
            v = jnp.dot(n2r, up, preferred_element_type=F32)
            s = jax.nn.sigmoid(g)
            sg = g * s
            q = (sg * v).astype(BF16)
            dq = lax.dot_general(efv[rs, :], wd[...], NT, preferred_element_type=F32)
            gg = (dq * v * s * (1.0 + g * (1.0 - s))).astype(BF16)
            gv = (dq * sg).astype(BF16)
            qs[rs, :] = q
            ggs[rs, :] = gg
            gvs[rs, :] = gv
            outv[rs, :] += jnp.dot(q, wd[...], preferred_element_type=F32)
            dnv[rs, :] += lax.dot_general(gg, gate, NT, preferred_element_type=F32) + lax.dot_general(
                gv, up, NT, preferred_element_type=F32
            )

        group = nz * ny // 4

        @pl.loop(0, 4)
        def _(t):
            ts = pl.ds(pl.multiple_of(t * 256, 256), 256)
            a = n2t[ts, :]
            for w, src in enumerate((ggs, gvs)):
                full = jnp.dot(a, src[...], preferred_element_type=F32).astype(BF16)
                full = full.reshape(group, nx, dn // nx, CHUNK)
                for h in range(nx):
                    for k in range(group):
                        j = t * group + k
                        ggu[slot, w, h, j // ny, j % ny] = full[k, h]

        for h in range(nx):
            lanes = pl.ds(h * (width // nx), width // nx)
            gd[slot, h] = lax.dot_general(
                qs[...], efv[:, lanes], TN, preferred_element_type=F32
            ).astype(BF16)

    def send_x(m):
        slot = m % slots
        for d in range(1, nx):
            xo = xp(d)
            remote(ggu.at[slot, :, xo], rxg.at[slot, d - 1], sx_g.at[slot, d - 1], rx_g.at[slot, d - 1], at(x=xo)).start()
            remote(gd.at[slot, xo], rxd.at[slot, d - 1], sx_d.at[slot, d - 1], rx_d.at[slot, d - 1], at(x=xo)).start()

    def send_y(m):
        slot = m % slots
        for d in range(1, nx):
            landed(rxg.at[slot, d - 1], rx_g.at[slot, d - 1])
            landed(rxd.at[slot, d - 1], rx_d.at[slot, d - 1])
            landed(rxg.at[slot, d - 1], sx_g.at[slot, d - 1])
            landed(rxd.at[slot, d - 1], sx_d.at[slot, d - 1])

        @pl.loop(0, nz)
        def _(zi):
            for yi in range(ny):
                for w in range(2):
                    total = ggu[slot, w, x, zi, yi].astype(F32)
                    for d in range(1, nx):
                        total += rxg[slot, d - 1, w, zi, yi].astype(F32)
                    s1g[slot, yi, w, zi] = total.astype(BF16)

        total = gd[slot, x].astype(F32)
        for d in range(1, nx):
            total += rxd[slot, d - 1].astype(F32)
        s1d[slot] = total.astype(BF16)
        for d in range(1, ny):
            yo = yp(d)
            remote(s1g.at[slot, yo], ryg.at[slot, d - 1], sy_g.at[slot, d - 1], ry_g.at[slot, d - 1], at(y=yo)).start()
        for q in range(pieces):
            zo, yo, _ = owner(m, q)
            part = pl.ds(q * gp, gp)

            @pl.when(yo != y)
            def _():
                d = lax.rem(yo - y + ny, ny)
                remote(
                    s1d.at[slot, part], ryd.at[slot, d - 1, part], sy_d.at[slot, q], ry_d.at[slot, d - 1, q], at(y=yo)
                ).start()

    def send_z(m):
        slot = m % slots
        for d in range(1, ny):
            landed(ryg.at[slot, d - 1], ry_g.at[slot, d - 1])
            landed(ryg.at[slot, d - 1], sy_g.at[slot, d - 1])
        for zi in range(nz):
            for w in range(2):
                total = s1g[slot, y, w, zi].astype(F32)
                for d in range(1, ny):
                    total += ryg[slot, d - 1, w, zi].astype(F32)
                s2g[slot, zi, w] = total.astype(BF16)
        for d in range(1, nz):
            zo = zp(d)
            remote(s2g.at[slot, zo], rzg.at[slot, d - 1], sz_g.at[slot, d - 1], rz_g.at[slot, d - 1], at(z=zo)).start()
        for q in range(pieces):
            zo, yo, _ = owner(m, q)
            part = pl.ds(q * gp, gp)

            @pl.when(yo != y)
            def _():
                landed(s1d.at[slot, part], sy_d.at[slot, q])

            @pl.when(yo == y)
            def _():
                total = s1d[slot, part].astype(F32)
                for d in range(1, ny):
                    landed(ryd.at[slot, d - 1, part], ry_d.at[slot, d - 1, q])
                    total += ryd[slot, d - 1, part].astype(F32)
                s2d[slot, part] = total.astype(BF16)

                @pl.when(zo != z)
                def _():
                    d = lax.rem(zo - z + nz, nz)
                    remote(
                        s2d.at[slot, part], rzd.at[slot, d - 1, part], sz_d.at[slot, q], rz_d.at[slot, d - 1, q], at(z=zo)
                    ).start()

    def finish(m):
        slot = m % slots
        for d in range(1, nz):
            landed(rzg.at[slot, d - 1], rz_g.at[slot, d - 1])
            landed(rzg.at[slot, d - 1], sz_g.at[slot, d - 1])
        for w in range(2):
            total = s2g[slot, z, w].astype(F32)
            for d in range(1, nz):
                total += rzg[slot, d - 1, w].astype(F32)
            fing[w] = total.astype(BF16)
        for q in range(pieces):
            zo, yo, row = owner(m, q)
            part = pl.ds(q * gp, gp)

            @pl.when(jnp.logical_and(yo == y, zo != z))
            def _():
                landed(s2d.at[slot, part], sz_d.at[slot, q])

            @pl.when(jnp.logical_and(yo == y, zo == z))
            def _():
                total = s2d[slot, part].astype(F32)
                for d in range(1, nz):
                    landed(rzd.at[slot, d - 1, part], rz_d.at[slot, d - 1, q])
                    total += rzd[slot, d - 1, part].astype(F32)
                find[part] = total.astype(BF16)
                out = pltpu.make_async_copy(find.at[part], down_out.at[pl.ds(row, gp)], sem_fin.at[2])
                out.start()
                out.wait()
        b = blocks(m)
        outs = []
        for k in range(2):
            cols = pl.ds(pl.multiple_of(b[k] * BLOCK, BLOCK), BLOCK)
            outs.append(
                pltpu.make_async_copy(fing.at[:, :, pl.ds(k * BLOCK, BLOCK)], gu_out.at[:, :, cols], sem_fin.at[k])
            )
            outs[k].start()
        for k in range(2):
            outs[k].wait()

    @pl.loop(0, steps + 3 * lag)
    def _(m):
        @pl.when(m < steps)
        def _():
            compute(m)

        @pl.when(m >= 3 * lag)
        def _():
            finish(m - 3 * lag)

        @pl.when(jnp.logical_and(m >= 2 * lag, m < steps + 2 * lag))
        def _():
            send_z(m - 2 * lag)

        @pl.when(jnp.logical_and(m >= lag, m < steps + lag))
        def _():
            send_y(m - lag)

        @pl.when(m < steps)
        def _():
            send_x(m)

        @pl.when(m + relay < steps)
        def _():
            second_hop(m + relay)

        @pl.when(m + 1 < steps)
        def _():
            load(m + 1)

        @pl.when(m == steps - 1)
        def _():
            for i, src in enumerate((outv, dnv)):
                give[i] = src[other, :].astype(BF16)
                remote(give.at[i], take.at[i], sem_pair.at[2, i], sem_pair.at[3, i], at(c=1 - c)).start()

    for i, (src, dst) in enumerate(((outv, ffn_out), (dnv, dn2_out))):
        landed(take.at[i], sem_pair.at[3, i])
        landed(take.at[i], sem_pair.at[2, i])
        src[mine, :] += take[i].astype(F32)
        out = pltpu.make_async_copy(src.at[mine], dst, sem_fin.at[i])
        out.start()
    for i, (src, dst) in enumerate(((outv, ffn_out), (dnv, dn2_out))):
        pltpu.make_async_copy(src.at[mine], dst, sem_fin.at[i]).wait()

    for p in range(len(ag_peers)):
        landed(all_gu.at[:, :, 0, 0], ag_send.at[p])

        @pl.when(in_half)
        def _():
            landed(all_down.at[:, pl.ds(0, gp)], ag_dsend.at[p])

    for d in range(1, nz):
        for e in range(1, ny):
            landed(all_gu.at[:, :, 0, 0], ag_relay.at[d - 1, e - 1])
    for k in range(2):
        zo = (n // 2 * c) // ny + k

        @pl.when(zo != z)
        def _():
            for e in range(1, ny):
                landed(all_down.at[:, pl.ds(0, gp)], ag_drelay.at[zo % 2, e - 1])


def ffn_call(sizes, n2, ef, gate, up, down, lag=1):
    nx, nz, ny, rows, width, hidden = sizes
    n = nz * ny
    dn = width // n
    half = hidden // 2
    steps = half // CHUNK
    own_rows = hidden // n
    gp = min(BLOCK, own_rows & -own_rows)
    pieces = CHUNK // gp
    s = 2 * lag
    dnx = dn // nx
    lanes = width // nx
    dma = pltpu.SemaphoreType.DMA
    anywhere = pl.BlockSpec(memory_space=pl.ANY)
    shape = jax.ShapeDtypeStruct
    return pl.pallas_call(
        functools.partial(ffn_kernel, sizes),
        out_shape=[
            shape((rows, width), F32),
            shape((rows, width), F32),
            shape((2, dnx, half), BF16),
            shape((own_rows, lanes), BF16),
            shape((steps, 2, nz, ny, dn, CHUNK), BF16),
            shape((steps, CHUNK, width), BF16),
        ],
        in_specs=[anywhere] * 5,
        out_specs=[anywhere] * 6,
        scratch_shapes=[
            pltpu.VMEM((2 * rows, width), BF16),
            pltpu.VMEM((2 * rows, width), BF16),
            pltpu.VMEM((width, 2 * rows), BF16),
            pltpu.VMEM((2, nz, ny, dn, CHUNK), BF16),
            pltpu.VMEM((CHUNK, width), BF16),
            pltpu.VMEM((2 * rows, width), F32),
            pltpu.VMEM((2 * rows, width), F32),
            pltpu.VMEM((2 * rows, CHUNK), BF16),
            pltpu.VMEM((2 * rows, CHUNK), BF16),
            pltpu.VMEM((2 * rows, CHUNK), BF16),
            pltpu.VMEM((s, 2, nx, nz, ny, dnx, CHUNK), BF16),
            pltpu.VMEM((s, nx, CHUNK, lanes), BF16),
            pltpu.VMEM((s, nx - 1, 2, nz, ny, dnx, CHUNK), BF16),
            pltpu.VMEM((s, nx - 1, CHUNK, lanes), BF16),
            pltpu.VMEM((s, ny, 2, nz, dnx, CHUNK), BF16),
            pltpu.VMEM((s, CHUNK, lanes), BF16),
            pltpu.VMEM((s, ny - 1, 2, nz, dnx, CHUNK), BF16),
            pltpu.VMEM((s, ny - 1, CHUNK, lanes), BF16),
            pltpu.VMEM((s, nz, 2, dnx, CHUNK), BF16),
            pltpu.VMEM((s, CHUNK, lanes), BF16),
            pltpu.VMEM((s, nz - 1, 2, dnx, CHUNK), BF16),
            pltpu.VMEM((s, nz - 1, CHUNK, lanes), BF16),
            pltpu.VMEM((2, dnx, CHUNK), BF16),
            pltpu.VMEM((CHUNK, lanes), BF16),
            pltpu.VMEM((2, rows, width), BF16),
            pltpu.VMEM((2, rows, width), BF16),
            dma((2,)),
            dma((2,)),
            dma((2,)),
            dma((4, 2)),
            dma((steps, nz - 1)),
            dma((steps, ny - 1)),
            dma((steps, pieces)),
            dma((steps, pieces)),
            dma((nz + ny - 2,)),
            dma((nz - 1, ny - 1)),
            dma((nz + ny - 2,)),
            dma((2, ny - 1)),
            dma((s, nx - 1)),
            dma((s, nx - 1)),
            dma((s, ny - 1)),
            dma((s, ny - 1, pieces)),
            dma((s, nz - 1)),
            dma((s, nz - 1, pieces)),
            dma((s, nx - 1)),
            dma((s, nx - 1)),
            dma((s, ny - 1)),
            dma((s, pieces)),
            dma((s, nz - 1)),
            dma((s, pieces)),
            dma((3,)),
        ],
        compiler_params=pltpu.CompilerParams(
            collective_id=0, has_side_effects=True, vmem_limit_bytes=63 << 20
        ),
        name="feed_forward",
    )(n2, ef, gate, up, down)[:4]


def row_scale(values):
    return lax.rsqrt(jnp.mean(values * values, axis=-1, keepdims=True) + EPS)


def norm_back(grad_unit, unit_rows, scale_rows):
    return scale_rows * (
        grad_unit - unit_rows * jnp.mean(grad_unit * unit_rows, axis=-1, keepdims=True)
    )


def over_rows(left_side, right_side):
    return lax.dot_general(
        left_side, right_side, (((0,), (0,)), ((), ())), preferred_element_type=F32
    )


def over_cols(left_side, right_side):
    return lax.dot_general(
        left_side, right_side, (((1,), (1,)), ((), ())), preferred_element_type=F32
    )


def dot(left_side, right_side):
    return jnp.dot(left_side, right_side, preferred_element_type=F32)


def live_mask(lengths, deal, span):
    slots = jnp.arange(deal.shape[1], dtype=jnp.int32)
    picked = deal[0][:, None] == slots[None, :]
    source_len = jnp.sum(jnp.where(picked, lengths[0][:, None], 0), axis=0)
    position = lax.axis_index(GROUP) * span + jnp.arange(span, dtype=jnp.int32)
    return (position[None, :] < source_len[:, None]).astype(F32)[..., None]


def shift(values, amount):
    size = (lax.axis_size("z") * lax.axis_size("y"))
    pairs = [(i, i + amount) for i in range(size) if 0 <= i + amount < size]
    return lax.ppermute(values, GROUP, pairs)


def body(
    tokens,
    cotangent,
    lengths,
    deal,
    norm_gain,
    in_weight,
    conv_weight,
    out_weight,
    ffn_gain,
    gate_weight,
    up_weight,
    down_weight,
):
    seqs, span, width = tokens.shape
    live = live_mask(lengths, deal, span)
    halo = shift(tokens[:, span - 2 :], 1)

    def gather(values):
        return lax.all_gather(values, GROUP, axis=0, tiled=True)

    norm_gain, in_weight, conv_weight, out_weight = map(
        gather, (norm_gain, in_weight, conv_weight, out_weight)
    )
    ffn_gain = gather(ffn_gain)
    gain_one = norm_gain.astype(F32)
    gain_two = ffn_gain.astype(F32)
    taps = conv_weight.astype(F32)
    extended = jnp.concatenate([halo, tokens], axis=1).astype(F32)
    scale_ext = row_scale(extended)
    unit_ext = extended * scale_ext
    normed_ext = (unit_ext * gain_one).astype(BF16)
    projected = dot(normed_ext.reshape(-1, width), in_weight).reshape(seqs, span + 2, 3 * width)
    b_gate = projected[:, :, :width]
    c_gate = projected[:, 2:, width : 2 * width]
    x_value = projected[:, :, 2 * width :]
    product = b_gate * x_value
    lags = (product[:, :span], product[:, 1 : span + 1], product[:, 2:])
    convolved = taps[:, 0] * lags[0] + taps[:, 1] * lags[1] + taps[:, 2] * lags[2]
    gated = (c_gate * convolved).astype(BF16).reshape(-1, width)
    token_rows = tokens.astype(F32).reshape(-1, width)
    middle = token_rows + dot(gated, out_weight)
    scale_two = row_scale(middle)
    unit_two = middle * scale_two
    normed_two = (unit_two * gain_two).astype(BF16)
    grad_out = (cotangent.astype(F32) * live).reshape(-1, width)
    grad_ffn = grad_out.astype(BF16)
    sizes = (
        lax.axis_size("x"),
        lax.axis_size("z"),
        lax.axis_size("y"),
        seqs * span,
        width,
        gate_weight.shape[1],
    )
    ffn_rows, grad_normed_two, gu_part, down_part = ffn_call(
        sizes, normed_two, grad_ffn, gate_weight, up_weight, down_weight
    )
    output = middle + ffn_rows
    gate_grad, up_grad, down_grad = whole_parts(sizes, gu_part, down_part)
    ffn_gain_grad = jnp.sum(grad_normed_two * unit_two, axis=0)
    grad_middle = grad_out + norm_back(grad_normed_two * gain_two, unit_two, scale_two)
    grad_mixed = grad_middle.astype(BF16)
    out_grad = over_rows(gated, grad_mixed)
    grad_gated = over_cols(grad_mixed, out_weight).reshape(seqs, span, width)
    grad_c = grad_gated * convolved
    grad_conv = grad_gated * c_gate
    conv_grad = jnp.stack([jnp.sum(grad_conv * lag, axis=(0, 1)) for lag in lags], axis=1)
    ahead = jnp.concatenate([grad_conv, shift(grad_conv[:, :2], -1)], axis=1)
    grad_product = (
        taps[:, 2] * ahead[:, :span]
        + taps[:, 1] * ahead[:, 1 : span + 1]
        + taps[:, 0] * ahead[:, 2:]
    )
    grad_projected = (
        jnp.concatenate(
            [grad_product * x_value[:, 2:], grad_c, grad_product * b_gate[:, 2:]], axis=2
        )
        .astype(BF16)
        .reshape(-1, 3 * width)
    )
    normed_one = normed_ext[:, 2:].reshape(-1, width)
    unit_one = unit_ext[:, 2:].reshape(-1, width)
    scale_one = scale_ext[:, 2:].reshape(-1, 1)
    in_grad = over_rows(normed_one, grad_projected)
    grad_normed_one = over_cols(grad_projected, in_weight)
    norm_gain_grad = jnp.sum(grad_normed_one * unit_one, axis=0)
    grad_tokens = grad_middle + norm_back(grad_normed_one * gain_one, unit_one, scale_one)

    def to_slots(rows):
        return (rows.reshape(seqs, span, width) * live).astype(BF16)

    def reduced(values):
        share = lax.psum_scatter(values.astype(BF16), GROUP, scatter_dimension=0, tiled=True)
        return lax.psum(share, ("x", "core")).astype(F32)

    return (
        to_slots(output),
        to_slots(grad_tokens),
        reduced(norm_gain_grad),
        reduced(in_grad),
        reduced(conv_grad),
        reduced(out_grad),
        reduced(ffn_gain_grad),
        gate_grad,
        up_grad,
        down_grad,
    )


def whole_parts(sizes, gu_part, down_part):
    nx, nz, ny, _, width, hidden = sizes
    both = lax.all_gather(gu_part, ("x", "core"))
    both = both.reshape(nx, 2, *gu_part.shape).transpose(2, 0, 3, 1, 4)
    both = both.reshape(2, width // (nz * ny), hidden).astype(F32)
    down = lax.all_gather(down_part, ("x", "core"))
    down = down.reshape(nx, 2, *down_part.shape)
    down = lax.dynamic_index_in_dim(down, lax.axis_index("z") // (nz // 2), 1, keepdims=False)
    down = down.transpose(1, 0, 2).reshape(down_part.shape[0], width).astype(F32)
    return both[0], both[1], down


def solution(mesh):
    rep, fsdp = mesh.shape["rep"], mesh.shape["fsdp"]
    grid = (rep // 2, 2, 4, fsdp // 4)
    split = Mesh(mesh.devices.reshape(grid), ("x", "core", "z", "y"))
    copies = ("x", "core")
    rows = P(copies, GROUP, None)
    lists = P(copies, None)
    vector = P(GROUP)
    matrix = P(GROUP, None)
    return jax.shard_map(
        body,
        mesh=split,
        in_specs=(
            rows,
            rows,
            lists,
            lists,
            vector,
            matrix,
            matrix,
            matrix,
            vector,
            matrix,
            matrix,
            matrix,
        ),
        out_specs=(rows, rows, vector, matrix, matrix, matrix, vector, matrix, matrix, matrix),
        check_vma=False,
    )
```

```python
import functools
import jax
import jax.numpy as jnp
from jax import lax
from jax.experimental import pallas as pl
from jax.experimental.pallas import tpu as pltpu
from jax.sharding import Mesh, PartitionSpec as P

EPS = 1e-05
F32 = jnp.float32
BF16 = jnp.bfloat16
NT = (((1,), (1,)), ((), ()))
TN = (((0,), (0,)), ((), ()))
MESH = pl.DeviceIdType.MESH
GROUP = ("z", "y")
CHUNK = 256
BLOCK = 128
TILE = 256
EDGE = 8
LAG = 1
AHEAD = 4
RELAY = 2


def dot(left, right):
    return jnp.dot(left, right, preferred_element_type=F32)


def dot_nt(left, right):
    return lax.dot_general(left, right, NT, preferred_element_type=F32)


def dot_tn(left, right):
    return lax.dot_general(left, right, TN, preferred_element_type=F32)


def row_scale(values):
    return lax.rsqrt(jnp.mean(values * values, axis=-1, keepdims=True) + EPS)


def block_kernel(
    sizes,
    tok_in, edge_in, cot_in, live_in, small_in, in_in, out_in, gate_in, up_in, down_in,
    y_out, dx_out, gu_full, down_full, in_full, out_full, small_out,
    all_gu, all_down, all_in, all_out, spill_p, spill_h, spill_t,
    act_a, act_b, tr, wgu, wd, outv, dnv, acts, wout, zv, take, og,
    ub, vb, hal, uh, kh, ks, chd, hf, smallv, vec, conv_acc, sg,
    ggu, gd, rxg, rxd, s1g, s1d, ryg, ryd, s2g, s2d, rzg, rzd, fing, find,
    sem_in, sem_load, sem_own, sem_pair, sem_small, sem_edge, sem_kh, sem_spill,
    ag_z, ag_y, ag_dz, ag_dy, ag_send, ag_relay, ag_dsend, ag_drelay,
    mg_own, mg_z, mg_y, mg_oz, mg_oy, mg_send, mg_relay, mg_osend, mg_orelay,
    rx_g, rx_d, ry_g, ry_d, rz_g, rz_d, sx_g, sx_d, sy_g, sy_d, sz_g, sz_d,
    sem_fin, fs_g, fs_d, fr_g, fr_i, fr_d, fr_o,
):
    nx, nz, ny, seqs, span, width, hidden = sizes
    n = nz * ny
    rows = seqs * span
    dn = width // n
    dnx = dn // nx
    half = hidden // 2
    chan = width // 2
    steps = half // CHUNK
    chunks = steps + 3
    per_half = half // BLOCK // 2
    own_rows = hidden // n
    gp = min(BLOCK, own_rows & -own_rows)
    pieces = CHUNK // gp
    lanes = width // nx
    slots = 2 * LAG
    tiles = rows // TILE
    tseq = TILE // span
    x, c = lax.axis_index("x"), lax.axis_index("core")
    z, y = lax.axis_index("z"), lax.axis_index("y")
    me = z * ny + y
    in_half = me // (n // 2) == c

    def at(x=x, c=c, z=z, y=y):
        return (x, c, z, y)

    def member(j, c=c):
        return at(c=c, z=j // ny, y=j % ny)

    def zp(d):
        return lax.rem(z + d, nz)

    def yp(d):
        return lax.rem(y + d, ny)

    def xp(d):
        return lax.rem(x + d, nx)

    def remote(src, dst, ssem, rsem, dev):
        return pltpu.make_async_remote_copy(
            src_ref=src, dst_ref=dst, send_sem=ssem, recv_sem=rsem, device_id=dev, device_id_type=MESH
        )

    def local(src, dst, sem):
        return pltpu.make_async_copy(src, dst, sem)

    def landed(ref, sem):
        pltpu.make_async_copy(ref, ref, sem).wait()

    def span_of(start, size, align):
        return pl.ds(pl.multiple_of(start, align), size)

    mine = span_of(c * rows, rows, rows)
    other = span_of((1 - c) * rows, rows, rows)

    barrier = pltpu.get_barrier_semaphore()
    peers = [member(lax.rem(me + d, n)) for d in range(1, n)]
    reps = [(d, e) for d in range(nx) for e in range(2) if d + e > 0]
    peers += [at(x=xp(d), c=lax.rem(c + e, 2)) for d, e in reps]
    peers += [member(lax.rem(me + d, n), c=1 - c) for d in (1, n - 1)]
    for dev in peers:
        pl.semaphore_signal(barrier, inc=1, device_id=dev, device_id_type=MESH)
    pl.semaphore_wait(barrier, len(peers))

    local(small_in, smallv.at[me], sem_small.at[0]).start()
    for d in range(1, n):
        remote(small_in, smallv.at[me], sem_small.at[1], sem_small.at[2], member(lax.rem(me + d, n))).start()

    @pl.when(me < n - 1)
    def _():
        for e in range(2):
            src = edge_in.at[:, pl.ds(span - EDGE, EDGE)]
            dev = member(lax.rem(me + 1, n), c=lax.rem(c + e, 2))
            remote(src, hal.at[c], sem_edge.at[e], sem_edge.at[2 + c], dev).start()

    local(tok_in, act_a.at[mine], sem_in.at[0]).start()
    local(cot_in, take.at[1], sem_in.at[1]).start()
    remote(tok_in, act_a.at[mine], sem_pair.at[0], sem_pair.at[1], at(c=1 - c)).start()

    ag_peers = [(0, d) for d in range(1, nz)] + [(1, d) for d in range(1, ny)]

    def toward(ax, d):
        return at(z=zp(d)) if ax == 0 else at(y=yp(d))

    for b in range(6):
        here = in_in.at[:, span_of((b // 2) * width + c * chan + (b % 2) * CHUNK, CHUNK, CHUNK)]
        there = all_in.at[b, z, y]
        local(here, there, mg_own.at[0]).start()
        for p, (ax, d) in enumerate(ag_peers):
            remote(here, there, mg_send.at[p], (mg_z, mg_y)[ax].at[d - 1], toward(ax, d)).start()

    @pl.when(in_half)
    def _():
        o = me - c * (n // 2)
        local(out_in, all_out.at[o], mg_own.at[1]).start()
        for p, (ax, d) in enumerate(ag_peers):
            remote(out_in, all_out.at[o], mg_osend.at[p], (mg_oz, mg_oy)[ax].at[o], toward(ax, d)).start()

    def out_owner(o):
        j = c * (n // 2) + o
        return j // ny, j % ny

    def mixer_second_hop():
        for d in range(1, nz):
            zs = lax.rem(z - d + nz, nz)
            block = all_in.at[:, zs, y]
            landed(block, mg_z.at[d - 1])
            for e in range(1, ny):
                remote(block, block, mg_relay.at[d - 1, e - 1], mg_y.at[e - 1], at(y=yp(e))).start()
        for o in range(n // 2):
            zo, yo = out_owner(o)

            @pl.when(jnp.logical_and(zo != z, yo == y))
            def _():
                landed(all_out.at[o], mg_oz.at[o])
                for e in range(1, ny):
                    remote(all_out.at[o], all_out.at[o], mg_orelay.at[o, e - 1], mg_oy.at[o], at(y=yp(e))).start()

    def mixer_arrived():
        for e in range(1, ny):
            landed(all_in.at[:, :, lax.rem(y - e + ny, ny)], mg_y.at[e - 1])
        for o in range(n // 2):
            _, yo = out_owner(o)

            @pl.when(yo != y)
            def _():
                landed(all_out.at[o], mg_oy.at[o])

        landed(all_in.at[:, 0, 0], mg_own.at[0])

        @pl.when(in_half)
        def _():
            landed(all_out.at[0], mg_own.at[1])

    def mixer_load():
        copies = [local(all_in, acts, sem_load.at[0])]
        copies += [local(all_out.at[o], wout.at[pl.ds(o * dn, dn)], sem_load.at[2 + o]) for o in range(n // 2)]
        for copy in copies:
            copy.start()
        for copy in copies:
            copy.wait()

    def blocks(m):
        h, i = m % 2, m // 2
        first = per_half * h + i
        return first, per_half * h + per_half - 1 - i + per_half * (m // (2 * (per_half // 2)))

    def column(b):
        return pl.multiple_of(c * half + b * BLOCK, BLOCK)

    def owner(m, q):
        b = blocks(m)[q * gp // BLOCK]
        row = c * half + b * BLOCK + (q * gp) % BLOCK
        j = row // own_rows
        return j // ny, j % ny, pl.multiple_of(row - j * own_rows, gp)

    def grad_owner(m, q):
        zo, yo, row = owner(jnp.minimum(m, steps - 1), q)
        mixed = c * chan + jnp.maximum(m - steps, 0) * CHUNK + q * gp
        j = mixed // dn
        late = m >= steps
        return (
            jnp.where(late, j // ny, zo),
            jnp.where(late, j % ny, yo),
            pl.multiple_of(jnp.where(late, mixed - j * dn, row), gp),
        )

    def first_hop(m):
        b = blocks(m)
        for k in range(2):
            for w, src in enumerate((gate_in, up_in)):
                here = src.at[:, pl.ds(column(b[k]), BLOCK)]
                there = all_gu.at[m, w, z, y, :, pl.ds(k * BLOCK, BLOCK)]
                local(here, there, sem_own.at[0, m]).start()
                for p, (ax, d) in enumerate(ag_peers):
                    remote(here, there, ag_send.at[p], (ag_z, ag_y)[ax].at[m, d - 1], toward(ax, d)).start()
        for q in range(pieces):
            zo, yo, row = owner(m, q)

            @pl.when(jnp.logical_and(zo == z, yo == y))
            def _():
                here = down_in.at[pl.ds(row, gp)]
                there = all_down.at[m, pl.ds(q * gp, gp)]
                local(here, there, sem_own.at[1, m * pieces + q]).start()
                for p, (ax, d) in enumerate(ag_peers):
                    remote(here, there, ag_dsend.at[p], (ag_dz, ag_dy)[ax].at[m, q], toward(ax, d)).start()

    def second_hop(m):
        for d in range(1, nz):
            zs = lax.rem(z - d + nz, nz)
            block = all_gu.at[m, :, zs, y]
            landed(block, ag_z.at[m, d - 1])
            for e in range(1, ny):
                remote(block, block, ag_relay.at[d - 1, e - 1], ag_y.at[m, e - 1], at(y=yp(e))).start()
        for q in range(pieces):
            zo, yo, _ = owner(m, q)

            @pl.when(jnp.logical_and(zo != z, yo == y))
            def _():
                block = all_down.at[m, pl.ds(q * gp, gp)]
                landed(block, ag_dz.at[m, q])
                for e in range(1, ny):
                    remote(block, block, ag_drelay.at[zo % 2, e - 1], ag_dy.at[m, q], at(y=yp(e))).start()

    def load(m):
        landed(all_gu.at[m, :, 0, 0], sem_own.at[0, m])
        for e in range(1, ny):
            landed(all_gu.at[m, :, :, lax.rem(y - e + ny, ny)], ag_y.at[m, e - 1])
        for q in range(pieces):
            zo, yo, _ = owner(m, q)
            block = all_down.at[m, pl.ds(q * gp, gp)]

            @pl.when(jnp.logical_and(zo == z, yo == y))
            def _():
                landed(block, sem_own.at[1, m * pieces + q])

            @pl.when(yo != y)
            def _():
                landed(block, ag_dy.at[m, q])

        a = local(all_gu.at[m], wgu, sem_load.at[0])
        b = local(all_down.at[m], wd, sem_load.at[1])
        a.start()
        b.start()
        a.wait()
        b.wait()

    local(cot_in, take.at[1], sem_in.at[1]).wait()

    @pl.loop(0, tiles)
    def _(t):
        rl = span_of(t * TILE, TILE, TILE)
        rs = span_of(c * rows + t * TILE, TILE, TILE)
        act_b[rs, :] = (take[1, rl, :].astype(F32) * live_in[rl, :]).astype(BF16)

    remote(act_b.at[mine], act_b.at[mine], sem_pair.at[2], sem_pair.at[3], at(c=1 - c)).start()

    landed(small_in, sem_small.at[0])
    landed(smallv.at[pl.ds(0, n - 1)], sem_small.at[1])
    landed(smallv.at[pl.ds(0, n - 1)], sem_small.at[2])
    for j in range(n):
        vec[:, j * dn : (j + 1) * dn] = smallv[j]

    @pl.when(me < n - 1)
    def _():
        for e in range(2):
            landed(hal.at[0], sem_edge.at[e])

    @pl.when(me > 0)
    def _():
        for e in range(2):
            landed(hal.at[e], sem_edge.at[2 + e])

    @pl.when(me == 0)
    def _():
        hal[...] = jnp.zeros_like(hal)

    mixer_second_hop()
    first_hop(0)
    first_hop(1)
    local(tok_in, act_a.at[mine], sem_in.at[0]).wait()
    landed(act_a.at[mine], sem_pair.at[0])
    landed(act_a.at[other], sem_pair.at[1])
    local(act_a.at[other], spill_t, sem_spill.at[6]).start()
    mixer_arrived()
    mixer_load()

    def win(b):
        return acts[b].reshape(width, CHUNK)

    def tap(k, h):
        return vec[2 + k : 3 + k, span_of(c * chan + h * CHUNK, CHUNK, CHUNK)].reshape(1, 1, CHUNK)

    def normed(tokens):
        return (tokens * row_scale(tokens) * vec[0:1, :]).astype(BF16)

    for cc in range(2):
        edge = normed(hal[cc].astype(F32).reshape(seqs * EDGE, width))
        for h in range(2):
            product = dot(edge, win(h)) * dot(edge, win(4 + h))
            uh[cc * seqs : (cc + 1) * seqs, :, h * CHUNK : (h + 1) * CHUNK] = product.reshape(seqs, EDGE, CHUNK)

    def convolve(product, first, h):
        ub[:, :EDGE, :] = uh[pl.ds(first, tseq), :, h * CHUNK : (h + 1) * CHUNK]
        ub[:, EDGE:, :] = product.reshape(tseq, span, CHUNK)
        lag_two = ub[:, EDGE - 2 : EDGE - 2 + span, :]
        lag_one = ub[:, EDGE - 1 : EDGE - 1 + span, :]
        lag_none = ub[:, EDGE:, :]
        return lag_two, lag_one, lag_none, tap(0, h) * lag_two + tap(1, h) * lag_one + tap(2, h) * lag_none

    def spilled(t, i, rs):
        slot = t % 2
        src = dnv.at[span_of(slot * 3 * TILE + i * TILE, TILE, TILE), pl.ds(0, chan)]
        return local(src, spill_p.at[i, rs], sem_spill.at[slot * 3 + i])

    def tile_start(t):
        return lax.rem(t + (1 - c) * tiles, 2 * tiles) * TILE

    @pl.loop(0, 2 * tiles)
    def _(t):
        start = tile_start(t)
        rs = span_of(start, TILE, TILE)
        first = start // span
        tokens = act_a[rs, :].astype(F32)
        n1 = normed(tokens)

        @pl.when(t >= 2)
        def _():
            for i in range(3):
                spilled(t, i, rs).wait()

        for h in range(2):
            parts = [dot(n1, win(2 * i + h)) for i in range(3)]
            hl = pl.ds(h * CHUNK, CHUNK)
            for i in range(3):
                dnv[span_of((t % 2) * 3 * TILE + i * TILE, TILE, TILE), hl] = parts[i]
            chd[pl.ds(first, tseq), :, hl] = parts[1].reshape(tseq, span, CHUNK)[:, :EDGE]
            conv = convolve(parts[0] * parts[2], first, h)[3].reshape(TILE, CHUNK)
            zv[rs, hl] = (parts[1] * conv).astype(BF16)
        for i in range(3):
            spilled(t, i, rs).start()
        mixed = dot(zv[rs, :], wout[...])

        @pl.when(t < tiles)
        def _():
            tr[span_of(t * TILE, TILE, TILE), pl.ds(0, width)] = mixed.astype(BF16)

        @pl.when(t >= tiles)
        def _():
            outv[rs, :] = act_a[rs, :].astype(F32) + mixed

        @pl.when(t == tiles - 1)
        def _():
            landed(act_a.at[other], sem_spill.at[6])
            remote(tr.at[:, pl.ds(0, width)], take.at[0], sem_pair.at[4], sem_pair.at[5], at(c=1 - c)).start()

    first_hop(2)
    second_hop(0)
    for slot in range(2):
        for i in range(3):
            spilled(slot, i, pl.ds(0, TILE)).wait()
    landed(take.at[0], sem_pair.at[5])

    @pl.loop(0, tiles)
    def _(t):
        rs = span_of(c * rows + t * TILE, TILE, TILE)
        middle = outv[rs, :] + take[0, span_of(t * TILE, TILE, TILE), :].astype(F32)
        outv[rs, :] = middle
        act_a[rs, :] = (middle * row_scale(middle) * vec[1:2, :]).astype(BF16)

    remote(act_a.at[mine], act_a.at[mine], sem_pair.at[6], sem_pair.at[7], at(c=1 - c)).start()
    local(outv.at[mine], spill_h, sem_spill.at[7]).start()
    landed(take.at[0], sem_pair.at[4])
    first_hop(3)
    second_hop(1)

    @pl.loop(0, tiles)
    def _(t):
        ro = span_of((1 - c) * rows + t * TILE, TILE, TILE)
        rs = span_of(c * rows + t * TILE, TILE, TILE)
        outv[ro, :] = jnp.zeros((TILE, width), F32)
        dnv[ro, :] = jnp.zeros((TILE, width), F32)
        dnv[rs, :] = jnp.zeros((TILE, width), F32)

    landed(act_a.at[other], sem_pair.at[7])
    landed(act_a.at[mine], sem_pair.at[6])
    landed(act_b.at[other], sem_pair.at[3])
    landed(act_b.at[mine], sem_pair.at[2])

    @pl.loop(0, 2 * tiles)
    def _(t):
        rs = span_of(t * TILE, TILE, TILE)
        tr[:, rs] = act_a[rs, :].T

    local(outv.at[mine], spill_h, sem_spill.at[7]).wait()
    load(0)

    big = 512
    zb = big // (ny * dn)

    def hid(w):
        return acts[2 * w : 2 * w + 2].reshape(2 * rows, CHUNK)

    def compute(m):
        slot = m % slots

        @pl.loop(0, 2 * rows // big)
        def _(r):
            rs = span_of(r * big, big, big)
            gate = wgu[0].reshape(width, CHUNK)
            up = wgu[1].reshape(width, CHUNK)
            n2r = act_a[rs, :]
            g = dot(n2r, gate)
            v = dot(n2r, up)
            s = jax.nn.sigmoid(g)
            sg_ = g * s
            q = (sg_ * v).astype(BF16)
            dq = dot_nt(act_b[rs, :], wd[...])
            gg = (dq * v * s * (1.0 + g * (1.0 - s))).astype(BF16)
            gv = (dq * sg_).astype(BF16)
            zi = pl.ds((r % 2) * zb, zb)
            for w, value in enumerate((q, gg, gv)):
                acts[2 * w + r // 2, zi] = value.reshape(zb, ny, dn, CHUNK)
            outv[rs, :] += dot(q, wd[...])
            dnv[rs, :] += dot_nt(gg, gate) + dot_nt(gv, up)

        weight_grads(slot, hid(1), hid(2))
        for h in range(nx):
            gd[slot, h] = dot_tn(hid(0), act_b[:, pl.ds(h * lanes, lanes)]).astype(BF16)

    def weight_grads(slot, first, second):
        group = n // 4

        @pl.loop(0, 4)
        def _(t):
            a = tr[span_of(t * TILE, TILE, TILE), :]
            for w, src in enumerate((first, second)):
                full = dot(a, src).astype(BF16).reshape(group, nx, dnx, CHUNK)
                for h in range(nx):
                    for k in range(group):
                        j = t * group + k
                        ggu[slot, w, h, j // ny, j % ny] = full[k, h]

    def send_x(m):
        slot = m % slots
        for d in range(1, nx):
            xo = xp(d)
            remote(ggu.at[slot, :, xo], rxg.at[slot, d - 1], sx_g.at[slot, d - 1], rx_g.at[slot, d - 1], at(x=xo)).start()

            @pl.when(m < chunks - 1)
            def _():
                remote(gd.at[slot, xo], rxd.at[slot, d - 1], sx_d.at[slot, d - 1], rx_d.at[slot, d - 1], at(x=xo)).start()

    def send_y(m):
        slot = m % slots
        for d in range(1, nx):
            landed(rxg.at[slot, d - 1], rx_g.at[slot, d - 1])
            landed(rxg.at[slot, d - 1], sx_g.at[slot, d - 1])

        @pl.loop(0, nz)
        def _(zi):
            for yi in range(ny):
                for w in range(2):
                    total = ggu[slot, w, x, zi, yi].astype(F32)
                    for d in range(1, nx):
                        total += rxg[slot, d - 1, w, zi, yi].astype(F32)
                    s1g[slot, yi, w, zi] = total.astype(BF16)

        for d in range(1, ny):
            yo = yp(d)
            remote(s1g.at[slot, yo], ryg.at[slot, d - 1], sy_g.at[slot, d - 1], ry_g.at[slot, d - 1], at(y=yo)).start()

        @pl.when(m < chunks - 1)
        def _():
            for d in range(1, nx):
                landed(rxd.at[slot, d - 1], rx_d.at[slot, d - 1])
                landed(rxd.at[slot, d - 1], sx_d.at[slot, d - 1])
            total = gd[slot, x].astype(F32)
            for d in range(1, nx):
                total += rxd[slot, d - 1].astype(F32)
            s1d[slot] = total.astype(BF16)
            for q in range(pieces):
                _, yo, _ = grad_owner(m, q)
                part = pl.ds(q * gp, gp)

                @pl.when(yo != y)
                def _():
                    d = lax.rem(yo - y + ny, ny)
                    remote(
                        s1d.at[slot, part], ryd.at[slot, d - 1, part], sy_d.at[slot, q], ry_d.at[slot, d - 1, q], at(y=yo)
                    ).start()

    def send_z(m):
        slot = m % slots
        for d in range(1, ny):
            landed(ryg.at[slot, d - 1], ry_g.at[slot, d - 1])
            landed(ryg.at[slot, d - 1], sy_g.at[slot, d - 1])
        for zi in range(nz):
            for w in range(2):
                total = s1g[slot, y, w, zi].astype(F32)
                for d in range(1, ny):
                    total += ryg[slot, d - 1, w, zi].astype(F32)
                s2g[slot, zi, w] = total.astype(BF16)
        for d in range(1, nz):
            zo = zp(d)
            remote(s2g.at[slot, zo], rzg.at[slot, d - 1], sz_g.at[slot, d - 1], rz_g.at[slot, d - 1], at(z=zo)).start()

        @pl.when(m < chunks - 1)
        def _():
            for q in range(pieces):
                zo, yo, _ = grad_owner(m, q)
                part = pl.ds(q * gp, gp)

                @pl.when(yo != y)
                def _():
                    landed(s1d.at[slot, part], sy_d.at[slot, q])

                @pl.when(yo == y)
                def _():
                    total = s1d[slot, part].astype(F32)
                    for d in range(1, ny):
                        landed(ryd.at[slot, d - 1, part], ry_d.at[slot, d - 1, q])
                        total += ryd[slot, d - 1, part].astype(F32)
                    s2d[slot, part] = total.astype(BF16)

                    @pl.when(zo != z)
                    def _():
                        d = lax.rem(zo - z + nz, nz)
                        remote(
                            s2d.at[slot, part], rzd.at[slot, d - 1, part], sz_d.at[slot, q], rz_d.at[slot, d - 1, q], at(z=zo)
                        ).start()

    def rep(p):
        d, e = reps[p]
        return at(x=xp(d), c=lax.rem(c + e, 2))

    def finals_left(m):
        landed(fing, sem_fin.at[0])
        for p in range(len(reps)):
            landed(fing, fs_g.at[p])

        @pl.when(m < chunks - 1)
        def _():
            for q in range(pieces):
                zo, yo, _ = grad_owner(m, q)
                part = pl.ds(q * gp, gp)

                @pl.when(jnp.logical_and(yo == y, zo == z))
                def _():
                    landed(find.at[part], sem_fin.at[1 + q])
                    for p in range(len(reps)):
                        landed(find.at[part], fs_d.at[p, q])

    def finish(m):
        slot = m % slots

        @pl.when(m > 0)
        def _():
            finals_left(m - 1)

        for d in range(1, nz):
            landed(rzg.at[slot, d - 1], rz_g.at[slot, d - 1])
            landed(rzg.at[slot, d - 1], sz_g.at[slot, d - 1])
        for w in range(2):
            total = s2g[slot, z, w].astype(F32)
            for d in range(1, nz):
                total += rzg[slot, d - 1, w].astype(F32)
            fing[w] = total.astype(BF16)

        @pl.when(m < steps)
        def _():
            b = blocks(m)
            for k in range(2):
                here = fing.at[:, :, pl.ds(k * BLOCK, BLOCK)]
                there = gu_full.at[x, c, :, :, span_of(b[k] * BLOCK, BLOCK, BLOCK)]
                local(here, there, sem_fin.at[0]).start()
                for p in range(len(reps)):
                    remote(here, there, fs_g.at[p], fr_g.at[p], rep(p)).start()

        @pl.when(m >= steps)
        def _():
            there = in_full.at[x, c, pl.ds(2 * (m - steps), 2)]
            local(fing, there, sem_fin.at[0]).start()
            for p in range(len(reps)):
                remote(fing, there, fs_g.at[p], fr_i.at[p], rep(p)).start()

        @pl.when(m < chunks - 1)
        def _():
            for q in range(pieces):
                zo, yo, row = grad_owner(m, q)
                part = pl.ds(q * gp, gp)

                @pl.when(jnp.logical_and(yo == y, zo != z))
                def _():
                    landed(s2d.at[slot, part], sz_d.at[slot, q])

                @pl.when(jnp.logical_and(yo == y, zo == z))
                def _():
                    total = s2d[slot, part].astype(F32)
                    for d in range(1, nz):
                        landed(rzd.at[slot, d - 1, part], rz_d.at[slot, d - 1, q])
                        total += rzd[slot, d - 1, part].astype(F32)
                    find[part] = total.astype(BF16)

                    @pl.when(m < steps)
                    def _():
                        there = down_full.at[x, pl.ds(row, gp)]
                        local(find.at[part], there, sem_fin.at[1 + q]).start()
                        for p in range(len(reps)):
                            remote(find.at[part], there, fs_d.at[p, q], fr_d.at[p], rep(p)).start()

                    @pl.when(m >= steps)
                    def _():
                        there = out_full.at[x, pl.ds(row, gp)]
                        local(find.at[part], there, sem_fin.at[1 + q]).start()
                        for p in range(len(reps)):
                            remote(find.at[part], there, fs_d.at[p, q], fr_o.at[p], rep(p)).start()

    def give_sums():
        for i, src in enumerate((dnv, outv)):
            side = pl.ds((1 - i) * width, width)

            @pl.loop(0, tiles)
            def _(t):
                ro = span_of((1 - c) * rows + t * TILE, TILE, TILE)
                tr[span_of(t * TILE, TILE, TILE), side] = src[ro, :].astype(BF16)

            remote(tr.at[:, side], take.at[1 - i], sem_pair.at[8 + 2 * i], sem_pair.at[9 + 2 * i], at(c=1 - c)).start()
        local(spill_h, outv.at[other], sem_spill.at[7]).start()
        local(tok_in, act_a.at[mine], sem_in.at[0]).start()
        local(spill_t, act_a.at[other], sem_spill.at[6]).start()

    def loaded(t, i):
        src = spill_p.at[i, span_of(t * TILE, TILE, TILE)]
        dst = dnv.at[span_of((1 - c) * rows + i * TILE, TILE, TILE), span_of((t % 2) * chan, chan, chan)]
        return local(src, dst, sem_spill.at[(t % 2) * 3 + i])

    def mixer_back():
        mixer_load()
        conv_acc[...] = jnp.zeros_like(conv_acc)
        sg[...] = jnp.zeros_like(sg)
        for i in range(2):
            landed(take.at[1 - i], sem_pair.at[9 + 2 * i])
            landed(take.at[1 - i], sem_pair.at[8 + 2 * i])
        local(spill_h, outv.at[other], sem_spill.at[7]).wait()
        for i in range(3):
            loaded(0, i).start()

        @pl.loop(0, tiles)
        def _(t):
            rl = span_of(t * TILE, TILE, TILE)
            rs = span_of(c * rows + t * TILE, TILE, TILE)
            ro = span_of((1 - c) * rows + t * TILE, TILE, TILE)
            total = outv[rs, :] + take[0, rl, :].astype(F32)
            tr[rl, pl.ds(0, width)] = (total * live_in[rl, :]).astype(BF16)
            dn2 = dnv[rs, :] + take[1, rl, :].astype(F32)
            middle = outv[ro, :]
            scale = row_scale(middle)
            unit = middle * scale
            sg[1:2, :] += jnp.sum(dn2 * unit, axis=0, keepdims=True)
            d2 = dn2 * vec[1:2, :]
            back = scale * (d2 - unit * jnp.mean(d2 * unit, axis=-1, keepdims=True))
            back = act_b[rs, :].astype(F32) + back
            dnv[rs, :] = back
            act_b[rs, :] = back.astype(BF16)

        out = local(tr.at[:, pl.ds(0, width)], y_out, sem_in.at[1])
        out.start()
        remote(act_b.at[mine], act_b.at[mine], sem_pair.at[2], sem_pair.at[3], at(c=1 - c)).start()
        local(tok_in, act_a.at[mine], sem_in.at[0]).wait()
        local(spill_t, act_a.at[other], sem_spill.at[6]).wait()
        out.wait()

        @pl.loop(0, 2 * tiles)
        def _(t):
            rs = span_of(t * TILE, TILE, TILE)
            tr[:, rs] = normed(act_a[rs, :].astype(F32)).T

        landed(act_b.at[mine], sem_pair.at[2])
        landed(act_b.at[other], sem_pair.at[3])

        for cc in range(2):

            @pl.loop(0, seqs)
            def _(s):
                hf[span_of(s * EDGE, EDGE, EDGE), :] = act_b[span_of(cc * rows + s * span, EDGE, span), :].astype(F32)

            head = dot_nt(hf[...].astype(BF16), wout[...]).reshape(seqs, EDGE, chan)
            ks[cc * seqs : (cc + 1) * seqs] = head * chd[cc * seqs : (cc + 1) * seqs]

        @pl.when(me > 0)
        def _():
            remote(ks, kh, sem_kh.at[0], sem_kh.at[1], member(lax.rem(me + n - 1, n))).start()

        @pl.when(me == n - 1)
        def _():
            kh[...] = jnp.zeros_like(kh)

        for h in range(nx):
            side = pl.ds(h * lanes, lanes)
            gd[steps % slots, h] = dot_tn(zv[:, :CHUNK], act_b[:, side]).astype(BF16)
            og[h] = dot_tn(zv[:, CHUNK:], act_b[:, side]).astype(BF16)

        @pl.when(me < n - 1)
        def _():
            landed(kh, sem_kh.at[1])

        @pl.loop(0, 2 * tiles)
        def _(t):
            rs = span_of(t * TILE, TILE, TILE)
            first = t * tseq
            for i in range(3):
                loaded(t, i).wait()

            @pl.when(t + 1 < 2 * tiles)
            def _():
                for i in range(3):
                    loaded(t + 1, i).start()

            for h in range(2):
                hl = pl.ds(h * CHUNK, CHUNK)
                dz = dot_nt(act_b[rs, :], wout[hl, :]).reshape(tseq, span, CHUNK)
                b_gate, c_gate, x_value = (
                    dnv[
                        span_of((1 - c) * rows + i * TILE, TILE, TILE),
                        span_of((t % 2) * chan + h * CHUNK, CHUNK, CHUNK),
                    ].reshape(tseq, span, CHUNK)
                    for i in range(3)
                )
                *lags, conv = convolve((b_gate * x_value).reshape(TILE, CHUNK), first, h)
                dk = dz * c_gate
                for k in range(3):
                    conv_acc[k : k + 1, hl] += jnp.sum((dk * lags[k]).reshape(TILE, CHUNK), axis=0, keepdims=True)
                vb[:, :span, :] = dk
                vb[:, span:, :] = kh[pl.ds(first, tseq), :, hl]
                du = tap(2, h) * dk + tap(1, h) * vb[:, 1 : 1 + span, :] + tap(0, h) * vb[:, 2 : 2 + span, :]
                act_a[rs, hl] = (du * x_value).astype(BF16).reshape(TILE, CHUNK)
                act_a[rs, pl.ds(chan + h * CHUNK, CHUNK)] = (dz * conv).astype(BF16).reshape(TILE, CHUNK)
                zv[rs, hl] = (du * b_gate).astype(BF16).reshape(TILE, CHUNK)

    def share_back():
        @pl.loop(0, 2 * tiles)
        def _(t):
            rs = span_of(tile_start(t), TILE, TILE)
            total = dot_nt(act_a[rs, :CHUNK], win(0))
            for b in range(1, 6):
                src = act_a[rs, b * CHUNK : (b + 1) * CHUNK] if b < 4 else zv[rs, (b - 4) * CHUNK : (b - 3) * CHUNK]
                total += dot_nt(src, win(b))

            @pl.when(t < tiles)
            def _():
                act_b[rs, :] = total.astype(BF16)

            @pl.when(t >= tiles)
            def _():
                outv[rs, :] = total

            @pl.when(t == tiles - 1)
            def _():
                remote(act_b.at[other], take.at[0], sem_pair.at[4], sem_pair.at[5], at(c=1 - c)).start()
                local(tok_in, act_b.at[mine], sem_in.at[0]).start()

    def finish_back():
        landed(take.at[0], sem_pair.at[5])
        local(tok_in, act_b.at[mine], sem_in.at[0]).wait()

        @pl.loop(0, tiles)
        def _(t):
            rl = span_of(t * TILE, TILE, TILE)
            rs = span_of(c * rows + t * TILE, TILE, TILE)
            tokens = act_b[rs, :].astype(F32)
            scale = row_scale(tokens)
            unit = tokens * scale
            dn1 = outv[rs, :] + take[0, rl, :].astype(F32)
            sg[0:1, :] += jnp.sum(dn1 * unit, axis=0, keepdims=True)
            d1 = dn1 * vec[0:1, :]
            back = dnv[rs, :] + scale * (d1 - unit * jnp.mean(d1 * unit, axis=-1, keepdims=True))
            take[1, rl, :] = (back * live_in[rl, :]).astype(BF16)

        local(take.at[1], dx_out, sem_in.at[1]).start()
        sg[2:5, span_of(c * chan, chan, chan)] = conv_acc[0:3, :]
        local(sg, small_out, sem_in.at[0]).start()

    @pl.loop(0, chunks + 3 * LAG)
    def _(m):
        @pl.when(m < steps)
        def _():
            compute(m)

        @pl.when(m == steps - 1)
        def _():
            give_sums()

        @pl.when(m == steps)
        def _():
            mixer_back()

        @pl.when(jnp.logical_and(m >= steps, m < chunks - 1))
        def _():
            b = (m - steps) * 2 * CHUNK
            weight_grads(
                m % slots, act_a[:, span_of(b, CHUNK, CHUNK)], act_a[:, span_of(b + CHUNK, CHUNK, CHUNK)]
            )

        @pl.when(m == steps + 1)
        def _():
            gd[(steps + 1) % slots] = og[...]
            share_back()

        @pl.when(m == chunks - 1)
        def _():
            weight_grads(m % slots, zv[:, :CHUNK], zv[:, CHUNK:])

        @pl.when(m >= 3 * LAG)
        def _():
            finish(m - 3 * LAG)

        @pl.when(jnp.logical_and(m >= 2 * LAG, m < chunks + 2 * LAG))
        def _():
            send_z(m - 2 * LAG)

        @pl.when(jnp.logical_and(m >= LAG, m < chunks + LAG))
        def _():
            send_y(m - LAG)

        @pl.when(m < chunks)
        def _():
            send_x(m)

        @pl.when(m == chunks - 1)
        def _():
            finish_back()

        @pl.when(m + AHEAD < steps)
        def _():
            first_hop(m + AHEAD)

        @pl.when(m + RELAY < steps)
        def _():
            second_hop(m + RELAY)

        @pl.when(m + 1 < steps)
        def _():
            load(m + 1)

    finals_left(chunks - 1)
    landed(take.at[1], sem_in.at[1])
    landed(sg, sem_in.at[0])
    landed(take.at[0], sem_pair.at[4])

    @pl.when(me > 0)
    def _():
        landed(ks, sem_kh.at[0])

    for p in range(len(ag_peers)):
        landed(all_in.at[:, 0, 0], mg_send.at[p])
        landed(all_gu.at[:, :, 0, 0], ag_send.at[p])

        @pl.when(in_half)
        def _():
            landed(all_out.at[0], mg_osend.at[p])
            landed(all_down.at[:, pl.ds(0, gp)], ag_dsend.at[p])

    for d in range(1, nz):
        for e in range(1, ny):
            landed(all_in.at[:, 0, 0], mg_relay.at[d - 1, e - 1])
            landed(all_gu.at[:, :, 0, 0], ag_relay.at[d - 1, e - 1])
    for o in range(n // 2):
        zo, yo = out_owner(o)

        @pl.when(jnp.logical_and(zo != z, yo == y))
        def _():
            for e in range(1, ny):
                landed(all_out.at[0], mg_orelay.at[o, e - 1])

    for k in range(2):
        zo = (n // 2 * c) // ny + k

        @pl.when(zo != z)
        def _():
            for e in range(1, ny):
                landed(all_down.at[:, pl.ds(0, gp)], ag_drelay.at[zo % 2, e - 1])

    for p, (d, e) in enumerate(reps):
        landed(gu_full.at[0, 0], fr_g.at[p])
        landed(in_full.at[0, 0], fr_i.at[p])

        @pl.when(in_half if e == 0 else jnp.logical_not(in_half))
        def _():
            landed(down_full.at[0], fr_d.at[p])
            landed(out_full.at[0], fr_o.at[p])


def block_call(sizes, *operands):
    nx, nz, ny, seqs, span, width, hidden = sizes
    n = nz * ny
    rows = seqs * span
    dn = width // n
    dnx = dn // nx
    half = hidden // 2
    chan = width // 2
    steps = half // CHUNK
    own_rows = hidden // n
    gp = min(BLOCK, own_rows & -own_rows)
    pieces = CHUNK // gp
    lanes = width // nx
    s = 2 * LAG
    tseq = TILE // span
    reps = 2 * nx - 1
    hops = nz + ny - 2
    dma = lambda *dims: pltpu.SemaphoreType.DMA(dims)
    bf = lambda *dims: pltpu.VMEM(dims, BF16)
    fl = lambda *dims: pltpu.VMEM(dims, F32)
    anywhere = pl.BlockSpec(memory_space=pl.ANY)
    shape = jax.ShapeDtypeStruct
    specs = [anywhere] * 10
    specs[3] = pl.BlockSpec(memory_space=pltpu.VMEM)
    return pl.pallas_call(
        functools.partial(block_kernel, sizes),
        out_shape=[
            shape((rows, width), BF16),
            shape((rows, width), BF16),
            shape((nx, 2, 2, dnx, half), BF16),
            shape((nx, own_rows, lanes), BF16),
            shape((nx, 2, 6, dnx, CHUNK), BF16),
            shape((nx, dn, lanes), BF16),
            shape((8, width), F32),
            shape((steps, 2, nz, ny, dn, CHUNK), BF16),
            shape((steps, CHUNK, width), BF16),
            shape((6, nz, ny, dn, CHUNK), BF16),
            shape((n // 2, dn, width), BF16),
            shape((3, 2 * rows, chan), F32),
            shape((rows, width), F32),
            shape((rows, width), BF16),
        ],
        in_specs=specs,
        out_specs=[anywhere] * 14,
        scratch_shapes=[
            bf(2 * rows, width),
            bf(2 * rows, width),
            bf(width, 2 * rows),
            bf(2, nz, ny, dn, CHUNK),
            bf(CHUNK, width),
            fl(2 * rows, width),
            fl(2 * rows, width),
            bf(6, nz, ny, dn, CHUNK),
            bf(chan, width),
            bf(2 * rows, chan),
            bf(2, rows, width),
            bf(nx, CHUNK, lanes),
            fl(tseq, span + EDGE, CHUNK),
            fl(tseq, span + EDGE, CHUNK),
            bf(2, seqs, EDGE, width),
            fl(2 * seqs, EDGE, chan),
            fl(2 * seqs, EDGE, chan),
            fl(2 * seqs, EDGE, chan),
            fl(2 * seqs, EDGE, chan),
            fl(seqs * EDGE, width),
            fl(n, 8, dn),
            fl(8, width),
            fl(8, chan),
            fl(8, width),
            bf(s, 2, nx, nz, ny, dnx, CHUNK),
            bf(s, nx, CHUNK, lanes),
            bf(s, nx - 1, 2, nz, ny, dnx, CHUNK),
            bf(s, nx - 1, CHUNK, lanes),
            bf(s, ny, 2, nz, dnx, CHUNK),
            bf(s, CHUNK, lanes),
            bf(s, ny - 1, 2, nz, dnx, CHUNK),
            bf(s, ny - 1, CHUNK, lanes),
            bf(s, nz, 2, dnx, CHUNK),
            bf(s, CHUNK, lanes),
            bf(s, nz - 1, 2, dnx, CHUNK),
            bf(s, nz - 1, CHUNK, lanes),
            bf(2, dnx, CHUNK),
            bf(CHUNK, lanes),
            dma(2),
            dma(2 + n // 2),
            dma(2, steps * pieces),
            dma(12),
            dma(3),
            dma(4),
            dma(2),
            dma(8),
            dma(steps, nz - 1),
            dma(steps, ny - 1),
            dma(steps, pieces),
            dma(steps, pieces),
            dma(hops),
            dma(nz - 1, ny - 1),
            dma(hops),
            dma(2, ny - 1),
            dma(2),
            dma(nz - 1),
            dma(ny - 1),
            dma(n // 2),
            dma(n // 2),
            dma(hops),
            dma(nz - 1, ny - 1),
            dma(hops),
            dma(n // 2, ny - 1),
            dma(s, nx - 1),
            dma(s, nx - 1),
            dma(s, ny - 1),
            dma(s, ny - 1, pieces),
            dma(s, nz - 1),
            dma(s, nz - 1, pieces),
            dma(s, nx - 1),
            dma(s, nx - 1),
            dma(s, ny - 1),
            dma(s, pieces),
            dma(s, nz - 1),
            dma(s, pieces),
            dma(1 + pieces),
            dma(reps),
            dma(reps, pieces),
            dma(reps),
            dma(reps),
            dma(reps),
            dma(reps),
        ],
        compiler_params=pltpu.CompilerParams(
            collective_id=0, has_side_effects=True, vmem_limit_bytes=63 << 20
        ),
        name="gated_block",
    )(*operands)[:7]


def live_mask(lengths, deal, span):
    slots = jnp.arange(deal.shape[1], dtype=jnp.int32)
    picked = deal[0][:, None] == slots[None, :]
    source_len = jnp.sum(jnp.where(picked, lengths[0][:, None], 0), axis=0)
    position = lax.axis_index(GROUP) * span + jnp.arange(span, dtype=jnp.int32)
    return (position[None, :] < source_len[:, None]).astype(F32).reshape(-1, 1)


def body(
    tokens,
    cotangent,
    lengths,
    deal,
    norm_gain,
    in_weight,
    conv_weight,
    out_weight,
    ffn_gain,
    gate_weight,
    up_weight,
    down_weight,
):
    seqs, span, width = tokens.shape
    hidden = gate_weight.shape[1]
    nx, nz, ny = (lax.axis_size(axis) for axis in ("x", "z", "y"))
    dn = width // (nz * ny)
    small = jnp.stack([norm_gain, ffn_gain, *(conv_weight[:, k] for k in range(3))]).astype(F32)
    small = jnp.pad(small, ((0, 3), (0, 0)))
    block_out, block_grad, gu, down, mixer_in, mixer_out, sums = block_call(
        (nx, nz, ny, seqs, span, width, hidden),
        tokens.reshape(-1, width),
        tokens,
        cotangent.reshape(-1, width),
        live_mask(lengths, deal, span),
        small,
        in_weight,
        out_weight,
        gate_weight,
        up_weight,
        down_weight,
    )
    sums = lax.psum(sums, ("x", "core", "z", "y"))
    sums = lax.dynamic_slice_in_dim(sums, lax.axis_index(GROUP) * dn, dn, axis=1)
    gate_grad = gu[:, :, 0].transpose(0, 2, 1, 3).reshape(dn, hidden).astype(F32)
    up_grad = gu[:, :, 1].transpose(0, 2, 1, 3).reshape(dn, hidden).astype(F32)
    mixer_in = mixer_in.reshape(nx, 2, 3, 2, dn // nx, CHUNK)
    in_grad = mixer_in.transpose(0, 4, 2, 1, 3, 5).reshape(dn, 3 * width).astype(F32)
    out_grad = mixer_out.transpose(1, 0, 2).reshape(dn, width).astype(F32)
    down_grad = down.transpose(1, 0, 2).reshape(-1, width).astype(F32)
    return (
        block_out.reshape(tokens.shape),
        block_grad.reshape(tokens.shape),
        sums[0],
        in_grad,
        sums[2:5].T,
        out_grad,
        sums[1],
        gate_grad,
        up_grad,
        down_grad,
    )


def solution(mesh):
    rep, fsdp = mesh.shape["rep"], mesh.shape["fsdp"]
    grid = (rep // 2, 2, 4, fsdp // 4)
    split = Mesh(mesh.devices.reshape(grid), ("x", "core", "z", "y"))
    copies = ("x", "core")
    rows = P(copies, GROUP, None)
    lists = P(copies, None)
    vector = P(GROUP)
    matrix = P(GROUP, None)
    return jax.shard_map(
        body,
        mesh=split,
        in_specs=(
            rows,
            rows,
            lists,
            lists,
            vector,
            matrix,
            matrix,
            matrix,
            vector,
            matrix,
            matrix,
            matrix,
        ),
        out_specs=(rows, rows, vector, matrix, matrix, matrix, vector, matrix, matrix, matrix),
        check_vma=False,
    )
```

```python
import functools
import jax
import jax.numpy as jnp
from jax import lax
from jax.experimental import pallas as pl
from jax.experimental.pallas import tpu as pltpu
from jax.sharding import Mesh, PartitionSpec as P

EPS = 1e-05
F32 = jnp.float32
BF16 = jnp.bfloat16
NT = (((1,), (1,)), ((), ()))
TN = (((0,), (0,)), ((), ()))
MESH = pl.DeviceIdType.MESH
GROUP = ("z", "y")
CHUNK = 256
BLOCK = 128
TILE = 256
EDGE = 8
AHEAD = 4
RELAY = 2
HOLD = 4


def dot(left, right):
    return jnp.dot(left, right, preferred_element_type=F32)


def dot_nt(left, right):
    return lax.dot_general(left, right, NT, preferred_element_type=F32)


def dot_tn(left, right):
    return lax.dot_general(left, right, TN, preferred_element_type=F32)


def row_scale(values):
    return lax.rsqrt(jnp.mean(values * values, axis=-1, keepdims=True) + EPS)


def block_kernel(
    sizes,
    tok_in, edge_in, cot_in, live_in, small_in, in_in, out_in, gate_in, up_in, down_in,
    y_out, dx_out, gu_full, down_full, in_full, out_full, small_out,
    all_gu, all_down, all_in, all_out, spill_p, spill_h, spill_t,
    h1g, h1d, hyg, hyd, h2g, h2d, hzg, hzd,
    act_a, act_b, tr, wgu, wd, outv, dnv, acts, wout, zv, take, og,
    ub, vb, hal, uh, kh, ks, chd, hf, smallv, vec, conv_acc, sg, sg_all, sg_mine, sg_parts,
    ggu, gd, rxg, rxd, s1g, s1d, y1g, y1d, yrg, yrd, z2g, z2d, zrg, zrd, fing, find,
    sem_in, sem_load, sem_own, sem_pair, sem_small, sem_edge, sem_kh, sem_spill,
    ag_far, ag_z, ag_y, ag_dz, ag_dy, ag_send, ag_relay, ag_dsend, ag_drelay,
    mg_own, mg_z, mg_y, mg_oz, mg_oy, mg_send, mg_relay, mg_osend, mg_orelay,
    rx_g, rx_d, sx_g, sx_d, st1, ry_g, ry_d, sy_g, sy_d, ld1, st2, rz_g, rz_d, sz_g, sz_d, ld2, st3,
    fs_g, fs_i, fs_d, fs_o, fr_g, fr_i, fr_d, fr_o, sem_sum,
):
    nx, nz, ny, seqs, span, width, hidden = sizes
    n = nz * ny
    rows = seqs * span
    dn = width // n
    dnx = dn // nx
    half = hidden // 2
    chan = width // 2
    steps = half // CHUNK
    chunks = steps + 3
    per_half = half // BLOCK // 2
    own_rows = hidden // n
    gp = min(BLOCK, own_rows & -own_rows)
    pieces = CHUNK // gp
    lanes = width // nx
    slots = 2
    tiles = rows // TILE
    tseq = TILE // span
    x, c = lax.axis_index("x"), lax.axis_index("core")
    z, y = lax.axis_index("z"), lax.axis_index("y")
    me = z * ny + y
    in_half = me // (n // 2) == c

    def at(x=x, c=c, z=z, y=y):
        return (x, c, z, y)

    def member(j, c=c):
        return at(c=c, z=j // ny, y=j % ny)

    def zp(d):
        return lax.rem(z + d, nz)

    def yp(d):
        return lax.rem(y + d, ny)

    def xp(d):
        return lax.rem(x + d, nx)

    def remote(src, dst, ssem, rsem, dev):
        return pltpu.make_async_remote_copy(
            src_ref=src, dst_ref=dst, send_sem=ssem, recv_sem=rsem, device_id=dev, device_id_type=MESH
        )

    def local(src, dst, sem):
        return pltpu.make_async_copy(src, dst, sem)

    def landed(ref, sem):
        pltpu.make_async_copy(ref, ref, sem).wait()

    def span_of(start, size, align):
        return pl.ds(pl.multiple_of(start, align), size)

    mine = span_of(c * rows, rows, rows)
    other = span_of((1 - c) * rows, rows, rows)

    barrier = pltpu.get_barrier_semaphore()
    peers = [member(lax.rem(me + d, n)) for d in range(1, n)]
    reps = [(d, e) for d in range(nx) for e in range(2) if d + e > 0]
    peers += [at(x=xp(d), c=lax.rem(c + e, 2)) for d, e in reps]
    peers += [member(lax.rem(me + d, n), c=1 - c) for d in (1, n - 1)]
    for dev in peers:
        pl.semaphore_signal(barrier, inc=1, device_id=dev, device_id_type=MESH)
    pl.semaphore_wait(barrier, len(peers))

    local(small_in, smallv.at[me], sem_small.at[0]).start()
    for d in range(1, n):
        remote(small_in, smallv.at[me], sem_small.at[1], sem_small.at[2], member(lax.rem(me + d, n))).start()

    @pl.when(me < n - 1)
    def _():
        for e in range(2):
            src = edge_in.at[:, pl.ds(span - EDGE, EDGE)]
            dev = member(lax.rem(me + 1, n), c=lax.rem(c + e, 2))
            remote(src, hal.at[c], sem_edge.at[e], sem_edge.at[2 + c], dev).start()

    local(tok_in, act_a.at[mine], sem_in.at[0]).start()
    local(cot_in, take.at[1], sem_in.at[1]).start()
    remote(tok_in, act_a.at[mine], sem_pair.at[0], sem_pair.at[1], at(c=1 - c)).start()

    ag_peers = [(0, d) for d in range(1, nz)] + [(1, d) for d in range(1, ny)]

    def toward(ax, d):
        return at(z=zp(d)) if ax == 0 else at(y=yp(d))

    def mixer_first_hop(b):
        here = in_in.at[:, span_of((b // 2) * width + c * chan + (b % 2) * CHUNK, CHUNK, CHUNK)]
        there = all_in.at[b, z, y]
        local(here, there, mg_own.at[0]).start()
        hops(here, there, mg_send, lambda d: mg_z.at[b, d - 1], lambda d: mg_y.at[b, d - 1])

    def out_first_hop():
        @pl.when(in_half)
        def _():
            o = me - c * (n // 2)
            local(out_in, all_out.at[o], mg_own.at[1]).start()
            hops(out_in, all_out.at[o], mg_osend, lambda d: mg_oz.at[o], lambda d: mg_oy.at[o])

    def off(zs):
        return (zs - z) * (zs - z)

    inner = jnp.logical_and(z > 0, z < nz - 1)
    end = jnp.where(z == 1, 0, nz - 1)
    end_slot = jnp.where(z == 1, 0, nz - 2)

    def hops(here, there, send, recv_z, recv_y):
        for p, (ax, d) in enumerate(ag_peers):
            if ax == 1:
                remote(here, there, send.at[p], recv_y(d), toward(ax, d)).start()
            elif d in (1, nz - 1):

                @pl.when(off(zp(d)) < (nz - 1) ** 2)
                def _():
                    remote(here, there, send.at[p], recv_z(d), toward(ax, d)).start()
            else:
                remote(here, there, send.at[p], recv_z(d), toward(ax, d)).start()

    def out_owner(o):
        j = c * (n // 2) + o
        return j // ny, j % ny

    def along_y(block, send, recv):
        for e in range(1, ny):
            remote(block, block, send.at[e - 1], recv(e), at(y=yp(e))).start()

    def along(block, d, near, arrived, far_send, far_recv, y_send, y_recv):
        if d in (1, nz - 1):
            this = off(lax.rem(z - d + nz, nz)) == (nz - 1) ** 2

            @pl.when(jnp.logical_not(this) if near else this)
            def _():
                landed(block, arrived)
                along_y(block, y_send, y_recv)
        elif near:
            landed(block, arrived)

            @pl.when(inner)
            def _():
                remote(block, block, far_send, far_recv, at(z=end)).start()

            along_y(block, y_send, y_recv)

    def mixer_hop(b, near):
        for d in range(1, nz):
            block = all_in.at[b, lax.rem(z - d + nz, nz), y]
            along(
                block, d, near, mg_z.at[b, d - 1], ag_far.at[0], mg_z.at[b, end_slot], mg_relay.at[d - 1], lambda e: mg_y.at[b, e - 1]
            )

    def owned(block, zo, near, arrived, far_send, y_send, y_recv):
        @pl.when(off(zo) < (nz - 1) ** 2 if near else off(zo) == (nz - 1) ** 2)
        def _():
            landed(block, arrived)

            @pl.when(jnp.logical_and(inner, off(zo) == 4))
            def _():
                remote(block, block, far_send, arrived, at(z=end)).start()

            along_y(block, y_send, y_recv)

    def out_hop(near):
        for o in range(n // 2):
            zo, yo = out_owner(o)

            @pl.when(jnp.logical_and(zo != z, yo == y))
            def _():
                owned(all_out.at[o], zo, near, mg_oz.at[o], ag_far.at[1], mg_orelay.at[o], lambda e: mg_oy.at[o])

    def mixer_arrived():
        for e in range(1, ny):
            for b in range(6):
                landed(all_in.at[b, :, lax.rem(y - e + ny, ny)], mg_y.at[b, e - 1])
        for o in range(n // 2):
            _, yo = out_owner(o)

            @pl.when(yo != y)
            def _():
                landed(all_out.at[o], mg_oy.at[o])

        landed(all_in.at[:, 0, 0], mg_own.at[0])

        @pl.when(in_half)
        def _():
            landed(all_out.at[0], mg_own.at[1])

    def mixer_load():
        copies = [local(all_in, acts, sem_load.at[0])]
        copies += [local(all_out.at[o], wout.at[pl.ds(o * dn, dn)], sem_load.at[2 + o]) for o in range(n // 2)]
        for copy in copies:
            copy.start()
        for copy in copies:
            copy.wait()

    def blocks(m):
        h, i = m % 2, m // 2
        first = per_half * h + i
        return first, per_half * h + per_half - 1 - i + per_half * (m // (2 * (per_half // 2)))

    def column(b):
        return pl.multiple_of(c * half + b * BLOCK, BLOCK)

    def owner(m, q):
        b = blocks(m)[q * gp // BLOCK]
        row = c * half + b * BLOCK + (q * gp) % BLOCK
        j = row // own_rows
        return j // ny, j % ny, pl.multiple_of(row - j * own_rows, gp)

    def grad_owner(m, q):
        zo, yo, row = owner(jnp.minimum(m, steps - 1), q)
        mixed = c * chan + jnp.maximum(m - steps, 0) * CHUNK + q * gp
        j = mixed // dn
        late = m >= steps
        return (
            jnp.where(late, j // ny, zo),
            jnp.where(late, j % ny, yo),
            pl.multiple_of(jnp.where(late, mixed - j * dn, row), gp),
        )

    def first_hop(m):
        b = blocks(m)
        for k in range(2):
            for w, src in enumerate((gate_in, up_in)):
                here = src.at[:, pl.ds(column(b[k]), BLOCK)]
                there = all_gu.at[m, w, z, y, :, pl.ds(k * BLOCK, BLOCK)]
                local(here, there, sem_own.at[0, m]).start()
                hops(here, there, ag_send, lambda d: ag_z.at[m, d - 1], lambda d: ag_y.at[m, d - 1])
        for q in range(pieces):
            zo, yo, row = owner(m, q)

            @pl.when(jnp.logical_and(zo == z, yo == y))
            def _():
                here = down_in.at[pl.ds(row, gp)]
                there = all_down.at[m, pl.ds(q * gp, gp)]
                local(here, there, sem_own.at[1, m * pieces + q]).start()
                hops(here, there, ag_dsend, lambda d: ag_dz.at[m, q], lambda d: ag_dy.at[m, q])

    def next_hop(m, near):
        for d in range(1, nz):
            block = all_gu.at[m, :, lax.rem(z - d + nz, nz), y]
            along(
                block, d, near, ag_z.at[m, d - 1], ag_far.at[2], ag_z.at[m, end_slot], ag_relay.at[d - 1], lambda e: ag_y.at[m, e - 1]
            )
        for q in range(pieces):
            zo, yo, _ = owner(m, q)

            @pl.when(jnp.logical_and(zo != z, yo == y))
            def _():
                block = all_down.at[m, pl.ds(q * gp, gp)]
                owned(block, zo, near, ag_dz.at[m, q], ag_far.at[3], ag_drelay.at[zo % 2], lambda e: ag_dy.at[m, q])

    def load(m):
        landed(all_gu.at[m, :, 0, 0], sem_own.at[0, m])
        for e in range(1, ny):
            landed(all_gu.at[m, :, :, lax.rem(y - e + ny, ny)], ag_y.at[m, e - 1])
        for q in range(pieces):
            zo, yo, _ = owner(m, q)
            block = all_down.at[m, pl.ds(q * gp, gp)]

            @pl.when(jnp.logical_and(zo == z, yo == y))
            def _():
                landed(block, sem_own.at[1, m * pieces + q])

            @pl.when(yo != y)
            def _():
                landed(block, ag_dy.at[m, q])

        local(all_gu.at[m], wgu, sem_load.at[0]).start()
        local(all_down.at[m], wd, sem_load.at[1]).start()

    def loaded_weights():
        landed(wgu, sem_load.at[0])
        landed(wd, sem_load.at[1])

    def pass_on(m):
        @pl.when(m < steps)
        def _():
            next_hop(m, True)

    def pass_on_far(m):
        @pl.when(m < steps)
        def _():
            next_hop(m, False)

        @pl.when(m + AHEAD - RELAY < steps)
        def _():
            first_hop(m + AHEAD - RELAY)

    for b in range(3):
        mixer_first_hop(b)

    local(cot_in, take.at[1], sem_in.at[1]).wait()

    @pl.loop(0, tiles)
    def _(t):
        rl = span_of(t * TILE, TILE, TILE)
        rs = span_of(c * rows + t * TILE, TILE, TILE)
        act_b[rs, :] = (take[1, rl, :].astype(F32) * live_in[rl, :]).astype(BF16)

    remote(act_b.at[mine], act_b.at[mine], sem_pair.at[2], sem_pair.at[3], at(c=1 - c)).start()

    landed(small_in, sem_small.at[0])
    landed(smallv.at[pl.ds(0, n - 1)], sem_small.at[1])
    landed(smallv.at[pl.ds(0, n - 1)], sem_small.at[2])
    for j in range(n):
        vec[:, j * dn : (j + 1) * dn] = smallv[j]

    @pl.when(me < n - 1)
    def _():
        for e in range(2):
            landed(hal.at[0], sem_edge.at[e])

    @pl.when(me > 0)
    def _():
        for e in range(2):
            landed(hal.at[e], sem_edge.at[2 + e])

    @pl.when(me == 0)
    def _():
        hal[...] = jnp.zeros_like(hal)

    for b in range(6):
        mixer_hop(b, True)
        if b > 0:
            mixer_hop(b - 1, False)
        if b < 3:
            mixer_first_hop(b + 3)
        elif b == 3:
            out_first_hop()
        else:
            first_hop(b - 4)
    mixer_hop(5, False)
    out_hop(True)
    out_hop(False)
    local(tok_in, act_a.at[mine], sem_in.at[0]).wait()
    landed(act_a.at[mine], sem_pair.at[0])
    landed(act_a.at[other], sem_pair.at[1])
    local(act_a.at[other], spill_t, sem_spill.at[6]).start()
    mixer_arrived()
    mixer_load()

    def win(b):
        return acts[b].reshape(width, CHUNK)

    def tap(k, h):
        return vec[2 + k : 3 + k, span_of(c * chan + h * CHUNK, CHUNK, CHUNK)].reshape(1, 1, CHUNK)

    def normed(tokens):
        return (tokens * row_scale(tokens) * vec[0:1, :]).astype(BF16)

    for cc in range(2):
        edge = normed(hal[cc].astype(F32).reshape(seqs * EDGE, width))
        for h in range(2):
            product = dot(edge, win(h)) * dot(edge, win(4 + h))
            uh[cc * seqs : (cc + 1) * seqs, :, h * CHUNK : (h + 1) * CHUNK] = product.reshape(seqs, EDGE, CHUNK)

    def convolve(product, first, h):
        ub[:, :EDGE, :] = uh[pl.ds(first, tseq), :, h * CHUNK : (h + 1) * CHUNK]
        ub[:, EDGE:, :] = product.reshape(tseq, span, CHUNK)
        lag_two = ub[:, EDGE - 2 : EDGE - 2 + span, :]
        lag_one = ub[:, EDGE - 1 : EDGE - 1 + span, :]
        lag_none = ub[:, EDGE:, :]
        return lag_two, lag_one, lag_none, tap(0, h) * lag_two + tap(1, h) * lag_one + tap(2, h) * lag_none

    def spilled(t, i, rs):
        slot = t % 2
        src = dnv.at[span_of(slot * 3 * TILE + i * TILE, TILE, TILE), pl.ds(0, chan)]
        return local(src, spill_p.at[i, rs], sem_spill.at[slot * 3 + i])

    def tile_start(t):
        return lax.rem(t + (1 - c) * tiles, 2 * tiles) * TILE

    @pl.loop(0, 2 * tiles)
    def _(t):
        start = tile_start(t)
        rs = span_of(start, TILE, TILE)
        first = start // span
        tokens = act_a[rs, :].astype(F32)
        n1 = normed(tokens)

        @pl.when(t >= 2)
        def _():
            for i in range(3):
                spilled(t, i, rs).wait()

        for h in range(2):
            parts = [dot(n1, win(2 * i + h)) for i in range(3)]
            hl = pl.ds(h * CHUNK, CHUNK)
            for i in range(3):
                dnv[span_of((t % 2) * 3 * TILE + i * TILE, TILE, TILE), hl] = parts[i]
            chd[pl.ds(first, tseq), :, hl] = parts[1].reshape(tseq, span, CHUNK)[:, :EDGE]
            conv = convolve(parts[0] * parts[2], first, h)[3].reshape(TILE, CHUNK)
            zv[rs, hl] = (parts[1] * conv).astype(BF16)
        for i in range(3):
            spilled(t, i, rs).start()
        mixed = dot(zv[rs, :], wout[...])

        @pl.when(t < tiles)
        def _():
            tr[span_of(t * TILE, TILE, TILE), pl.ds(0, width)] = mixed.astype(BF16)

        @pl.when(t >= tiles)
        def _():
            outv[rs, :] = act_a[rs, :].astype(F32) + mixed

        @pl.when(lax.rem(t, tiles) == 1)
        def _():
            pass_on(t // tiles)

        @pl.when(lax.rem(t, tiles) == tiles - 1)
        def _():
            pass_on_far(t // tiles)

        @pl.when(t == tiles - 1)
        def _():
            landed(act_a.at[other], sem_spill.at[6])
            remote(tr.at[:, pl.ds(0, width)], take.at[0], sem_pair.at[4], sem_pair.at[5], at(c=1 - c)).start()

    for slot in range(2):
        for i in range(3):
            spilled(slot, i, pl.ds(0, TILE)).wait()
    landed(take.at[0], sem_pair.at[5])

    @pl.loop(0, tiles)
    def _(t):
        rs = span_of(c * rows + t * TILE, TILE, TILE)
        middle = outv[rs, :] + take[0, span_of(t * TILE, TILE, TILE), :].astype(F32)
        outv[rs, :] = middle
        act_a[rs, :] = (middle * row_scale(middle) * vec[1:2, :]).astype(BF16)

    remote(act_a.at[mine], act_a.at[mine], sem_pair.at[6], sem_pair.at[7], at(c=1 - c)).start()
    local(outv.at[mine], spill_h, sem_spill.at[7]).start()
    landed(take.at[0], sem_pair.at[4])

    @pl.loop(0, tiles)
    def _(t):
        ro = span_of((1 - c) * rows + t * TILE, TILE, TILE)
        rs = span_of(c * rows + t * TILE, TILE, TILE)
        outv[ro, :] = jnp.zeros((TILE, width), F32)
        dnv[ro, :] = jnp.zeros((TILE, width), F32)
        dnv[rs, :] = jnp.zeros((TILE, width), F32)

    landed(act_a.at[other], sem_pair.at[7])
    landed(act_a.at[mine], sem_pair.at[6])
    landed(act_b.at[other], sem_pair.at[3])
    landed(act_b.at[mine], sem_pair.at[2])

    @pl.loop(0, 2 * tiles)
    def _(t):
        rs = span_of(t * TILE, TILE, TILE)
        tr[:, rs] = act_a[rs, :].T

    local(outv.at[mine], spill_h, sem_spill.at[7]).wait()
    load(0)
    loaded_weights()

    big = 512
    zb = big // (ny * dn)

    def hid(w):
        return acts[2 * w : 2 * w + 2].reshape(2 * rows, CHUNK)

    def compute(m):
        slot = m % slots

        @pl.loop(0, 2 * rows // big)
        def _(r):
            rs = span_of(r * big, big, big)
            gate = wgu[0].reshape(width, CHUNK)
            up = wgu[1].reshape(width, CHUNK)
            n2r = act_a[rs, :]
            g = dot(n2r, gate)
            v = dot(n2r, up)
            s = jax.nn.sigmoid(g)
            sg_ = g * s
            q = (sg_ * v).astype(BF16)
            dq = dot_nt(act_b[rs, :], wd[...])
            gg = (dq * v * s * (1.0 + g * (1.0 - s))).astype(BF16)
            gv = (dq * sg_).astype(BF16)
            zi = pl.ds((r % 2) * zb, zb)
            for w, value in enumerate((q, gg, gv)):
                acts[2 * w + r // 2, zi] = value.reshape(zb, ny, dn, CHUNK)
            outv[rs, :] += dot(q, wd[...])

            @pl.when(r == 1)
            def _():
                pass_on(m + RELAY)

            dnv[rs, :] += dot_nt(gg, gate) + dot_nt(gv, up)

        @pl.when(m + 1 < steps)
        def _():
            load(m + 1)

        weight_grads(slot, hid(1), hid(2))
        for h in range(nx):
            gd[slot, h] = dot_tn(hid(0), act_b[:, pl.ds(h * lanes, lanes)]).astype(BF16)

    def weight_grads(slot, first, second):
        group = n // 4

        @pl.loop(0, 4)
        def _(t):
            a = tr[span_of(t * TILE, TILE, TILE), :]
            for w, src in enumerate((first, second)):
                full = dot(a, src).astype(BF16).reshape(group, nx, dnx, CHUNK)
                for h in range(nx):
                    for k in range(group):
                        j = t * group + k
                        ggu[slot, w, h, j // ny, j % ny] = full[k, h]

    def send_x(m):
        slot = m % slots
        for d in range(1, nx):
            xo = xp(d)
            remote(ggu.at[slot, :, xo], rxg.at[slot, d - 1], sx_g.at[slot, d - 1], rx_g.at[slot, d - 1], at(x=xo)).start()

            @pl.when(m < chunks - 1)
            def _():
                remote(gd.at[slot, xo], rxd.at[slot, d - 1], sx_d.at[slot, d - 1], rx_d.at[slot, d - 1], at(x=xo)).start()

    def sum_x(m):
        slot = m % slots
        for d in range(1, nx):
            landed(rxg.at[slot, d - 1], rx_g.at[slot, d - 1])
            landed(rxg.at[slot, d - 1], sx_g.at[slot, d - 1])

        @pl.loop(0, nz)
        def _(zi):
            for yi in range(ny):
                for w in range(2):
                    total = ggu[slot, w, x, zi, yi].astype(F32)
                    for d in range(1, nx):
                        total += rxg[slot, d - 1, w, zi, yi].astype(F32)
                    s1g[yi, w, zi] = total.astype(BF16)

        local(s1g, h1g.at[m], st1.at[0]).start()

        @pl.when(m < chunks - 1)
        def _():
            for d in range(1, nx):
                landed(rxd.at[slot, d - 1], rx_d.at[slot, d - 1])
                landed(rxd.at[slot, d - 1], sx_d.at[slot, d - 1])
            total = gd[slot, x].astype(F32)
            for d in range(1, nx):
                total += rxd[slot, d - 1].astype(F32)
            s1d[...] = total.astype(BF16)
            copy = local(s1d, h1d.at[m], st1.at[1])
            copy.start()
            copy.wait()

        landed(s1g, st1.at[0])

    def send_y(m, _):
        for d in range(1, ny):
            yo = yp(d)
            remote(h1g.at[m, yo], hyg.at[m, d - 1], sy_g.at[m], ry_g.at[m], at(y=yo)).start()

        @pl.when(m < chunks - 1)
        def _():
            for q in range(pieces):
                _, yo, _ = grad_owner(m, q)
                part = pl.ds(q * gp, gp)

                @pl.when(yo != y)
                def _():
                    d = lax.rem(yo - y + ny, ny)
                    remote(h1d.at[m, part], hyd.at[m, d - 1, part], sy_d.at[m, q], ry_d.at[m, q], at(y=yo)).start()

    def y_copies(m, i):
        copies = [local(h1g.at[m, y], y1g.at[i], ld1.at[i, 0]), local(hyg.at[m], yrg.at[i], ld1.at[i, 1])]
        late = [local(h1d.at[m], y1d.at[i], ld1.at[i, 2]), local(hyd.at[m], yrd.at[i], ld1.at[i, 3])]
        return copies, late

    def fetch_y(m, i):
        landed(hyg.at[m], ry_g.at[m])
        copies, late = y_copies(m, i)
        for copy in copies:
            copy.start()

        @pl.when(m < chunks - 1)
        def _():
            for q in range(pieces):
                _, yo, _ = grad_owner(m, q)

                @pl.when(yo == y)
                def _():
                    landed(hyd.at[m, :, pl.ds(q * gp, gp)], ry_d.at[m, q])

            for copy in late:
                copy.start()

    def send_z(m, i):
        copies, late = y_copies(m, i)
        for copy in copies:
            copy.wait()
        for zi in range(nz):
            for w in range(2):
                total = y1g[i, w, zi].astype(F32)
                for d in range(1, ny):
                    total += yrg[i, d - 1, w, zi].astype(F32)
                s1g[0, w, zi] = total.astype(BF16)
        stores = [local(s1g.at[0], h2g.at[m], st2.at[0]), local(s1d, h2d.at[m], st2.at[1])]
        stores[0].start()

        @pl.when(m < chunks - 1)
        def _():
            for copy in late:
                copy.wait()
            total = y1d[i].astype(F32)
            for d in range(1, ny):
                total += yrd[i, d - 1].astype(F32)
            s1d[...] = total.astype(BF16)
            stores[1].start()
            stores[1].wait()

        stores[0].wait()
        for d in range(1, nz):
            zo = zp(d)
            remote(h2g.at[m, :, zo], hzg.at[m, d - 1], sz_g.at[m], rz_g.at[m], at(z=zo)).start()

        @pl.when(m < chunks - 1)
        def _():
            for q in range(pieces):
                zo, yo, _ = grad_owner(m, q)
                part = pl.ds(q * gp, gp)

                @pl.when(jnp.logical_and(yo == y, zo != z))
                def _():
                    d = lax.rem(zo - z + nz, nz)
                    remote(h2d.at[m, part], hzd.at[m, d - 1, part], sz_d.at[m, q], rz_d.at[m, q], at(z=zo)).start()

    def z_copies(m, i):
        copies = [local(h2g.at[m, :, z], z2g.at[i], ld2.at[i, 0]), local(hzg.at[m], zrg.at[i], ld2.at[i, 1])]
        late = [local(h2d.at[m], z2d.at[i], ld2.at[i, 2]), local(hzd.at[m], zrd.at[i], ld2.at[i, 3])]
        return copies, late

    def fetch_z(m, i):
        landed(hzg.at[m], rz_g.at[m])
        copies, late = z_copies(m, i)
        for copy in copies:
            copy.start()

        @pl.when(m < chunks - 1)
        def _():
            for q in range(pieces):
                zo, yo, _ = grad_owner(m, q)

                @pl.when(jnp.logical_and(yo == y, zo == z))
                def _():
                    landed(hzd.at[m, :, pl.ds(q * gp, gp)], rz_d.at[m, q])

            for copy in late:
                copy.start()

    def rep(p):
        d, e = reps[p]
        return at(x=xp(d), c=lax.rem(c + e, 2))

    def spread(there, ssem, rsem):
        for p in range(len(reps)):
            remote(there, there, ssem.at[p], rsem.at[p], rep(p)).start()

    def finish(m, i):
        copies, late = z_copies(m, i)
        for copy in copies:
            copy.wait()
        for w in range(2):
            total = z2g[i, w].astype(F32)
            for d in range(1, nz):
                total += zrg[i, d - 1, w].astype(F32)
            fing[w] = total.astype(BF16)

        @pl.when(m < steps)
        def _():
            b = blocks(m)
            for k in range(2):
                there = gu_full.at[x, c, :, :, span_of(b[k] * BLOCK, BLOCK, BLOCK)]
                copy = local(fing.at[:, :, pl.ds(k * BLOCK, BLOCK)], there, st3.at[0])
                copy.start()
                copy.wait()
                spread(there, fs_g, fr_g)

        @pl.when(m >= steps)
        def _():
            there = in_full.at[x, c, pl.ds(2 * (m - steps), 2)]
            copy = local(fing, there, st3.at[0])
            copy.start()
            copy.wait()
            spread(there, fs_i, fr_i)

        @pl.when(m < chunks - 1)
        def _():
            for copy in late:
                copy.wait()
            for q in range(pieces):
                zo, yo, row = grad_owner(m, q)
                part = pl.ds(q * gp, gp)

                @pl.when(jnp.logical_and(yo == y, zo == z))
                def _():
                    total = z2d[i, part].astype(F32)
                    for d in range(1, nz):
                        total += zrd[i, d - 1, part].astype(F32)
                    find[...] = total.astype(BF16)

                    @pl.when(m < steps)
                    def _():
                        there = down_full.at[x, pl.ds(row, gp)]
                        copy = local(find, there, st3.at[1])
                        copy.start()
                        copy.wait()
                        spread(there, fs_d, fr_d)

                    @pl.when(m >= steps)
                    def _():
                        there = out_full.at[x, pl.ds(row, gp)]
                        copy = local(find, there, st3.at[1])
                        copy.start()
                        copy.wait()
                        spread(there, fs_o, fr_o)

    def gone(m):
        return jnp.clip(jnp.minimum(m, 2 * (m - HOLD)), 0, chunks)

    def two(m, do):
        for i in range(2):
            k = gone(m - 1) + i

            @pl.when(k < gone(m))
            def _():
                do(k, i)

    def own_rep():
        return x * 2 + c

    def sum_reps():
        local(sg, sg_all.at[own_rep()], sem_sum.at[0]).start()
        for p in range(len(reps)):
            remote(sg, sg_all.at[own_rep()], sem_sum.at[1], sem_sum.at[2], rep(p)).start()

    def sum_group():
        landed(sg, sem_sum.at[0])
        landed(sg_all.at[pl.ds(0, len(reps))], sem_sum.at[1])
        landed(sg_all.at[pl.ds(0, len(reps))], sem_sum.at[2])
        total = sg_all[0]
        for p in range(1, 2 * nx):
            total += sg_all[p]
        for j in range(n):
            sg_mine[j] = total[:, j * dn : (j + 1) * dn]
        local(sg_mine.at[me], sg_parts.at[me], sem_sum.at[3]).start()
        for d in range(1, n):
            j = lax.rem(me + d, n)
            remote(sg_mine.at[j], sg_parts.at[me], sem_sum.at[4], sem_sum.at[5], member(j)).start()

    def sum_last():
        landed(sg_mine.at[0], sem_sum.at[3])
        landed(sg_parts.at[pl.ds(0, n - 1)], sem_sum.at[4])
        landed(sg_parts.at[pl.ds(0, n - 1)], sem_sum.at[5])
        total = sg_parts[0]
        for j in range(1, n):
            total += sg_parts[j]
        smallv[0] = total
        local(smallv.at[0], small_out, sem_in.at[0]).start()

    def give_sums():
        for i, src in enumerate((dnv, outv)):
            side = pl.ds((1 - i) * width, width)

            @pl.loop(0, tiles)
            def _(t):
                ro = span_of((1 - c) * rows + t * TILE, TILE, TILE)
                tr[span_of(t * TILE, TILE, TILE), side] = src[ro, :].astype(BF16)

            remote(tr.at[:, side], take.at[1 - i], sem_pair.at[8 + 2 * i], sem_pair.at[9 + 2 * i], at(c=1 - c)).start()
        local(spill_h, outv.at[other], sem_spill.at[7]).start()
        local(tok_in, act_a.at[mine], sem_in.at[0]).start()
        local(spill_t, act_a.at[other], sem_spill.at[6]).start()

    def loaded(t, i):
        src = spill_p.at[i, span_of(t * TILE, TILE, TILE)]
        dst = dnv.at[span_of((1 - c) * rows + i * TILE, TILE, TILE), span_of((t % 2) * chan, chan, chan)]
        return local(src, dst, sem_spill.at[(t % 2) * 3 + i])

    def mixer_back():
        mixer_load()
        conv_acc[...] = jnp.zeros_like(conv_acc)
        sg[...] = jnp.zeros_like(sg)
        for i in range(2):
            landed(take.at[1 - i], sem_pair.at[9 + 2 * i])
            landed(take.at[1 - i], sem_pair.at[8 + 2 * i])
        local(spill_h, outv.at[other], sem_spill.at[7]).wait()
        for i in range(3):
            loaded(0, i).start()

        @pl.loop(0, tiles)
        def _(t):
            rl = span_of(t * TILE, TILE, TILE)
            rs = span_of(c * rows + t * TILE, TILE, TILE)
            ro = span_of((1 - c) * rows + t * TILE, TILE, TILE)
            total = outv[rs, :] + take[0, rl, :].astype(F32)
            tr[rl, pl.ds(0, width)] = (total * live_in[rl, :]).astype(BF16)
            dn2 = dnv[rs, :] + take[1, rl, :].astype(F32)
            middle = outv[ro, :]
            scale = row_scale(middle)
            unit = middle * scale
            sg[1:2, :] += jnp.sum(dn2 * unit, axis=0, keepdims=True)
            d2 = dn2 * vec[1:2, :]
            back = scale * (d2 - unit * jnp.mean(d2 * unit, axis=-1, keepdims=True))
            back = act_b[rs, :].astype(F32) + back
            dnv[rs, :] = back
            act_b[rs, :] = back.astype(BF16)

        out = local(tr.at[:, pl.ds(0, width)], y_out, sem_in.at[1])
        out.start()
        remote(act_b.at[mine], act_b.at[mine], sem_pair.at[2], sem_pair.at[3], at(c=1 - c)).start()
        local(tok_in, act_a.at[mine], sem_in.at[0]).wait()
        local(spill_t, act_a.at[other], sem_spill.at[6]).wait()
        out.wait()

        @pl.loop(0, 2 * tiles)
        def _(t):
            rs = span_of(t * TILE, TILE, TILE)
            tr[:, rs] = normed(act_a[rs, :].astype(F32)).T

        landed(act_b.at[mine], sem_pair.at[2])
        landed(act_b.at[other], sem_pair.at[3])

        for cc in range(2):

            @pl.loop(0, seqs)
            def _(s):
                hf[span_of(s * EDGE, EDGE, EDGE), :] = act_b[span_of(cc * rows + s * span, EDGE, span), :].astype(F32)

            head = dot_nt(hf[...].astype(BF16), wout[...]).reshape(seqs, EDGE, chan)
            ks[cc * seqs : (cc + 1) * seqs] = head * chd[cc * seqs : (cc + 1) * seqs]

        @pl.when(me > 0)
        def _():
            remote(ks, kh, sem_kh.at[0], sem_kh.at[1], member(lax.rem(me + n - 1, n))).start()

        @pl.when(me == n - 1)
        def _():
            kh[...] = jnp.zeros_like(kh)

        for h in range(nx):
            side = pl.ds(h * lanes, lanes)
            gd[steps % slots, h] = dot_tn(zv[:, :CHUNK], act_b[:, side]).astype(BF16)
            og[h] = dot_tn(zv[:, CHUNK:], act_b[:, side]).astype(BF16)

        @pl.when(me < n - 1)
        def _():
            landed(kh, sem_kh.at[1])

        @pl.loop(0, 2 * tiles)
        def _(t):
            rs = span_of(t * TILE, TILE, TILE)
            first = t * tseq
            for i in range(3):
                loaded(t, i).wait()

            @pl.when(t + 1 < 2 * tiles)
            def _():
                for i in range(3):
                    loaded(t + 1, i).start()

            for h in range(2):
                hl = pl.ds(h * CHUNK, CHUNK)
                dz = dot_nt(act_b[rs, :], wout[hl, :]).reshape(tseq, span, CHUNK)
                b_gate, c_gate, x_value = (
                    dnv[
                        span_of((1 - c) * rows + i * TILE, TILE, TILE),
                        span_of((t % 2) * chan + h * CHUNK, CHUNK, CHUNK),
                    ].reshape(tseq, span, CHUNK)
                    for i in range(3)
                )
                *lags, conv = convolve((b_gate * x_value).reshape(TILE, CHUNK), first, h)
                dk = dz * c_gate
                for k in range(3):
                    conv_acc[k : k + 1, hl] += jnp.sum((dk * lags[k]).reshape(TILE, CHUNK), axis=0, keepdims=True)
                vb[:, :span, :] = dk
                vb[:, span:, :] = kh[pl.ds(first, tseq), :, hl]
                du = tap(2, h) * dk + tap(1, h) * vb[:, 1 : 1 + span, :] + tap(0, h) * vb[:, 2 : 2 + span, :]
                act_a[rs, hl] = (du * x_value).astype(BF16).reshape(TILE, CHUNK)
                act_a[rs, pl.ds(chan + h * CHUNK, CHUNK)] = (dz * conv).astype(BF16).reshape(TILE, CHUNK)
                zv[rs, hl] = (du * b_gate).astype(BF16).reshape(TILE, CHUNK)

    def share_back():
        @pl.loop(0, 2 * tiles)
        def _(t):
            rs = span_of(tile_start(t), TILE, TILE)
            total = dot_nt(act_a[rs, :CHUNK], win(0))
            for b in range(1, 6):
                src = act_a[rs, b * CHUNK : (b + 1) * CHUNK] if b < 4 else zv[rs, (b - 4) * CHUNK : (b - 3) * CHUNK]
                total += dot_nt(src, win(b))

            @pl.when(t < tiles)
            def _():
                act_b[rs, :] = total.astype(BF16)

            @pl.when(t >= tiles)
            def _():
                outv[rs, :] = total

            @pl.when(t == tiles - 1)
            def _():
                remote(act_b.at[other], take.at[0], sem_pair.at[4], sem_pair.at[5], at(c=1 - c)).start()
                local(tok_in, act_b.at[mine], sem_in.at[0]).start()

    def finish_back():
        landed(take.at[0], sem_pair.at[5])
        local(tok_in, act_b.at[mine], sem_in.at[0]).wait()

        @pl.loop(0, tiles)
        def _(t):
            rl = span_of(t * TILE, TILE, TILE)
            rs = span_of(c * rows + t * TILE, TILE, TILE)
            tokens = act_b[rs, :].astype(F32)
            scale = row_scale(tokens)
            unit = tokens * scale
            dn1 = outv[rs, :] + take[0, rl, :].astype(F32)
            sg[0:1, :] += jnp.sum(dn1 * unit, axis=0, keepdims=True)
            d1 = dn1 * vec[0:1, :]
            back = dnv[rs, :] + scale * (d1 - unit * jnp.mean(d1 * unit, axis=-1, keepdims=True))
            take[1, rl, :] = (back * live_in[rl, :]).astype(BF16)

        local(take.at[1], dx_out, sem_in.at[1]).start()
        sg[2:5, span_of(c * chan, chan, chan)] = conv_acc[0:3, :]
        sum_reps()

    @pl.loop(0, chunks + 3)
    def _(m):
        @pl.when(m < steps)
        def _():
            compute(m)

        @pl.when(m == steps - 1)
        def _():
            give_sums()

        @pl.when(m == steps)
        def _():
            mixer_back()

        @pl.when(jnp.logical_and(m >= steps, m < chunks - 1))
        def _():
            b = (m - steps) * 2 * CHUNK
            weight_grads(
                m % slots, act_a[:, span_of(b, CHUNK, CHUNK)], act_a[:, span_of(b + CHUNK, CHUNK, CHUNK)]
            )

        @pl.when(m == steps + 1)
        def _():
            gd[(steps + 1) % slots] = og[...]

        @pl.when(m == chunks - 1)
        def _():
            weight_grads(m % slots, zv[:, :CHUNK], zv[:, CHUNK:])

        @pl.when(jnp.logical_and(m >= 1, m < chunks + 1))
        def _():
            sum_x(m - 1)

        @pl.when(m < chunks)
        def _():
            send_x(m)

        two(m - 1, fetch_y)
        two(m - 2, fetch_z)
        pass_on_far(m + RELAY)
        two(m, send_y)
        two(m - 1, send_z)
        two(m - 2, finish)

        @pl.when(m == steps + 1)
        def _():
            share_back()

        @pl.when(m == chunks - 1)
        def _():
            finish_back()

        @pl.when(m == chunks)
        def _():
            sum_group()

        @pl.when(m == chunks + 1)
        def _():
            sum_last()

        @pl.when(m + 1 < steps)
        def _():
            loaded_weights()

    landed(take.at[1], sem_in.at[1])
    landed(smallv.at[0], sem_in.at[0])

    @pl.loop(0, chunks)
    def _(m):
        landed(hyg.at[m], sy_g.at[m])
        landed(hzg.at[m], sz_g.at[m])

        @pl.when(m < chunks - 1)
        def _():
            for q in range(pieces):
                zo, yo, _ = grad_owner(m, q)
                part = pl.ds(q * gp, gp)

                @pl.when(yo != y)
                def _():
                    landed(h1d.at[m, part], sy_d.at[m, q])

                @pl.when(jnp.logical_and(yo == y, zo != z))
                def _():
                    landed(h2d.at[m, part], sz_d.at[m, q])

    for p in range(len(reps)):
        landed(gu_full.at[0, 0], fs_g.at[p])
        landed(in_full.at[0, 0], fs_i.at[p])

        @pl.when(in_half)
        def _():
            landed(down_full.at[0], fs_d.at[p])
            landed(out_full.at[0], fs_o.at[p])
    landed(take.at[0], sem_pair.at[4])

    @pl.when(me > 0)
    def _():
        landed(ks, sem_kh.at[0])

    for p, (ax, d) in enumerate(ag_peers):
        direct = ax == 1 or off(zp(d)) < (nz - 1) ** 2

        @pl.when(direct)
        def _():
            landed(all_in.at[:, 0, 0], mg_send.at[p])
            landed(all_gu.at[:, :, 0, 0], ag_send.at[p])

        @pl.when(jnp.logical_and(direct, in_half))
        def _():
            landed(all_out.at[0], mg_osend.at[p])
            landed(all_down.at[:, pl.ds(0, gp)], ag_dsend.at[p])

    @pl.when(inner)
    def _():
        landed(all_in.at[:, 0, 0], ag_far.at[0])
        landed(all_gu.at[:, :, 0, 0], ag_far.at[2])

    @pl.when(z == jnp.where(c == 0, 2, 1))
    def _():
        landed(all_out.at[0], ag_far.at[1])
        landed(all_down.at[:, pl.ds(0, gp)], ag_far.at[3])

    for d in range(1, nz):
        for e in range(1, ny):
            landed(all_in.at[:, 0, 0], mg_relay.at[d - 1, e - 1])
            landed(all_gu.at[:, :, 0, 0], ag_relay.at[d - 1, e - 1])
    for o in range(n // 2):
        zo, yo = out_owner(o)

        @pl.when(jnp.logical_and(zo != z, yo == y))
        def _():
            for e in range(1, ny):
                landed(all_out.at[0], mg_orelay.at[o, e - 1])

    for k in range(2):
        zo = (n // 2 * c) // ny + k

        @pl.when(zo != z)
        def _():
            for e in range(1, ny):
                landed(all_down.at[:, pl.ds(0, gp)], ag_drelay.at[zo % 2, e - 1])

    for p, (d, e) in enumerate(reps):
        landed(gu_full.at[0, 0], fr_g.at[p])
        landed(in_full.at[0, 0], fr_i.at[p])

        @pl.when(in_half if e == 0 else jnp.logical_not(in_half))
        def _():
            landed(down_full.at[0], fr_d.at[p])
            landed(out_full.at[0], fr_o.at[p])


def block_call(sizes, *operands):
    nx, nz, ny, seqs, span, width, hidden = sizes
    n = nz * ny
    rows = seqs * span
    dn = width // n
    dnx = dn // nx
    half = hidden // 2
    chan = width // 2
    steps = half // CHUNK
    own_rows = hidden // n
    gp = min(BLOCK, own_rows & -own_rows)
    pieces = CHUNK // gp
    lanes = width // nx
    chunks = steps + 3
    tseq = TILE // span
    reps = 2 * nx - 1
    hops = nz + ny - 2
    dma = lambda *dims: pltpu.SemaphoreType.DMA(dims)
    bf = lambda *dims: pltpu.VMEM(dims, BF16)
    fl = lambda *dims: pltpu.VMEM(dims, F32)
    anywhere = pl.BlockSpec(memory_space=pl.ANY)
    shape = jax.ShapeDtypeStruct
    specs = [anywhere] * 10
    specs[3] = pl.BlockSpec(memory_space=pltpu.VMEM)
    return pl.pallas_call(
        functools.partial(block_kernel, sizes),
        out_shape=[
            shape((rows, width), BF16),
            shape((rows, width), BF16),
            shape((nx, 2, 2, dnx, half), BF16),
            shape((nx, own_rows, lanes), BF16),
            shape((nx, 2, 6, dnx, CHUNK), BF16),
            shape((nx, dn, lanes), BF16),
            shape((8, dn), F32),
            shape((steps, 2, nz, ny, dn, CHUNK), BF16),
            shape((steps, CHUNK, width), BF16),
            shape((6, nz, ny, dn, CHUNK), BF16),
            shape((n // 2, dn, width), BF16),
            shape((3, 2 * rows, chan), F32),
            shape((rows, width), F32),
            shape((rows, width), BF16),
            shape((chunks, ny, 2, nz, dnx, CHUNK), BF16),
            shape((chunks, CHUNK, lanes), BF16),
            shape((chunks, ny - 1, 2, nz, dnx, CHUNK), BF16),
            shape((chunks, ny - 1, CHUNK, lanes), BF16),
            shape((chunks, 2, nz, dnx, CHUNK), BF16),
            shape((chunks, CHUNK, lanes), BF16),
            shape((chunks, nz - 1, 2, dnx, CHUNK), BF16),
            shape((chunks, nz - 1, CHUNK, lanes), BF16),
        ],
        in_specs=specs,
        out_specs=[anywhere] * 22,
        scratch_shapes=[
            bf(2 * rows, width),
            bf(2 * rows, width),
            bf(width, 2 * rows),
            bf(2, nz, ny, dn, CHUNK),
            bf(CHUNK, width),
            fl(2 * rows, width),
            fl(2 * rows, width),
            bf(6, nz, ny, dn, CHUNK),
            bf(chan, width),
            bf(2 * rows, chan),
            bf(2, rows, width),
            bf(nx, CHUNK, lanes),
            fl(tseq, span + EDGE, CHUNK),
            fl(tseq, span + EDGE, CHUNK),
            bf(2, seqs, EDGE, width),
            fl(2 * seqs, EDGE, chan),
            fl(2 * seqs, EDGE, chan),
            fl(2 * seqs, EDGE, chan),
            fl(2 * seqs, EDGE, chan),
            fl(seqs * EDGE, width),
            fl(n, 8, dn),
            fl(8, width),
            fl(8, chan),
            fl(8, width),
            fl(2 * nx, 8, width),
            fl(n, 8, dn),
            fl(n, 8, dn),
            bf(2, 2, nx, nz, ny, dnx, CHUNK),
            bf(2, nx, CHUNK, lanes),
            bf(2, nx - 1, 2, nz, ny, dnx, CHUNK),
            bf(2, nx - 1, CHUNK, lanes),
            bf(ny, 2, nz, dnx, CHUNK),
            bf(CHUNK, lanes),
            bf(2, 2, nz, dnx, CHUNK),
            bf(2, CHUNK, lanes),
            bf(2, ny - 1, 2, nz, dnx, CHUNK),
            bf(2, ny - 1, CHUNK, lanes),
            bf(2, 2, dnx, CHUNK),
            bf(2, CHUNK, lanes),
            bf(2, nz - 1, 2, dnx, CHUNK),
            bf(2, nz - 1, CHUNK, lanes),
            bf(2, dnx, CHUNK),
            bf(gp, lanes),
            dma(2),
            dma(2 + n // 2),
            dma(2, steps * pieces),
            dma(12),
            dma(3),
            dma(4),
            dma(2),
            dma(8),
            dma(4),
            dma(steps, nz - 1),
            dma(steps, ny - 1),
            dma(steps, pieces),
            dma(steps, pieces),
            dma(hops),
            dma(nz - 1, ny - 1),
            dma(hops),
            dma(2, ny - 1),
            dma(2),
            dma(6, nz - 1),
            dma(6, ny - 1),
            dma(n // 2),
            dma(n // 2),
            dma(hops),
            dma(nz - 1, ny - 1),
            dma(hops),
            dma(n // 2, ny - 1),
            dma(2, nx - 1),
            dma(2, nx - 1),
            dma(2, nx - 1),
            dma(2, nx - 1),
            dma(2),
            dma(chunks),
            dma(chunks, pieces),
            dma(chunks),
            dma(chunks, pieces),
            dma(2, 4),
            dma(2),
            dma(chunks),
            dma(chunks, pieces),
            dma(chunks),
            dma(chunks, pieces),
            dma(2, 4),
            dma(2),
            dma(reps),
            dma(reps),
            dma(reps),
            dma(reps),
            dma(reps),
            dma(reps),
            dma(reps),
            dma(reps),
            dma(6),
        ],
        compiler_params=pltpu.CompilerParams(
            collective_id=0, has_side_effects=True, vmem_limit_bytes=63 << 20
        ),
        name="gated_block",
    )(*operands)[:7]


def live_mask(lengths, deal, span):
    slots = jnp.arange(deal.shape[1], dtype=jnp.int32)
    picked = deal[0][:, None] == slots[None, :]
    source_len = jnp.sum(jnp.where(picked, lengths[0][:, None], 0), axis=0)
    position = lax.axis_index(GROUP) * span + jnp.arange(span, dtype=jnp.int32)
    return (position[None, :] < source_len[:, None]).astype(F32).reshape(-1, 1)


def body(
    tokens,
    cotangent,
    lengths,
    deal,
    norm_gain,
    in_weight,
    conv_weight,
    out_weight,
    ffn_gain,
    gate_weight,
    up_weight,
    down_weight,
):
    seqs, span, width = tokens.shape
    hidden = gate_weight.shape[1]
    nx, nz, ny = (lax.axis_size(axis) for axis in ("x", "z", "y"))
    dn = width // (nz * ny)
    small = jnp.stack([norm_gain, ffn_gain, *(conv_weight[:, k] for k in range(3))]).astype(F32)
    small = jnp.pad(small, ((0, 3), (0, 0)))
    block_out, block_grad, gu, down, mixer_in, mixer_out, sums = block_call(
        (nx, nz, ny, seqs, span, width, hidden),
        tokens.reshape(-1, width),
        tokens,
        cotangent.reshape(-1, width),
        live_mask(lengths, deal, span),
        small,
        in_weight,
        out_weight,
        gate_weight,
        up_weight,
        down_weight,
    )
    gate_grad = gu[:, :, 0].transpose(0, 2, 1, 3).reshape(dn, hidden).astype(F32)
    up_grad = gu[:, :, 1].transpose(0, 2, 1, 3).reshape(dn, hidden).astype(F32)
    mixer_in = mixer_in.reshape(nx, 2, 3, 2, dn // nx, CHUNK)
    in_grad = mixer_in.transpose(0, 4, 2, 1, 3, 5).reshape(dn, 3 * width).astype(F32)
    out_grad = mixer_out.transpose(1, 0, 2).reshape(dn, width).astype(F32)
    down_grad = down.transpose(1, 0, 2).reshape(-1, width).astype(F32)
    return (
        block_out.reshape(tokens.shape),
        block_grad.reshape(tokens.shape),
        sums[0],
        in_grad,
        sums[2:5].T,
        out_grad,
        sums[1],
        gate_grad,
        up_grad,
        down_grad,
    )


def solution(mesh):
    rep, fsdp = mesh.shape["rep"], mesh.shape["fsdp"]
    grid = (rep // 2, 2, 4, fsdp // 4)
    split = Mesh(mesh.devices.reshape(grid), ("x", "core", "z", "y"))
    copies = ("x", "core")
    rows = P(copies, GROUP, None)
    lists = P(copies, None)
    vector = P(GROUP)
    matrix = P(GROUP, None)
    return jax.shard_map(
        body,
        mesh=split,
        in_specs=(
            rows,
            rows,
            lists,
            lists,
            vector,
            matrix,
            matrix,
            matrix,
            vector,
            matrix,
            matrix,
            matrix,
        ),
        out_specs=(rows, rows, vector, matrix, matrix, matrix, vector, matrix, matrix, matrix),
        check_vma=False,
    )
```

```python
import functools
import jax
import jax.numpy as jnp
from jax import lax
from jax.experimental import pallas as pl
from jax.experimental.pallas import tpu as pltpu
from jax.sharding import Mesh, PartitionSpec as P

EPS = 1e-05
F32 = jnp.float32
BF16 = jnp.bfloat16
NT = (((1,), (1,)), ((), ()))
TN = (((0,), (0,)), ((), ()))
MESH = pl.DeviceIdType.MESH
GROUP = ("z", "y")
CHUNK = 256
BLOCK = 128
TILE = 256
EDGE = 8
AHEAD = 4
RELAY = 2
HOLD = 5
SHARED = 2


def dot(left, right):
    return jnp.dot(left, right, preferred_element_type=F32)


def dot_nt(left, right):
    return lax.dot_general(left, right, NT, preferred_element_type=F32)


def dot_tn(left, right):
    return lax.dot_general(left, right, TN, preferred_element_type=F32)


def row_scale(values):
    return lax.rsqrt(jnp.mean(values * values, axis=-1, keepdims=True) + EPS)


def block_kernel(
    sizes,
    tok_in, edge_in, cot_in, live_in, small_in, in_in, out_in, gate_in, up_in, down_in,
    y_out, dx_out, gu_full, down_full, in_full, out_full, small_out,
    all_gu, all_down, all_in, all_out, spill_p, spill_h, spill_t,
    h0g, h0d, h1g, h1d, hyg, hyd, h2g, h2d, hzg, hzd,
    act_a, act_b, tr, wgu, wd, outv, dnv, acts, wout, zv, take,
    ub, vb, hal, uh, kh, ks, chd, hf, smallv, vec, conv_acc, sg, sg_all, sg_mine, sg_parts,
    ggu, gd, vag, vad, s1g, s1d, og, y1g, y1d, yrg, yrd, z2g, z2d, zrg, zrd, fing, find,
    sem_in, sem_load, sem_own, sem_pair, sem_half, sem_n2, sem_sums, sem_dm, sem_small, sem_edge, sem_kh, sem_spill,
    ag_cross, ag_x, mg_cross, mg_x, ag_far, ag_z, ag_y, ag_dz, ag_dy, ag_send, ag_relay, ag_dsend, ag_drelay,
    mg_own, mg_z, mg_y, mg_oz, mg_oy, mg_send, mg_relay, mg_osend, mg_orelay,
    ra_g, ra_d, sa_g, sa_d, ld0, st1, ry_g, ry_d, sy_g, sy_d, ld1, st2, rz_g, rz_d, sz_g, sz_d, ld2, st3,
    fs_g, fs_i, fs_d, fs_o, fr_g, fr_i, fr_d, fr_o, sem_sum,
):
    nx, nz, ny, seqs, span, width, hidden = sizes
    n = nz * ny
    rows = seqs * span
    dn = width // n
    dnx = dn // nx
    half = hidden // 2
    chan = width // 2
    steps = half // CHUNK
    chunks = steps + 3
    per_half = half // BLOCK // 2
    own_rows = hidden // n
    gp = min(BLOCK, own_rows & -own_rows)
    pieces = CHUNK // gp
    lanes = width // nx
    slots = 3
    tiles = rows // TILE
    tseq = TILE // span
    x, c = lax.axis_index("x"), lax.axis_index("core")
    z, y = lax.axis_index("z"), lax.axis_index("y")
    me = z * ny + y
    in_half = me // (n // 2) == c

    def at(x=x, c=c, z=z, y=y):
        return (x, c, z, y)

    def member(j, c=c):
        return at(c=c, z=j // ny, y=j % ny)

    def zp(d):
        return lax.rem(z + d, nz)

    def yp(d):
        return lax.rem(y + d, ny)

    def xp(d):
        return lax.rem(x + d, nx)

    def remote(src, dst, ssem, rsem, dev):
        return pltpu.make_async_remote_copy(
            src_ref=src, dst_ref=dst, send_sem=ssem, recv_sem=rsem, device_id=dev, device_id_type=MESH
        )

    def local(src, dst, sem):
        return pltpu.make_async_copy(src, dst, sem)

    def landed(ref, sem):
        pltpu.make_async_copy(ref, ref, sem).wait()

    def span_of(start, size, align):
        return pl.ds(pl.multiple_of(start, align), size)

    mine = span_of(c * rows, rows, rows)
    other = span_of((1 - c) * rows, rows, rows)

    barrier = pltpu.get_barrier_semaphore()
    peers = [member(lax.rem(me + d, n)) for d in range(1, n)]
    reps = [(d, e) for d in range(nx) for e in range(2) if d + e > 0]
    peers += [at(x=xp(d), c=lax.rem(c + e, 2)) for d, e in reps]
    peers += [member(lax.rem(me + d, n), c=1 - c) for d in (1, n - 1)]
    for dev in peers:
        pl.semaphore_signal(barrier, inc=1, device_id=dev, device_id_type=MESH)
    pl.semaphore_wait(barrier, len(peers))

    local(small_in, smallv.at[me], sem_small.at[0]).start()
    for d in range(1, n):
        remote(small_in, smallv.at[me], sem_small.at[1], sem_small.at[2], member(lax.rem(me + d, n))).start()

    @pl.when(me < n - 1)
    def _():
        for e in range(2):
            dev = member(lax.rem(me + 1, n), c=lax.rem(c + e, 2))
            remote(edge_in, hal.at[c], sem_edge.at[e], sem_edge.at[2 + c], dev).start()

    local(tok_in, act_a.at[mine], sem_in.at[0]).start()
    local(cot_in, take.at[1], sem_in.at[1]).start()
    remote(tok_in, act_a.at[mine], sem_pair.at[0], sem_pair.at[1], at(c=1 - c)).start()

    ag_peers = [(0, d) for d in range(1, nz)] + [(1, d) for d in range(1, ny)]

    def toward(ax, d):
        return at(z=zp(d)) if ax == 0 else at(y=yp(d))

    def mixer_first_hop(b):
        here = in_in.at[:, span_of((b // 2) * width + c * chan + (b % 2) * CHUNK, CHUNK, CHUNK)]
        there = all_in.at[b, z, y]
        local(here, there, mg_own.at[0]).start()
        hops(here, there, mg_send, lambda d: mg_z.at[b, d - 1], lambda d: mg_y.at[b, d - 1], b % 2)

    def out_first_hop():
        @pl.when(in_half)
        def _():
            o = me - c * (n // 2)
            local(out_in, all_out.at[o], mg_own.at[1]).start()
            hops(out_in, all_out.at[o], mg_osend, lambda d: mg_oz.at[o], lambda d: mg_oy.at[o])

    def off(zs):
        return (zs - z) * (zs - z)

    inner = jnp.logical_and(z > 0, z < nz - 1)
    end = jnp.where(z == 1, 0, nz - 1)
    end_slot = jnp.where(z == 1, 0, nz - 2)

    plane = x % 2
    partner = x + 1 - 2 * plane

    def hops(here, there, send, recv_z, recv_y, only=None):
        for p, (ax, d) in enumerate(ag_peers):
            if ax == 1:

                @pl.when(True if only is None else plane == only)
                def _():
                    remote(here, there, send.at[p], recv_y(d), toward(ax, d)).start()
            elif d in (1, nz - 1):

                @pl.when(off(zp(d)) < (nz - 1) ** 2)
                def _():
                    remote(here, there, send.at[p], recv_z(d), toward(ax, d)).start()
            else:
                remote(here, there, send.at[p], recv_z(d), toward(ax, d)).start()

    def out_owner(o):
        j = c * (n // 2) + o
        return j // ny, j % ny

    def along_y(block, send, recv):
        for e in range(1, ny):
            remote(block, block, send.at[e - 1], recv(e), at(y=yp(e))).start()

    def along(block, part, wanted, d, near, arrived, far_send, far_recv, y_send, y_recv):
        if d in (1, nz - 1):
            this = off(lax.rem(z - d + nz, nz)) == (nz - 1) ** 2

            @pl.when(jnp.logical_not(this) if near else this)
            def _():
                landed(block, arrived)

                @pl.when(wanted)
                def _():
                    along_y(part, y_send, y_recv)
        elif near:
            landed(block, arrived)

            @pl.when(inner)
            def _():
                remote(block, block, far_send, far_recv, at(z=end)).start()

            @pl.when(wanted)
            def _():
                along_y(part, y_send, y_recv)

    def mixer_cross(b):
        @pl.when(plane == b % 2)
        def _():
            for e in range(1, ny):
                block = all_in.at[b, :, lax.rem(y - e + ny, ny)]
                landed(block, mg_y.at[b, e - 1])
                remote(block, block, mg_cross.at[e - 1], mg_x.at[b, e - 1], at(x=partner)).start()

    def mixer_hop(b, near):
        for d in range(1, nz):
            block = all_in.at[b, lax.rem(z - d + nz, nz), y]
            along(
                block, block, plane == b % 2, d, near, mg_z.at[b, d - 1], ag_far.at[0], mg_z.at[b, end_slot], mg_relay.at[d - 1], lambda e: mg_y.at[b, e - 1]
            )

    def owned(block, zo, near, arrived, far_send, y_send, y_recv):
        @pl.when(off(zo) < (nz - 1) ** 2 if near else off(zo) == (nz - 1) ** 2)
        def _():
            landed(block, arrived)

            @pl.when(jnp.logical_and(inner, off(zo) == 4))
            def _():
                remote(block, block, far_send, arrived, at(z=end)).start()

            along_y(block, y_send, y_recv)

    def out_hop(near):
        for o in range(n // 2):
            zo, yo = out_owner(o)

            @pl.when(jnp.logical_and(zo != z, yo == y))
            def _():
                owned(all_out.at[o], zo, near, mg_oz.at[o], ag_far.at[1], mg_orelay.at[o], lambda e: mg_oy.at[o])

    def mixer_arrived():
        for e in range(1, ny):
            for b in range(6):

                @pl.when(plane != b % 2)
                def _():
                    landed(all_in.at[b, :, lax.rem(y - e + ny, ny)], mg_x.at[b, e - 1])
        for o in range(n // 2):
            _, yo = out_owner(o)

            @pl.when(yo != y)
            def _():
                landed(all_out.at[o], mg_oy.at[o])

        landed(all_in.at[:, 0, 0], mg_own.at[0])

        @pl.when(in_half)
        def _():
            landed(all_out.at[0], mg_own.at[1])

    def mixer_load():
        copies = [local(all_in, acts, sem_load.at[0])]
        copies += [local(all_out.at[o], wout.at[pl.ds(o * dn, dn)], sem_load.at[2 + o]) for o in range(n // 2)]
        for copy in copies:
            copy.start()
        for copy in copies:
            copy.wait()

    def blocks(m):
        h, i = m % 2, m // 2
        first = per_half * h + i
        return first, per_half * h + per_half - 1 - i + per_half * (m // (2 * (per_half // 2)))

    def column(b):
        return pl.multiple_of(c * half + b * BLOCK, BLOCK)

    def owner(m, q):
        b = blocks(m)[q * gp // BLOCK]
        row = c * half + b * BLOCK + (q * gp) % BLOCK
        j = row // own_rows
        return j // ny, j % ny, pl.multiple_of(row - j * own_rows, gp)

    def grad_owner(m, q):
        zo, yo, row = owner(jnp.minimum(m, steps - 1), q)
        mixed = c * chan + jnp.maximum(m - steps, 0) * CHUNK + q * gp
        j = mixed // dn
        late = m >= steps
        return (
            jnp.where(late, j // ny, zo),
            jnp.where(late, j % ny, yo),
            pl.multiple_of(jnp.where(late, mixed - j * dn, row), gp),
        )

    def first_hop(m, shared=False):
        b = blocks(m)
        for k in range(2):
            for w, src in enumerate((gate_in, up_in)):
                here = src.at[:, pl.ds(column(b[k]), BLOCK)]
                there = all_gu.at[m, w, z, y, :, pl.ds(k * BLOCK, BLOCK)]
                local(here, there, sem_own.at[0, m]).start()
                hops(here, there, ag_send, lambda d: ag_z.at[m, d - 1], lambda d: ag_y.at[m, d - 1], k if shared else None)
        for q in range(pieces):
            zo, yo, row = owner(m, q)

            @pl.when(jnp.logical_and(zo == z, yo == y))
            def _():
                here = down_in.at[pl.ds(row, gp)]
                there = all_down.at[m, pl.ds(q * gp, gp)]
                local(here, there, sem_own.at[1, m * pieces + q]).start()
                hops(here, there, ag_dsend, lambda d: ag_dz.at[m, q], lambda d: ag_dy.at[m, q])

    def half_of(m, ys, side):
        return all_gu.at[m, :, :, ys, :, span_of(side * BLOCK, BLOCK, BLOCK)]

    def cross(m):
        for e in range(1, ny):
            block = half_of(m, lax.rem(y - e + ny, ny), plane)
            landed(block, ag_y.at[m, e - 1])
            remote(block, block, ag_cross.at[e - 1], ag_x.at[m, e - 1], at(x=partner)).start()

    def next_hop(m, near, shared=False):
        for d in range(1, nz):
            zs = lax.rem(z - d + nz, nz)
            block = all_gu.at[m, :, zs, y]
            part = all_gu.at[m, :, zs, y, :, span_of(plane * BLOCK, BLOCK, BLOCK)] if shared else block
            along(
                block, part, True, d, near, ag_z.at[m, d - 1], ag_far.at[2], ag_z.at[m, end_slot], ag_relay.at[d - 1], lambda e: ag_y.at[m, e - 1]
            )
        for q in range(pieces):
            zo, yo, _ = owner(m, q)

            @pl.when(jnp.logical_and(zo != z, yo == y))
            def _():
                block = all_down.at[m, pl.ds(q * gp, gp)]
                owned(block, zo, near, ag_dz.at[m, q], ag_far.at[3], ag_drelay.at[zo % 2], lambda e: ag_dy.at[m, q])

    def arrived_shared(m):
        for e in range(1, ny):
            landed(half_of(m, lax.rem(y - e + ny, ny), 1 - plane), ag_x.at[m, e - 1])

    def arrived(m):
        for e in range(1, ny):
            landed(all_gu.at[m, :, :, lax.rem(y - e + ny, ny)], ag_y.at[m, e - 1])

    def load(m):
        landed(all_gu.at[m, :, 0, 0], sem_own.at[0, m])
        for q in range(pieces):
            zo, yo, _ = owner(m, q)
            block = all_down.at[m, pl.ds(q * gp, gp)]

            @pl.when(jnp.logical_and(zo == z, yo == y))
            def _():
                landed(block, sem_own.at[1, m * pieces + q])

            @pl.when(yo != y)
            def _():
                landed(block, ag_dy.at[m, q])

        local(all_gu.at[m], wgu, sem_load.at[0]).start()
        local(all_down.at[m], wd, sem_load.at[1]).start()

    def loaded_weights():
        landed(wgu, sem_load.at[0])
        landed(wd, sem_load.at[1])

    def pass_on(m):
        @pl.when(m < steps)
        def _():
            next_hop(m, True)

    def pass_on_far(m):
        @pl.when(m < steps)
        def _():
            next_hop(m, False)

        @pl.when(m + AHEAD - RELAY < steps)
        def _():
            first_hop(m + AHEAD - RELAY)

    for b in range(3):
        mixer_first_hop(b)

    local(cot_in, take.at[1], sem_in.at[1]).wait()

    @pl.loop(0, tiles)
    def _(t):
        rl = span_of(t * TILE, TILE, TILE)
        rs = span_of(c * rows + t * TILE, TILE, TILE)
        act_b[rs, :] = (take[1, rl, :].astype(F32) * live_in[rl, :]).astype(BF16)

    remote(act_b.at[mine], act_b.at[mine], sem_pair.at[2], sem_pair.at[3], at(c=1 - c)).start()

    landed(small_in, sem_small.at[0])
    landed(smallv.at[pl.ds(0, n - 1)], sem_small.at[1])
    landed(smallv.at[pl.ds(0, n - 1)], sem_small.at[2])
    for j in range(n):
        vec[:, j * dn : (j + 1) * dn] = smallv[j]

    @pl.when(me < n - 1)
    def _():
        for e in range(2):
            landed(hal.at[0], sem_edge.at[e])

    @pl.when(me > 0)
    def _():
        for e in range(2):
            landed(hal.at[e], sem_edge.at[2 + e])

    @pl.when(me == 0)
    def _():
        hal[...] = jnp.zeros_like(hal)

    for b in range(8):
        if b < 6:
            mixer_hop(b, True)
        if 0 < b < 7:
            mixer_hop(b - 1, False)
        if b < 3:
            mixer_first_hop(b + 3)
        elif b == 3:
            out_first_hop()
        elif b > 5:
            out_hop(b == 6)
            first_hop(b - 6, True)
        if b > 1:
            mixer_cross(b - 2)
    local(tok_in, act_a.at[mine], sem_in.at[0]).wait()
    landed(act_a.at[mine], sem_pair.at[0])
    landed(act_a.at[other], sem_pair.at[1])
    local(act_a.at[other], spill_t, sem_spill.at[6]).start()
    mixer_arrived()
    mixer_load()

    def win(b):
        return acts[b].reshape(width, CHUNK)

    def tap(k, h):
        return vec[2 + k : 3 + k, span_of(c * chan + h * CHUNK, CHUNK, CHUNK)].reshape(1, 1, CHUNK)

    def normed(tokens):
        return (tokens * row_scale(tokens) * vec[0:1, :]).astype(BF16)

    for cc in range(2):
        for k in range(2):
            edge = normed(hal[cc, k].astype(F32))
            for h in range(2):
                hl = slice(h * CHUNK, (h + 1) * CHUNK)
                uh[k, cc * seqs : (cc + 1) * seqs, hl] = dot(edge, win(h)) * dot(edge, win(4 + h))

    def convolve(product, first, h):
        for i in range(tseq):
            for k in range(2):
                row = EDGE - 2 + k
                ub[i, row : row + 1, :] = uh[k, pl.ds(first + i, 1), h * CHUNK : (h + 1) * CHUNK]
        ub[:, EDGE:, :] = product.reshape(tseq, span, CHUNK)
        lag_two = ub[:, EDGE - 2 : EDGE - 2 + span, :]
        lag_one = ub[:, EDGE - 1 : EDGE - 1 + span, :]
        lag_none = ub[:, EDGE:, :]
        return lag_two, lag_one, lag_none, tap(0, h) * lag_two + tap(1, h) * lag_one + tap(2, h) * lag_none

    def spilled(t, i, rs):
        slot = t % 2
        src = dnv.at[span_of(slot * 3 * TILE + i * TILE, TILE, TILE), pl.ds(0, chan)]
        return local(src, spill_p.at[i, rs], sem_spill.at[slot * 3 + i])

    def tile_start(t):
        return lax.rem(t + (1 - c) * tiles, 2 * tiles) * TILE

    @pl.loop(0, 2 * tiles)
    def _(t):
        start = tile_start(t)
        rs = span_of(start, TILE, TILE)
        first = start // span
        tokens = act_a[rs, :].astype(F32)
        n1 = normed(tokens)

        @pl.when(t >= 2)
        def _():
            for i in range(3):
                spilled(t, i, rs).wait()

        for h in range(2):
            parts = [dot(n1, win(2 * i + h)) for i in range(3)]
            hl = pl.ds(h * CHUNK, CHUNK)
            for i in range(3):
                dnv[span_of((t % 2) * 3 * TILE + i * TILE, TILE, TILE), hl] = parts[i]
            for i in range(tseq):
                for k in range(2):
                    chd[k, pl.ds(first + i, 1), hl] = parts[1][i * span + k : i * span + k + 1, :]
            conv = convolve(parts[0] * parts[2], first, h)[3].reshape(TILE, CHUNK)
            zv[rs, hl] = (parts[1] * conv).astype(BF16)
        for i in range(3):
            spilled(t, i, rs).start()
        mixed = dot(zv[rs, :], wout[...])

        i = lax.rem(t, tiles)
        half_rows = span_of(i * TILE, TILE, TILE)

        @pl.when(t == 0)
        def _():
            landed(act_a.at[other], sem_spill.at[6])

        @pl.when(t < tiles)
        def _():
            tr[half_rows, other] = mixed.astype(BF16)
            remote(
                tr.at[half_rows, other], take.at[0, half_rows], sem_half.at[0, i], sem_half.at[1, i], at(c=1 - c)
            ).start()
            outv[rs, :] = jnp.zeros((TILE, width), F32)

        @pl.when(t >= tiles)
        def _():
            landed(take.at[0, half_rows], sem_half.at[1, i])
            middle = act_a[rs, :].astype(F32) + mixed + take[0, half_rows, :].astype(F32)
            outv[rs, :] = middle
            n2 = (middle * row_scale(middle) * vec[1:2, :]).astype(BF16)
            act_a[rs, :] = n2
            remote(act_a.at[rs], act_a.at[rs], sem_n2.at[0, i], sem_n2.at[1, i], at(c=1 - c)).start()
            tr[:, rs] = n2.T

        @pl.when(lax.rem(t, tiles) == 1)
        def _():
            next_hop(t // tiles, True, True)

        @pl.when(t == tiles + 1)
        def _():
            cross(0)

        @pl.when(lax.rem(t, tiles) == tiles - 1)
        def _():
            next_hop(t // tiles, False, True)
            first_hop(t // tiles + 2)


    for slot in range(2):
        for i in range(3):
            spilled(slot, i, pl.ds(0, TILE)).wait()
    local(outv.at[mine], spill_h, sem_spill.at[7]).start()
    cross(1)

    @pl.loop(0, tiles)
    def _(t):
        half_rows = span_of(t * TILE, TILE, TILE)
        rs = span_of(c * rows + t * TILE, TILE, TILE)
        ro = span_of((1 - c) * rows + t * TILE, TILE, TILE)
        dnv[ro, :] = jnp.zeros((TILE, width), F32)
        dnv[rs, :] = jnp.zeros((TILE, width), F32)
        landed(tr.at[half_rows, other], sem_half.at[0, t])

    @pl.loop(0, tiles)
    def _(t):
        rs = span_of(c * rows + t * TILE, TILE, TILE)
        ro = span_of((1 - c) * rows + t * TILE, TILE, TILE)
        landed(act_a.at[rs], sem_n2.at[0, t])
        landed(act_a.at[ro], sem_n2.at[1, t])
        tr[:, ro] = act_a[ro, :].T

    landed(act_b.at[other], sem_pair.at[3])
    landed(act_b.at[mine], sem_pair.at[2])
    local(outv.at[mine], spill_h, sem_spill.at[7]).wait()
    arrived_shared(0)
    load(0)
    loaded_weights()

    big = 512
    zb = big // (ny * dn)

    def hid(w):
        return acts[2 * w : 2 * w + 2].reshape(2 * rows, CHUNK)

    def compute(m):
        slot = m % slots

        @pl.loop(0, 2 * rows // big)
        def _(r):
            rs = span_of(r * big, big, big)
            gate = wgu[0].reshape(width, CHUNK)
            up = wgu[1].reshape(width, CHUNK)
            n2r = act_a[rs, :]
            g = dot(n2r, gate)
            v = dot(n2r, up)
            s = jax.nn.sigmoid(g)
            sg_ = g * s
            q = (sg_ * v).astype(BF16)
            dq = dot_nt(act_b[rs, :], wd[...])
            gg = (dq * v * s * (1.0 + g * (1.0 - s))).astype(BF16)
            gv = (dq * sg_).astype(BF16)
            zi = pl.ds((r % 2) * zb, zb)
            for w, value in enumerate((q, gg, gv)):
                acts[2 * w + r // 2, zi] = value.reshape(zb, ny, dn, CHUNK)
            outv[rs, :] += dot(q, wd[...])

            @pl.when(r == 1)
            def _():
                pass_on(m + RELAY)

            dnv[rs, :] += dot_nt(gg, gate) + dot_nt(gv, up)

        @pl.when(m == 0)
        def _():
            arrived_shared(1)

        @pl.when(jnp.logical_and(m >= 1, m + 1 < steps))
        def _():
            arrived(m + 1)

        @pl.when(m + 1 < steps)
        def _():
            load(m + 1)

        weight_grads(slot, hid(1), hid(2))
        for h in range(nx):
            gd[slot, h] = dot_tn(hid(0), act_b[:, pl.ds(h * lanes, lanes)]).astype(BF16)

    def weight_grads(slot, first, second):
        group = n // 4

        @pl.loop(0, 4)
        def _(t):
            a = tr[span_of(t * TILE, TILE, TILE), :]
            for w, src in enumerate((first, second)):
                full = dot(a, src).astype(BF16).reshape(group, nx, dnx, CHUNK)
                for h in range(nx):
                    for k in range(group):
                        j = t * group + k
                        ggu[slot, w, h, j // ny, j % ny] = full[k, h]

    def has_rows(m):
        return m < chunks - 1

    def send_x(m):
        slot = m % slots
        for d in range(1, nx):
            xo = xp(d)
            remote(ggu.at[slot, :, xo], h0g.at[m, d - 1], sa_g.at[slot], ra_g.at[m], at(x=xo)).start()

            @pl.when(has_rows(m))
            def _():
                remote(gd.at[slot, xo], h0d.at[m, d - 1], sa_d.at[slot], ra_d.at[m], at(x=xo)).start()

    def fetch_x(m):
        landed(h0g.at[m], ra_g.at[m])
        local(h0g.at[m], vag, ld0.at[0]).start()

        @pl.when(has_rows(m))
        def _():
            landed(h0d.at[m], ra_d.at[m])
            local(h0d.at[m], vad, ld0.at[1]).start()

    def sum_x(m):
        slot = m % slots
        landed(h0g.at[m], sa_g.at[slot])
        landed(vag, ld0.at[0])

        @pl.loop(0, nz)
        def _(zi):
            for yi in range(ny):
                for w in range(2):
                    total = ggu[slot, w, x, zi, yi].astype(F32)
                    for d in range(1, nx):
                        total += vag[d - 1, w, zi, yi].astype(F32)
                    s1g[yi, w, zi] = total.astype(BF16)

        local(s1g, h1g.at[m], st1.at[0]).start()

        @pl.when(has_rows(m))
        def _():
            landed(h0d.at[m], sa_d.at[slot])
            landed(vad, ld0.at[1])
            total = gd[slot, x].astype(F32)
            for d in range(1, nx):
                total += vad[d - 1].astype(F32)
            s1d[...] = total.astype(BF16)
            copy = local(s1d, h1d.at[m], st1.at[1])
            copy.start()
            copy.wait()

        landed(s1g, st1.at[0])

    def send_y(m, _):
        for d in range(1, ny):
            yo = yp(d)
            remote(h1g.at[m, yo], hyg.at[m, d - 1], sy_g.at[m], ry_g.at[m], at(y=yo)).start()

        @pl.when(has_rows(m))
        def _():
            for q in range(pieces):
                _, yo, _ = grad_owner(m, q)
                part = pl.ds(q * gp, gp)

                @pl.when(yo != y)
                def _():
                    d = lax.rem(yo - y + ny, ny)
                    remote(h1d.at[m, part], hyd.at[m, d - 1, part], sy_d.at[m, q], ry_d.at[m, q], at(y=yo)).start()

    def y_copies(m, i):
        copies = [local(h1g.at[m, y], y1g.at[i], ld1.at[i, 0]), local(hyg.at[m], yrg.at[i], ld1.at[i, 1])]
        late = [local(h1d.at[m], y1d.at[i], ld1.at[i, 2]), local(hyd.at[m], yrd.at[i], ld1.at[i, 3])]
        return copies, late

    def fetch_y(m, i):
        landed(hyg.at[m], ry_g.at[m])
        copies, late = y_copies(m, i)
        for copy in copies:
            copy.start()

        @pl.when(m < chunks - 1)
        def _():
            for q in range(pieces):
                _, yo, _ = grad_owner(m, q)

                @pl.when(yo == y)
                def _():
                    landed(hyd.at[m, :, pl.ds(q * gp, gp)], ry_d.at[m, q])

            for copy in late:
                copy.start()

    def send_z(m, i):
        copies, late = y_copies(m, i)
        for copy in copies:
            copy.wait()
        for zi in range(nz):
            for w in range(2):
                total = y1g[i, w, zi].astype(F32)
                for d in range(1, ny):
                    total += yrg[i, d - 1, w, zi].astype(F32)
                s1g[0, w, zi] = total.astype(BF16)
        stores = [local(s1g.at[0], h2g.at[m], st2.at[0]), local(s1d, h2d.at[m], st2.at[1])]
        stores[0].start()

        @pl.when(m < chunks - 1)
        def _():
            for copy in late:
                copy.wait()
            total = y1d[i].astype(F32)
            for d in range(1, ny):
                total += yrd[i, d - 1].astype(F32)
            s1d[...] = total.astype(BF16)
            stores[1].start()
            stores[1].wait()

        stores[0].wait()
        for d in range(1, nz):
            zo = zp(d)
            remote(h2g.at[m, :, zo], hzg.at[m, d - 1], sz_g.at[m], rz_g.at[m], at(z=zo)).start()

        @pl.when(m < chunks - 1)
        def _():
            for q in range(pieces):
                zo, yo, _ = grad_owner(m, q)
                part = pl.ds(q * gp, gp)

                @pl.when(jnp.logical_and(yo == y, zo != z))
                def _():
                    d = lax.rem(zo - z + nz, nz)
                    remote(h2d.at[m, part], hzd.at[m, d - 1, part], sz_d.at[m, q], rz_d.at[m, q], at(z=zo)).start()

    def z_copies(m, i):
        copies = [local(h2g.at[m, :, z], z2g.at[i], ld2.at[i, 0]), local(hzg.at[m], zrg.at[i], ld2.at[i, 1])]
        late = [local(h2d.at[m], z2d.at[i], ld2.at[i, 2]), local(hzd.at[m], zrd.at[i], ld2.at[i, 3])]
        return copies, late

    def fetch_z(m, i):
        landed(hzg.at[m], rz_g.at[m])
        copies, late = z_copies(m, i)
        for copy in copies:
            copy.start()

        @pl.when(m < chunks - 1)
        def _():
            for q in range(pieces):
                zo, yo, _ = grad_owner(m, q)

                @pl.when(jnp.logical_and(yo == y, zo == z))
                def _():
                    landed(hzd.at[m, :, pl.ds(q * gp, gp)], rz_d.at[m, q])

            for copy in late:
                copy.start()

    def rep(p):
        d, e = reps[p]
        return at(x=xp(d), c=lax.rem(c + e, 2))

    direct_reps = [p for p, (d, e) in enumerate(reps) if d == 0 or e == 0]

    def spread(there, ssem, rsem):
        for p in direct_reps:
            remote(there, there, ssem.at[p], rsem.at[p], rep(p)).start()

    def own_gu(xs, cs):
        return gu_full.at[:, pl.ds(pl.multiple_of(xs * dnx, dnx), dnx), span_of(cs * half, half, BLOCK)]

    def own_in(xs, k):
        return in_full.at[
            pl.ds(pl.multiple_of(xs * dnx, dnx), dnx), span_of(k * width + c * chan, chan, chan)
        ]

    in_size = in_full.at[pl.ds(0, dnx), pl.ds(0, 3 * chan)]

    def own_lanes(ref, xs):
        return ref.at[:, span_of(xs * lanes, lanes, BLOCK)]

    def hand_over(mixer):
        for d in range(1, nx):
            p, q = reps.index((d, 0)), reps.index((d, 1))
            xs = lax.rem(x - d + nx, nx)
            sems = (fs_i, fr_i) if mixer else (fs_g, fr_g)
            landed(in_size if mixer else own_gu(xs, c), sems[1].at[p])
            for part in [own_in(xs, k) for k in range(3)] if mixer else [own_gu(xs, c)]:
                remote(part, part, sems[0].at[q], sems[1].at[q], at(c=1 - c)).start()

            @pl.when(in_half)
            def _():
                part = own_lanes(out_full if mixer else down_full, xs)
                landed(part, (fr_o if mixer else fr_d).at[p])
                remote(part, part, (fs_o if mixer else fs_d).at[q], (fr_o if mixer else fr_d).at[q], at(c=1 - c)).start()

    def finish(m, i):
        copies, late = z_copies(m, i)
        for copy in copies:
            copy.wait()
        for w in range(2):
            total = z2g[i, w].astype(F32)
            for d in range(1, nz):
                total += zrg[i, d - 1, w].astype(F32)
            fing[w] = total.astype(BF16)

        @pl.when(m < steps)
        def _():
            b = blocks(m)
            for k in range(2):
                there = gu_full.at[
                    :, pl.ds(pl.multiple_of(x * dnx, dnx), dnx), span_of(c * half + b[k] * BLOCK, BLOCK, BLOCK)
                ]
                copy = local(fing.at[:, :, pl.ds(k * BLOCK, BLOCK)], there, st3.at[0])
                copy.start()
                copy.wait()
                spread(there, fs_g, fr_g)

        @pl.when(m >= steps)
        def _():
            for w in range(2):
                there = in_full.at[
                    pl.ds(pl.multiple_of(x * dnx, dnx), dnx),
                    span_of((m - steps) * width + c * chan + w * CHUNK, CHUNK, CHUNK),
                ]
                copy = local(fing.at[w], there, st3.at[0])
                copy.start()
                copy.wait()
                spread(there, fs_i, fr_i)

        @pl.when(m < chunks - 1)
        def _():
            for copy in late:
                copy.wait()
            for q in range(pieces):
                zo, yo, row = grad_owner(m, q)
                part = pl.ds(q * gp, gp)

                @pl.when(jnp.logical_and(yo == y, zo == z))
                def _():
                    total = z2d[i, part].astype(F32)
                    for d in range(1, nz):
                        total += zrd[i, d - 1, part].astype(F32)
                    find[...] = total.astype(BF16)

                    @pl.when(m < steps)
                    def _():
                        there = down_full.at[pl.ds(row, gp), span_of(x * lanes, lanes, BLOCK)]
                        copy = local(find, there, st3.at[1])
                        copy.start()
                        copy.wait()
                        spread(there, fs_d, fr_d)

                    @pl.when(m >= steps)
                    def _():
                        there = out_full.at[pl.ds(row, gp), span_of(x * lanes, lanes, BLOCK)]
                        copy = local(find, there, st3.at[1])
                        copy.start()
                        copy.wait()
                        spread(there, fs_o, fr_o)

    def gone(m):
        return jnp.clip(jnp.minimum(m - 1, 2 * (m - HOLD)), 0, chunks)

    def two(m, do):
        for i in range(2):
            k = gone(m - 1) + i

            @pl.when(k < gone(m))
            def _():
                do(k, i)

    def own_rep():
        return x * 2 + c

    def sum_reps():
        local(sg, sg_all.at[own_rep()], sem_sum.at[0]).start()
        for p in range(len(reps)):
            remote(sg, sg_all.at[own_rep()], sem_sum.at[1], sem_sum.at[2], rep(p)).start()

    def sum_group():
        landed(sg, sem_sum.at[0])
        landed(sg_all.at[pl.ds(0, len(reps))], sem_sum.at[1])
        landed(sg_all.at[pl.ds(0, len(reps))], sem_sum.at[2])
        total = sg_all[0]
        for p in range(1, 2 * nx):
            total += sg_all[p]
        for j in range(n):
            sg_mine[j] = total[:, j * dn : (j + 1) * dn]
        local(sg_mine.at[me], sg_parts.at[me], sem_sum.at[3]).start()
        for d in range(1, n):
            j = lax.rem(me + d, n)
            remote(sg_mine.at[j], sg_parts.at[me], sem_sum.at[4], sem_sum.at[5], member(j)).start()

    def sum_last():
        landed(sg_mine.at[0], sem_sum.at[3])
        landed(sg_parts.at[pl.ds(0, n - 1)], sem_sum.at[4])
        landed(sg_parts.at[pl.ds(0, n - 1)], sem_sum.at[5])
        total = sg_parts[0]
        for j in range(1, n):
            total += sg_parts[j]
        smallv[0] = total
        local(smallv.at[0], small_out, sem_in.at[0]).start()

    def give_sums():
        @pl.loop(0, tiles)
        def _(t):
            rl = span_of(t * TILE, TILE, TILE)
            ro = span_of((1 - c) * rows + t * TILE, TILE, TILE)
            for i, src in enumerate((outv, dnv)):
                side = pl.ds(i * width, width)
                tr[rl, side] = src[ro, :].astype(BF16)
                remote(
                    tr.at[rl, side], take.at[i, rl], sem_sums.at[i, t], sem_sums.at[2 + i, t], at(c=1 - c)
                ).start()

        local(spill_h, outv.at[other], sem_spill.at[7]).start()
        local(tok_in, act_a.at[mine], sem_in.at[0]).start()
        local(spill_t, act_a.at[other], sem_spill.at[6]).start()

    def loaded(t, i):
        src = spill_p.at[i, span_of(t * TILE, TILE, TILE)]
        dst = dnv.at[span_of((1 - c) * rows + i * TILE, TILE, TILE), span_of((t % 2) * chan, chan, chan)]
        return local(src, dst, sem_spill.at[(t % 2) * 3 + i])

    def mixer_back():
        mixer_load()
        conv_acc[...] = jnp.zeros_like(conv_acc)
        sg[...] = jnp.zeros_like(sg)
        local(spill_h, outv.at[other], sem_spill.at[7]).wait()
        for i in range(3):
            loaded(0, i).start()

        @pl.loop(0, tiles)
        def _(t):
            rl = span_of(t * TILE, TILE, TILE)
            rs = span_of(c * rows + t * TILE, TILE, TILE)
            ro = span_of((1 - c) * rows + t * TILE, TILE, TILE)
            for i in range(2):
                landed(take.at[i, rl], sem_sums.at[2 + i, t])
                landed(take.at[i, rl], sem_sums.at[i, t])
            total = outv[rs, :] + take[0, rl, :].astype(F32)
            tr[rl, pl.ds(0, width)] = (total * live_in[rl, :]).astype(BF16)
            dn2 = dnv[rs, :] + take[1, rl, :].astype(F32)
            middle = outv[ro, :]
            scale = row_scale(middle)
            unit = middle * scale
            sg[1:2, :] += jnp.sum(dn2 * unit, axis=0, keepdims=True)
            d2 = dn2 * vec[1:2, :]
            back = scale * (d2 - unit * jnp.mean(d2 * unit, axis=-1, keepdims=True))
            back = act_b[rs, :].astype(F32) + back
            dnv[rs, :] = back
            act_b[rs, :] = back.astype(BF16)
            remote(act_b.at[rs], act_b.at[rs], sem_dm.at[0, t], sem_dm.at[1, t], at(c=1 - c)).start()

        out = local(tr.at[:, pl.ds(0, width)], y_out, sem_in.at[1])
        out.start()
        local(tok_in, act_a.at[mine], sem_in.at[0]).wait()
        local(spill_t, act_a.at[other], sem_spill.at[6]).wait()
        out.wait()

        @pl.loop(0, 2 * tiles)
        def _(t):
            rs = span_of(t * TILE, TILE, TILE)
            tr[:, rs] = normed(act_a[rs, :].astype(F32)).T

        @pl.loop(0, tiles)
        def _(t):
            landed(act_b.at[span_of(c * rows + t * TILE, TILE, TILE)], sem_dm.at[0, t])
            landed(act_b.at[span_of((1 - c) * rows + t * TILE, TILE, TILE)], sem_dm.at[1, t])

        for cc in range(2):

            @pl.loop(0, seqs)
            def _(s):
                head = act_b[span_of(cc * rows + s * span, EDGE, span), :].astype(F32)
                for k in range(2):
                    hf[k, pl.ds(s, 1), :] = head[k : k + 1, :]

            for k in range(2):
                own = slice(cc * seqs, (cc + 1) * seqs)
                ks[k, own, :] = dot_nt(hf[k].astype(BF16), wout[...]) * chd[k, own, :]

        @pl.when(me > 0)
        def _():
            remote(ks, kh, sem_kh.at[0], sem_kh.at[1], member(lax.rem(me + n - 1, n))).start()

        @pl.when(me == n - 1)
        def _():
            kh[...] = jnp.zeros_like(kh)

        for h in range(nx):
            side = pl.ds(h * lanes, lanes)
            gd[steps % slots, h] = dot_tn(zv[:, :CHUNK], act_b[:, side]).astype(BF16)
            og[h] = dot_tn(zv[:, CHUNK:], act_b[:, side]).astype(BF16)

        @pl.when(me < n - 1)
        def _():
            landed(kh, sem_kh.at[1])

        @pl.loop(0, 2 * tiles)
        def _(t):
            rs = span_of(t * TILE, TILE, TILE)
            first = t * tseq
            for i in range(3):
                loaded(t, i).wait()

            @pl.when(t + 1 < 2 * tiles)
            def _():
                for i in range(3):
                    loaded(t + 1, i).start()

            for h in range(2):
                hl = pl.ds(h * CHUNK, CHUNK)
                dz = dot_nt(act_b[rs, :], wout[hl, :]).reshape(tseq, span, CHUNK)
                b_gate, c_gate, x_value = (
                    dnv[
                        span_of((1 - c) * rows + i * TILE, TILE, TILE),
                        span_of((t % 2) * chan + h * CHUNK, CHUNK, CHUNK),
                    ].reshape(tseq, span, CHUNK)
                    for i in range(3)
                )
                *lags, conv = convolve((b_gate * x_value).reshape(TILE, CHUNK), first, h)
                dk = dz * c_gate
                for k in range(3):
                    conv_acc[k : k + 1, hl] += jnp.sum((dk * lags[k]).reshape(TILE, CHUNK), axis=0, keepdims=True)
                vb[:, :span, :] = dk
                for i in range(tseq):
                    for k in range(2):
                        vb[i, span + k : span + k + 1, :] = kh[k, pl.ds(first + i, 1), hl]
                du = tap(2, h) * dk + tap(1, h) * vb[:, 1 : 1 + span, :] + tap(0, h) * vb[:, 2 : 2 + span, :]
                act_a[rs, hl] = (du * x_value).astype(BF16).reshape(TILE, CHUNK)
                act_a[rs, pl.ds(chan + h * CHUNK, CHUNK)] = (dz * conv).astype(BF16).reshape(TILE, CHUNK)
                zv[rs, hl] = (du * b_gate).astype(BF16).reshape(TILE, CHUNK)

    def share_back():
        @pl.loop(0, 2 * tiles)
        def _(t):
            rs = span_of(tile_start(t), TILE, TILE)
            total = dot_nt(act_a[rs, :CHUNK], win(0))
            for b in range(1, 6):
                src = act_a[rs, b * CHUNK : (b + 1) * CHUNK] if b < 4 else zv[rs, (b - 4) * CHUNK : (b - 3) * CHUNK]
                total += dot_nt(src, win(b))

            @pl.when(t < tiles)
            def _():
                act_b[rs, :] = total.astype(BF16)

            @pl.when(t >= tiles)
            def _():
                outv[rs, :] = total

            @pl.when(t == tiles - 1)
            def _():
                remote(act_b.at[other], take.at[0], sem_pair.at[4], sem_pair.at[5], at(c=1 - c)).start()
                local(tok_in, act_b.at[mine], sem_in.at[0]).start()

    def finish_back():
        landed(take.at[0], sem_pair.at[5])
        local(tok_in, act_b.at[mine], sem_in.at[0]).wait()

        @pl.loop(0, tiles)
        def _(t):
            rl = span_of(t * TILE, TILE, TILE)
            rs = span_of(c * rows + t * TILE, TILE, TILE)
            tokens = act_b[rs, :].astype(F32)
            scale = row_scale(tokens)
            unit = tokens * scale
            dn1 = outv[rs, :] + take[0, rl, :].astype(F32)
            sg[0:1, :] += jnp.sum(dn1 * unit, axis=0, keepdims=True)
            d1 = dn1 * vec[0:1, :]
            back = dnv[rs, :] + scale * (d1 - unit * jnp.mean(d1 * unit, axis=-1, keepdims=True))
            take[1, rl, :] = (back * live_in[rl, :]).astype(BF16)

        local(take.at[1], dx_out, sem_in.at[1]).start()
        sg[2:5, span_of(c * chan, chan, chan)] = conv_acc[0:3, :]
        sum_reps()

    @pl.loop(0, chunks + 4)
    def _(m):
        @pl.when(m < steps)
        def _():
            compute(m)

        @pl.when(m == steps - 1)
        def _():
            give_sums()

        @pl.when(m == steps)
        def _():
            mixer_back()

        @pl.when(jnp.logical_and(m >= steps, m < chunks - 1))
        def _():
            b = (m - steps) * 2 * CHUNK
            weight_grads(
                m % slots, act_a[:, span_of(b, CHUNK, CHUNK)], act_a[:, span_of(b + CHUNK, CHUNK, CHUNK)]
            )

        @pl.when(m == steps + 1)
        def _():
            gd[(steps + 1) % slots] = og[...]

        @pl.when(m == chunks - 1)
        def _():
            weight_grads(m % slots, zv[:, :CHUNK], zv[:, CHUNK:])

        @pl.when(m < chunks)
        def _():
            send_x(m)

        @pl.when(jnp.logical_and(m >= 2, m < chunks + 2))
        def _():
            fetch_x(m - 2)

        two(m - 1, fetch_y)
        two(m - 2, fetch_z)
        pass_on_far(m + RELAY)

        @pl.when(jnp.logical_and(m >= 2, m < chunks + 2))
        def _():
            sum_x(m - 2)

        two(m, send_y)
        two(m - 1, send_z)
        two(m - 2, finish)

        @pl.when(m == steps + 1)
        def _():
            share_back()

        @pl.when(m == chunks - 1)
        def _():
            finish_back()

        @pl.when(m == chunks)
        def _():
            sum_group()

        @pl.when(m == chunks + 1)
        def _():
            sum_last()
            hand_over(False)

        @pl.when(m + 1 < steps)
        def _():
            loaded_weights()

    landed(take.at[1], sem_in.at[1])
    landed(smallv.at[0], sem_in.at[0])

    @pl.loop(0, chunks)
    def _(m):
        landed(hyg.at[m], sy_g.at[m])
        landed(hzg.at[m], sz_g.at[m])

        @pl.when(m < chunks - 1)
        def _():
            for q in range(pieces):
                zo, yo, _ = grad_owner(m, q)
                part = pl.ds(q * gp, gp)

                @pl.when(yo != y)
                def _():
                    landed(h1d.at[m, part], sy_d.at[m, q])

                @pl.when(jnp.logical_and(yo == y, zo != z))
                def _():
                    landed(h2d.at[m, part], sz_d.at[m, q])

    hand_over(True)
    for p in range(len(reps)):
        landed(own_gu(0, 0), fs_g.at[p])
        landed(in_size, fs_i.at[p])

        @pl.when(in_half)
        def _():
            landed(own_lanes(down_full, 0), fs_d.at[p])
            landed(own_lanes(out_full, 0), fs_o.at[p])
    landed(take.at[0], sem_pair.at[4])

    @pl.when(me > 0)
    def _():
        landed(ks, sem_kh.at[0])

    for p, (ax, d) in enumerate(ag_peers):
        direct = ax == 1 or off(zp(d)) < (nz - 1) ** 2

        @pl.when(direct)
        def _():
            landed(all_in.at[pl.ds(0, 3) if ax else pl.ds(0, 6), 0, 0], mg_send.at[p])
            landed(all_gu.at[pl.ds(0, steps - ax), :, 0, 0], ag_send.at[p])

        @pl.when(jnp.logical_and(direct, in_half))
        def _():
            landed(all_out.at[0], mg_osend.at[p])
            landed(all_down.at[:, pl.ds(0, gp)], ag_dsend.at[p])

    @pl.when(inner)
    def _():
        landed(all_in.at[:, 0, 0], ag_far.at[0])
        landed(all_gu.at[:, :, 0, 0], ag_far.at[2])

    @pl.when(z == jnp.where(c == 0, 2, 1))
    def _():
        landed(all_out.at[0], ag_far.at[1])
        landed(all_down.at[:, pl.ds(0, gp)], ag_far.at[3])

    for d in range(1, nz):
        for e in range(1, ny):
            landed(all_in.at[pl.ds(0, 3), 0, 0], mg_relay.at[d - 1, e - 1])
            landed(all_gu.at[pl.ds(0, steps - 1), :, 0, 0], ag_relay.at[d - 1, e - 1])
    for e in range(1, ny):
        landed(all_in.at[pl.ds(0, 3), :, 0], mg_cross.at[e - 1])
        landed(all_gu.at[0, :, :, 0], ag_cross.at[e - 1])
    for o in range(n // 2):
        zo, yo = out_owner(o)

        @pl.when(jnp.logical_and(zo != z, yo == y))
        def _():
            for e in range(1, ny):
                landed(all_out.at[0], mg_orelay.at[o, e - 1])

    for k in range(2):
        zo = (n // 2 * c) // ny + k

        @pl.when(zo != z)
        def _():
            for e in range(1, ny):
                landed(all_down.at[:, pl.ds(0, gp)], ag_drelay.at[zo % 2, e - 1])

    for p, (d, e) in enumerate(reps):
        if d == 0 or e == 1:
            landed(own_gu(0, 0), fr_g.at[p])
            landed(in_size, fr_i.at[p])

            @pl.when(jnp.logical_not(in_half))
            def _():
                landed(own_lanes(down_full, 0), fr_d.at[p])
                landed(own_lanes(out_full, 0), fr_o.at[p])


def block_call(sizes, *operands):
    nx, nz, ny, seqs, span, width, hidden = sizes
    n = nz * ny
    rows = seqs * span
    dn = width // n
    dnx = dn // nx
    half = hidden // 2
    chan = width // 2
    steps = half // CHUNK
    own_rows = hidden // n
    gp = min(BLOCK, own_rows & -own_rows)
    pieces = CHUNK // gp
    lanes = width // nx
    chunks = steps + 3
    tseq = TILE // span
    tiles = rows // TILE
    reps = 2 * nx - 1
    hops = nz + ny - 2
    dma = lambda *dims: pltpu.SemaphoreType.DMA(dims)
    bf = lambda *dims: pltpu.VMEM(dims, BF16)
    fl = lambda *dims: pltpu.VMEM(dims, F32)
    anywhere = pl.BlockSpec(memory_space=pl.ANY)
    shape = jax.ShapeDtypeStruct
    specs = [anywhere] * 10
    specs[3] = pl.BlockSpec(memory_space=pltpu.VMEM)
    return pl.pallas_call(
        functools.partial(block_kernel, sizes),
        out_shape=[
            shape((rows, width), BF16),
            shape((rows, width), BF16),
            shape((2, dn, hidden), BF16),
            shape((own_rows, width), BF16),
            shape((dn, 3 * width), BF16),
            shape((dn, width), BF16),
            shape((8, dn), F32),
            shape((steps, 2, nz, ny, dn, CHUNK), BF16),
            shape((steps, CHUNK, width), BF16),
            shape((6, nz, ny, dn, CHUNK), BF16),
            shape((n // 2, dn, width), BF16),
            shape((3, 2 * rows, chan), F32),
            shape((rows, width), F32),
            shape((rows, width), BF16),
            shape((chunks, nx - 1, 2, nz, ny, dnx, CHUNK), BF16),
            shape((chunks, nx - 1, CHUNK, lanes), BF16),
            shape((chunks, ny, 2, nz, dnx, CHUNK), BF16),
            shape((chunks, CHUNK, lanes), BF16),
            shape((chunks, ny - 1, 2, nz, dnx, CHUNK), BF16),
            shape((chunks, ny - 1, CHUNK, lanes), BF16),
            shape((chunks, 2, nz, dnx, CHUNK), BF16),
            shape((chunks, CHUNK, lanes), BF16),
            shape((chunks, nz - 1, 2, dnx, CHUNK), BF16),
            shape((chunks, nz - 1, CHUNK, lanes), BF16),
        ],
        in_specs=specs,
        out_specs=[anywhere] * 24,
        scratch_shapes=[
            bf(2 * rows, width),
            bf(2 * rows, width),
            bf(width, 2 * rows),
            bf(2, nz, ny, dn, CHUNK),
            bf(CHUNK, width),
            fl(2 * rows, width),
            fl(2 * rows, width),
            bf(6, nz, ny, dn, CHUNK),
            bf(chan, width),
            bf(2 * rows, chan),
            bf(2, rows, width),
            fl(tseq, span + EDGE, CHUNK),
            fl(tseq, span + EDGE, CHUNK),
            bf(2, 2, seqs, width),
            fl(2, 2 * seqs, chan),
            fl(2, 2 * seqs, chan),
            fl(2, 2 * seqs, chan),
            fl(2, 2 * seqs, chan),
            fl(2, seqs, width),
            fl(n, 8, dn),
            fl(8, width),
            fl(8, chan),
            fl(8, width),
            fl(2 * nx, 8, width),
            fl(n, 8, dn),
            fl(n, 8, dn),
            bf(3, 2, nx, nz, ny, dnx, CHUNK),
            bf(3, nx, CHUNK, lanes),
            bf(nx - 1, 2, nz, ny, dnx, CHUNK),
            bf(nx - 1, CHUNK, lanes),
            bf(ny, 2, nz, dnx, CHUNK),
            bf(CHUNK, lanes),
            bf(nx, CHUNK, lanes),
            bf(2, 2, nz, dnx, CHUNK),
            bf(2, CHUNK, lanes),
            bf(2, ny - 1, 2, nz, dnx, CHUNK),
            bf(2, ny - 1, CHUNK, lanes),
            bf(2, 2, dnx, CHUNK),
            bf(2, CHUNK, lanes),
            bf(2, nz - 1, 2, dnx, CHUNK),
            bf(2, nz - 1, CHUNK, lanes),
            bf(2, dnx, CHUNK),
            bf(gp, lanes),
            dma(2),
            dma(2 + n // 2),
            dma(2, steps * pieces),
            dma(6),
            dma(2, tiles),
            dma(2, tiles),
            dma(4, tiles),
            dma(2, tiles),
            dma(3),
            dma(4),
            dma(2),
            dma(8),
            dma(ny - 1),
            dma(SHARED, ny - 1),
            dma(ny - 1),
            dma(6, ny - 1),
            dma(4),
            dma(steps, nz - 1),
            dma(steps, ny - 1),
            dma(steps, pieces),
            dma(steps, pieces),
            dma(hops),
            dma(nz - 1, ny - 1),
            dma(hops),
            dma(2, ny - 1),
            dma(2),
            dma(6, nz - 1),
            dma(6, ny - 1),
            dma(n // 2),
            dma(n // 2),
            dma(hops),
            dma(nz - 1, ny - 1),
            dma(hops),
            dma(n // 2, ny - 1),
            dma(chunks),
            dma(chunks),
            dma(3),
            dma(3),
            dma(2),
            dma(2),
            dma(chunks),
            dma(chunks, pieces),
            dma(chunks),
            dma(chunks, pieces),
            dma(2, 4),
            dma(2),
            dma(chunks),
            dma(chunks, pieces),
            dma(chunks),
            dma(chunks, pieces),
            dma(2, 4),
            dma(2),
            dma(reps),
            dma(reps),
            dma(reps),
            dma(reps),
            dma(reps),
            dma(reps),
            dma(reps),
            dma(reps),
            dma(6),
        ],
        compiler_params=pltpu.CompilerParams(
            collective_id=0, has_side_effects=True, vmem_limit_bytes=63 << 20
        ),
        name="gated_block",
    )(*operands)[:7]


def live_mask(lengths, deal, span):
    slots = jnp.arange(deal.shape[1], dtype=jnp.int32)
    picked = deal[0][:, None] == slots[None, :]
    source_len = jnp.sum(jnp.where(picked, lengths[0][:, None], 0), axis=0)
    position = lax.axis_index(GROUP) * span + jnp.arange(span, dtype=jnp.int32)
    return (position[None, :] < source_len[:, None]).astype(F32).reshape(-1, 1)


def body(
    tokens,
    cotangent,
    lengths,
    deal,
    norm_gain,
    in_weight,
    conv_weight,
    out_weight,
    ffn_gain,
    gate_weight,
    up_weight,
    down_weight,
):
    seqs, span, width = tokens.shape
    hidden = gate_weight.shape[1]
    nx, nz, ny = (lax.axis_size(axis) for axis in ("x", "z", "y"))
    dn = width // (nz * ny)
    small = jnp.stack([norm_gain, ffn_gain, *(conv_weight[:, k] for k in range(3))]).astype(F32)
    small = jnp.pad(small, ((0, 3), (0, 0)))
    block_out, block_grad, gu, down, mixer_in, mixer_out, sums = block_call(
        (nx, nz, ny, seqs, span, width, hidden),
        tokens.reshape(-1, width),
        tokens[:, span - 2 :].transpose(1, 0, 2),
        cotangent.reshape(-1, width),
        live_mask(lengths, deal, span),
        small,
        in_weight,
        out_weight,
        gate_weight,
        up_weight,
        down_weight,
    )
    return (
        block_out.reshape(tokens.shape),
        block_grad.reshape(tokens.shape),
        sums[0],
        mixer_in.astype(F32),
        sums[2:5].T,
        mixer_out.astype(F32),
        sums[1],
        gu[0].astype(F32),
        gu[1].astype(F32),
        down.astype(F32),
    )


def solution(mesh):
    rep, fsdp = mesh.shape["rep"], mesh.shape["fsdp"]
    grid = (rep // 2, 2, 4, fsdp // 4)
    split = Mesh(mesh.devices.reshape(grid), ("x", "core", "z", "y"))
    copies = ("x", "core")
    rows = P(copies, GROUP, None)
    lists = P(copies, None)
    vector = P(GROUP)
    matrix = P(GROUP, None)
    return jax.shard_map(
        body,
        mesh=split,
        in_specs=(
            rows,
            rows,
            lists,
            lists,
            vector,
            matrix,
            matrix,
            matrix,
            vector,
            matrix,
            matrix,
            matrix,
        ),
        out_specs=(rows, rows, vector, matrix, matrix, matrix, vector, matrix, matrix, matrix),
        check_vma=False,
    )
```

```python
import functools
import jax
import jax.numpy as jnp
from jax import lax
from jax.experimental import pallas as pl
from jax.experimental.pallas import tpu as pltpu
from jax.sharding import Mesh, PartitionSpec as P

EPS = 1e-05
F32 = jnp.float32
BF16 = jnp.bfloat16
NT = (((1,), (1,)), ((), ()))
TN = (((0,), (0,)), ((), ()))
MESH = pl.DeviceIdType.MESH
GROUP = ("z", "y")
CHUNK = 256
BLOCK = 128
TILE = 256
EDGE = 8
AHEAD = 4
RELAY = 2
HOLD = 5
SHARED = 2


def dot(left, right):
    return jnp.dot(left, right, preferred_element_type=F32)


def dot_nt(left, right):
    return lax.dot_general(left, right, NT, preferred_element_type=F32)


def dot_tn(left, right):
    return lax.dot_general(left, right, TN, preferred_element_type=F32)


def row_scale(values):
    return lax.rsqrt(jnp.mean(values * values, axis=-1, keepdims=True) + EPS)


def block_kernel(
    sizes,
    tok_in, edge_in, cot_in, live_in, small_in, in_in, out_in, gate_in, up_in, down_in,
    y_out, dx_out, gu_full, down_full, in_full, out_full, small_out,
    all_gu, all_down, all_in, all_out, spill_p, spill_h, spill_t,
    h0g, h0d, h1g, h1d, hyg, hyd, h2g, h2d, hzg, hzd,
    act_a, act_b, tr, wgu, wd, outv, dnv, acts, wout, zv, take,
    ub, vb, hal, uh, kh, ks, chd, hf, smallv, vec, conv_acc, sg, sg_all, sg_mine, sg_parts,
    ggu, gd, vag, vad, s1g, s1d, og, y1g, y1d, yrg, yrd, z2g, z2d, zrg, zrd, fing, find,
    sem_in, sem_load, sem_own, sem_pair, sem_half, sem_n2, sem_sums, sem_dm, sem_small, sem_edge, sem_kh, sem_spill,
    ag_cross, ag_x, mg_cross, mg_x, ag_far, ag_z, ag_y, ag_dz, ag_dy, ag_send, ag_relay, ag_dsend, ag_drelay,
    mg_own, mg_z, mg_y, mg_oz, mg_oy, mg_send, mg_relay, mg_osend, mg_orelay,
    ra_g, ra_d, sa_g, sa_d, ld0, st1, ry_g, ry_d, sy_g, sy_d, ld1, st2, rz_g, rz_d, sz_g, sz_d, ld2, st3,
    fs_g, fs_i, fs_d, fs_o, fr_g, fr_i, fr_d, fr_o, sem_sum,
):
    nx, nz, ny, seqs, span, width, hidden = sizes
    n = nz * ny
    rows = seqs * span
    dn = width // n
    dnx = dn // nx
    half = hidden // 2
    chan = width // 2
    steps = half // CHUNK
    chunks = steps + 3
    per_half = half // BLOCK // 2
    own_rows = hidden // n
    gp = min(BLOCK, own_rows & -own_rows)
    pieces = CHUNK // gp
    lanes = width // nx
    slots = 3
    tiles = rows // TILE
    tseq = TILE // span
    x, c = lax.axis_index("x"), lax.axis_index("core")
    z, y = lax.axis_index("z"), lax.axis_index("y")
    me = z * ny + y
    in_half = me // (n // 2) == c

    def at(x=x, c=c, z=z, y=y):
        return (x, c, z, y)

    def member(j, c=c):
        return at(c=c, z=j // ny, y=j % ny)

    def zp(d):
        return lax.rem(z + d, nz)

    def yp(d):
        return lax.rem(y + d, ny)

    def xp(d):
        return lax.rem(x + d, nx)

    def remote(src, dst, ssem, rsem, dev):
        return pltpu.make_async_remote_copy(
            src_ref=src, dst_ref=dst, send_sem=ssem, recv_sem=rsem, device_id=dev, device_id_type=MESH
        )

    def local(src, dst, sem):
        return pltpu.make_async_copy(src, dst, sem)

    def landed(ref, sem):
        pltpu.make_async_copy(ref, ref, sem).wait()

    def span_of(start, size, align):
        return pl.ds(pl.multiple_of(start, align), size)

    mine = span_of(c * rows, rows, rows)
    other = span_of((1 - c) * rows, rows, rows)

    barrier = pltpu.get_barrier_semaphore()
    peers = [member(lax.rem(me + d, n)) for d in range(1, n)]
    reps = [(d, e) for d in range(nx) for e in range(2) if d + e > 0]
    peers += [at(x=xp(d), c=lax.rem(c + e, 2)) for d, e in reps]
    peers += [member(lax.rem(me + d, n), c=1 - c) for d in (1, n - 1)]
    for dev in peers:
        pl.semaphore_signal(barrier, inc=1, device_id=dev, device_id_type=MESH)
    pl.semaphore_wait(barrier, len(peers))

    local(small_in, smallv.at[me], sem_small.at[0]).start()
    for d in range(1, n):
        remote(small_in, smallv.at[me], sem_small.at[1], sem_small.at[2], member(lax.rem(me + d, n))).start()

    @pl.when(me < n - 1)
    def _():
        for e in range(2):
            dev = member(lax.rem(me + 1, n), c=lax.rem(c + e, 2))
            remote(edge_in, hal.at[c], sem_edge.at[e], sem_edge.at[2 + c], dev).start()

    local(tok_in, act_a.at[mine], sem_in.at[0]).start()
    local(cot_in, take.at[1], sem_in.at[1]).start()
    remote(tok_in, act_a.at[mine], sem_pair.at[0], sem_pair.at[1], at(c=1 - c)).start()

    ag_peers = [(0, d) for d in range(1, nz)] + [(1, d) for d in range(1, ny)]

    def toward(ax, d):
        return at(z=zp(d)) if ax == 0 else at(y=yp(d))

    def mixer_first_hop(b):
        here = in_in.at[:, span_of((b // 2) * width + c * chan + (b % 2) * CHUNK, CHUNK, CHUNK)]
        there = all_in.at[b, z, y]
        local(here, there, mg_own.at[0]).start()
        hops(here, there, mg_send, lambda d: mg_z.at[b, d - 1], lambda d: mg_y.at[b, d - 1], b % 2)

    def out_first_hop():
        @pl.when(in_half)
        def _():
            o = me - c * (n // 2)
            local(out_in, all_out.at[o], mg_own.at[1]).start()
            hops(out_in, all_out.at[o], mg_osend, lambda d: mg_oz.at[o], lambda d: mg_oy.at[o])

    def off(zs):
        return (zs - z) * (zs - z)

    inner = jnp.logical_and(z > 0, z < nz - 1)
    end = jnp.where(z == 1, 0, nz - 1)
    end_slot = jnp.where(z == 1, 0, nz - 2)

    plane = x % 2
    partner = x + 1 - 2 * plane

    def hops(here, there, send, recv_z, recv_y, only=None):
        for p, (ax, d) in enumerate(ag_peers):
            if ax == 1:

                @pl.when(True if only is None else plane == only)
                def _():
                    remote(here, there, send.at[p], recv_y(d), toward(ax, d)).start()
            elif d in (1, nz - 1):

                @pl.when(off(zp(d)) < (nz - 1) ** 2)
                def _():
                    remote(here, there, send.at[p], recv_z(d), toward(ax, d)).start()
            else:
                remote(here, there, send.at[p], recv_z(d), toward(ax, d)).start()

    def out_owner(o):
        j = c * (n // 2) + o
        return j // ny, j % ny

    def along_y(block, send, recv):
        for e in range(1, ny):
            remote(block, block, send.at[e - 1], recv(e), at(y=yp(e))).start()

    def along(block, part, wanted, d, near, arrived, far_send, far_recv, y_send, y_recv):
        if d in (1, nz - 1):
            this = off(lax.rem(z - d + nz, nz)) == (nz - 1) ** 2

            @pl.when(jnp.logical_not(this) if near else this)
            def _():
                landed(block, arrived)

                @pl.when(wanted)
                def _():
                    along_y(part, y_send, y_recv)
        elif near:
            landed(block, arrived)

            @pl.when(inner)
            def _():
                remote(block, block, far_send, far_recv, at(z=end)).start()

            @pl.when(wanted)
            def _():
                along_y(part, y_send, y_recv)

    def mixer_cross(b):
        @pl.when(plane == b % 2)
        def _():
            for e in range(1, ny):
                block = all_in.at[b, :, lax.rem(y - e + ny, ny)]
                landed(block, mg_y.at[b, e - 1])
                remote(block, block, mg_cross.at[e - 1], mg_x.at[b, e - 1], at(x=partner)).start()

    def mixer_hop(b, near):
        for d in range(1, nz):
            block = all_in.at[b, lax.rem(z - d + nz, nz), y]
            along(
                block, block, plane == b % 2, d, near, mg_z.at[b, d - 1], ag_far.at[0], mg_z.at[b, end_slot], mg_relay.at[d - 1], lambda e: mg_y.at[b, e - 1]
            )

    def owned(block, zo, near, arrived, far_send, y_send, y_recv):
        @pl.when(off(zo) < (nz - 1) ** 2 if near else off(zo) == (nz - 1) ** 2)
        def _():
            landed(block, arrived)

            @pl.when(jnp.logical_and(inner, off(zo) == 4))
            def _():
                remote(block, block, far_send, arrived, at(z=end)).start()

            along_y(block, y_send, y_recv)

    def out_hop(near):
        for o in range(n // 2):
            zo, yo = out_owner(o)

            @pl.when(jnp.logical_and(zo != z, yo == y))
            def _():
                owned(all_out.at[o], zo, near, mg_oz.at[o], ag_far.at[1], mg_orelay.at[o], lambda e: mg_oy.at[o])

    def mixer_arrived():
        for e in range(1, ny):
            for b in range(6):

                @pl.when(plane != b % 2)
                def _():
                    landed(all_in.at[b, :, lax.rem(y - e + ny, ny)], mg_x.at[b, e - 1])
        for o in range(n // 2):
            _, yo = out_owner(o)

            @pl.when(yo != y)
            def _():
                landed(all_out.at[o], mg_oy.at[o])

        landed(all_in.at[:, 0, 0], mg_own.at[0])

        @pl.when(in_half)
        def _():
            landed(all_out.at[0], mg_own.at[1])

    def mixer_load():
        copies = [local(all_in, acts, sem_load.at[0])]
        copies += [local(all_out.at[o], wout.at[pl.ds(o * dn, dn)], sem_load.at[2 + o]) for o in range(n // 2)]
        for copy in copies:
            copy.start()
        for copy in copies:
            copy.wait()

    def blocks(m):
        h, i = m % 2, m // 2
        first = per_half * h + i
        return first, per_half * h + per_half - 1 - i + per_half * (m // (2 * (per_half // 2)))

    def column(b):
        return pl.multiple_of(c * half + b * BLOCK, BLOCK)

    def owner(m, q):
        b = blocks(m)[q * gp // BLOCK]
        row = c * half + b * BLOCK + (q * gp) % BLOCK
        j = row // own_rows
        return j // ny, j % ny, pl.multiple_of(row - j * own_rows, gp)

    def grad_owner(m, q):
        zo, yo, row = owner(jnp.minimum(m, steps - 1), q)
        mixed = c * chan + jnp.maximum(m - steps, 0) * CHUNK + q * gp
        j = mixed // dn
        late = m >= steps
        return (
            jnp.where(late, j // ny, zo),
            jnp.where(late, j % ny, yo),
            pl.multiple_of(jnp.where(late, mixed - j * dn, row), gp),
        )

    def first_hop(m, shared=False):
        b = blocks(m)
        for k in range(2):
            for w, src in enumerate((gate_in, up_in)):
                here = src.at[:, pl.ds(column(b[k]), BLOCK)]
                there = all_gu.at[m, w, z, y, :, pl.ds(k * BLOCK, BLOCK)]
                local(here, there, sem_own.at[0, m]).start()
                hops(here, there, ag_send, lambda d: ag_z.at[m, d - 1], lambda d: ag_y.at[m, d - 1], k if shared else None)
        for q in range(pieces):
            zo, yo, row = owner(m, q)

            @pl.when(jnp.logical_and(zo == z, yo == y))
            def _():
                here = down_in.at[pl.ds(row, gp)]
                there = all_down.at[m, pl.ds(q * gp, gp)]
                local(here, there, sem_own.at[1, m * pieces + q]).start()
                hops(here, there, ag_dsend, lambda d: ag_dz.at[m, q], lambda d: ag_dy.at[m, q])

    def half_of(m, ys, side):
        return all_gu.at[m, :, :, ys, :, span_of(side * BLOCK, BLOCK, BLOCK)]

    def cross(m):
        for e in range(1, ny):
            block = half_of(m, lax.rem(y - e + ny, ny), plane)
            landed(block, ag_y.at[m, e - 1])
            remote(block, block, ag_cross.at[e - 1], ag_x.at[m, e - 1], at(x=partner)).start()

    def next_hop(m, near, shared=False):
        for d in range(1, nz):
            zs = lax.rem(z - d + nz, nz)
            block = all_gu.at[m, :, zs, y]
            part = all_gu.at[m, :, zs, y, :, span_of(plane * BLOCK, BLOCK, BLOCK)] if shared else block
            along(
                block, part, True, d, near, ag_z.at[m, d - 1], ag_far.at[2], ag_z.at[m, end_slot], ag_relay.at[d - 1], lambda e: ag_y.at[m, e - 1]
            )
        for q in range(pieces):
            zo, yo, _ = owner(m, q)

            @pl.when(jnp.logical_and(zo != z, yo == y))
            def _():
                block = all_down.at[m, pl.ds(q * gp, gp)]
                owned(block, zo, near, ag_dz.at[m, q], ag_far.at[3], ag_drelay.at[zo % 2], lambda e: ag_dy.at[m, q])

    def arrived_shared(m):
        for e in range(1, ny):
            landed(half_of(m, lax.rem(y - e + ny, ny), 1 - plane), ag_x.at[m, e - 1])

    def arrived(m):
        for e in range(1, ny):
            landed(all_gu.at[m, :, :, lax.rem(y - e + ny, ny)], ag_y.at[m, e - 1])

    def load(m):
        landed(all_gu.at[m, :, 0, 0], sem_own.at[0, m])
        for q in range(pieces):
            zo, yo, _ = owner(m, q)
            block = all_down.at[m, pl.ds(q * gp, gp)]

            @pl.when(jnp.logical_and(zo == z, yo == y))
            def _():
                landed(block, sem_own.at[1, m * pieces + q])

            @pl.when(yo != y)
            def _():
                landed(block, ag_dy.at[m, q])

        local(all_gu.at[m], wgu, sem_load.at[0]).start()
        local(all_down.at[m], wd, sem_load.at[1]).start()

    def loaded_weights():
        landed(wgu, sem_load.at[0])
        landed(wd, sem_load.at[1])

    def pass_on(m):
        @pl.when(m < steps)
        def _():
            next_hop(m, True)

    def pass_on_far(m):
        @pl.when(m < steps)
        def _():
            next_hop(m, False)

        @pl.when(m + AHEAD - RELAY < steps)
        def _():
            first_hop(m + AHEAD - RELAY)

    for b in range(3):
        mixer_first_hop(b)

    local(cot_in, take.at[1], sem_in.at[1]).wait()

    @pl.loop(0, tiles)
    def _(t):
        rl = span_of(t * TILE, TILE, TILE)
        rs = span_of(c * rows + t * TILE, TILE, TILE)
        act_b[rs, :] = (take[1, rl, :].astype(F32) * live_in[rl, :]).astype(BF16)

    remote(act_b.at[mine], act_b.at[mine], sem_pair.at[2], sem_pair.at[3], at(c=1 - c)).start()

    landed(small_in, sem_small.at[0])
    landed(smallv.at[pl.ds(0, n - 1)], sem_small.at[1])
    landed(smallv.at[pl.ds(0, n - 1)], sem_small.at[2])
    for j in range(n):
        vec[:, j * dn : (j + 1) * dn] = smallv[j]

    @pl.when(me < n - 1)
    def _():
        for e in range(2):
            landed(hal.at[0], sem_edge.at[e])

    @pl.when(me > 0)
    def _():
        for e in range(2):
            landed(hal.at[e], sem_edge.at[2 + e])

    @pl.when(me == 0)
    def _():
        hal[...] = jnp.zeros_like(hal)

    for b in range(8):
        if b < 6:
            mixer_hop(b, True)
        if 0 < b < 7:
            mixer_hop(b - 1, False)
        if b < 3:
            mixer_first_hop(b + 3)
        elif b == 3:
            out_first_hop()
        elif b > 5:
            out_hop(b == 6)
            first_hop(b - 6, True)
        if b > 1:
            mixer_cross(b - 2)
    local(tok_in, act_a.at[mine], sem_in.at[0]).wait()
    landed(act_a.at[mine], sem_pair.at[0])
    landed(act_a.at[other], sem_pair.at[1])
    local(act_a.at[other], spill_t, sem_spill.at[6]).start()
    mixer_arrived()
    mixer_load()

    def win(b):
        return acts[b].reshape(width, CHUNK)

    def tap(k, h):
        return vec[2 + k : 3 + k, span_of(c * chan + h * CHUNK, CHUNK, CHUNK)].reshape(1, 1, CHUNK)

    def normed(tokens):
        return (tokens * row_scale(tokens) * vec[0:1, :]).astype(BF16)

    for cc in range(2):
        for k in range(2):
            edge = normed(hal[cc, k].astype(F32))
            for h in range(2):
                hl = slice(h * CHUNK, (h + 1) * CHUNK)
                uh[k, cc * seqs : (cc + 1) * seqs, hl] = dot(edge, win(h)) * dot(edge, win(4 + h))

    def convolve(product, first, h):
        for i in range(tseq):
            for k in range(2):
                row = EDGE - 2 + k
                ub[i, row : row + 1, :] = uh[k, pl.ds(first + i, 1), h * CHUNK : (h + 1) * CHUNK]
        ub[:, EDGE:, :] = product.reshape(tseq, span, CHUNK)
        lag_two = ub[:, EDGE - 2 : EDGE - 2 + span, :]
        lag_one = ub[:, EDGE - 1 : EDGE - 1 + span, :]
        lag_none = ub[:, EDGE:, :]
        return lag_two, lag_one, lag_none, tap(0, h) * lag_two + tap(1, h) * lag_one + tap(2, h) * lag_none

    def spilled(t, i, rs):
        slot = t % 2
        src = dnv.at[span_of(slot * 3 * TILE + i * TILE, TILE, TILE), pl.ds(0, chan)]
        return local(src, spill_p.at[i, rs], sem_spill.at[slot * 3 + i])

    def tile_start(t):
        return lax.rem(t + (1 - c) * tiles, 2 * tiles) * TILE

    @pl.loop(0, 2 * tiles)
    def _(t):
        start = tile_start(t)
        rs = span_of(start, TILE, TILE)
        first = start // span
        tokens = act_a[rs, :].astype(F32)
        n1 = normed(tokens)

        @pl.when(t >= 2)
        def _():
            for i in range(3):
                spilled(t, i, rs).wait()

        for h in range(2):
            parts = [dot(n1, win(2 * i + h)) for i in range(3)]
            hl = pl.ds(h * CHUNK, CHUNK)
            for i in range(3):
                dnv[span_of((t % 2) * 3 * TILE + i * TILE, TILE, TILE), hl] = parts[i]
            for i in range(tseq):
                for k in range(2):
                    chd[k, pl.ds(first + i, 1), hl] = parts[1][i * span + k : i * span + k + 1, :]
            conv = convolve(parts[0] * parts[2], first, h)[3].reshape(TILE, CHUNK)
            zv[rs, hl] = (parts[1] * conv).astype(BF16)
        for i in range(3):
            spilled(t, i, rs).start()
        mixed = dot(zv[rs, :], wout[...])

        i = lax.rem(t, tiles)
        half_rows = span_of(i * TILE, TILE, TILE)

        @pl.when(t == 0)
        def _():
            landed(act_a.at[other], sem_spill.at[6])

        @pl.when(t < tiles)
        def _():
            tr[half_rows, other] = mixed.astype(BF16)
            remote(
                tr.at[half_rows, other], take.at[0, half_rows], sem_half.at[0, i], sem_half.at[1, i], at(c=1 - c)
            ).start()
            outv[rs, :] = jnp.zeros((TILE, width), F32)

        @pl.when(t >= tiles)
        def _():
            landed(take.at[0, half_rows], sem_half.at[1, i])
            middle = act_a[rs, :].astype(F32) + mixed + take[0, half_rows, :].astype(F32)
            outv[rs, :] = middle
            n2 = (middle * row_scale(middle) * vec[1:2, :]).astype(BF16)
            act_a[rs, :] = n2
            remote(act_a.at[rs], act_a.at[rs], sem_n2.at[0, i], sem_n2.at[1, i], at(c=1 - c)).start()
            tr[:, rs] = n2.T

        @pl.when(lax.rem(t, tiles) == 1)
        def _():
            next_hop(t // tiles, True, True)

        @pl.when(t == tiles + 1)
        def _():
            cross(0)

        @pl.when(lax.rem(t, tiles) == tiles - 1)
        def _():
            next_hop(t // tiles, False, True)
            first_hop(t // tiles + 2)


    for slot in range(2):
        for i in range(3):
            spilled(slot, i, pl.ds(0, TILE)).wait()
    local(outv.at[mine], spill_h, sem_spill.at[7]).start()
    cross(1)

    @pl.loop(0, tiles)
    def _(t):
        half_rows = span_of(t * TILE, TILE, TILE)
        rs = span_of(c * rows + t * TILE, TILE, TILE)
        ro = span_of((1 - c) * rows + t * TILE, TILE, TILE)
        dnv[ro, :] = jnp.zeros((TILE, width), F32)
        dnv[rs, :] = jnp.zeros((TILE, width), F32)
        landed(tr.at[half_rows, other], sem_half.at[0, t])

    @pl.loop(0, tiles)
    def _(t):
        rs = span_of(c * rows + t * TILE, TILE, TILE)
        ro = span_of((1 - c) * rows + t * TILE, TILE, TILE)
        landed(act_a.at[rs], sem_n2.at[0, t])
        landed(act_a.at[ro], sem_n2.at[1, t])
        tr[:, ro] = act_a[ro, :].T

    landed(act_b.at[other], sem_pair.at[3])
    landed(act_b.at[mine], sem_pair.at[2])
    local(outv.at[mine], spill_h, sem_spill.at[7]).wait()
    arrived_shared(0)
    load(0)
    loaded_weights()

    big = 512
    zb = big // (ny * dn)

    def hid(w):
        return acts[2 * w : 2 * w + 2].reshape(2 * rows, CHUNK)

    def compute(m):
        slot = m % slots

        @pl.loop(0, 2 * rows // big)
        def _(r):
            rs = span_of(r * big, big, big)
            gate = wgu[0].reshape(width, CHUNK)
            up = wgu[1].reshape(width, CHUNK)
            n2r = act_a[rs, :]
            g = dot(n2r, gate)
            v = dot(n2r, up)
            s = jax.nn.sigmoid(g)
            sg_ = g * s
            q = (sg_ * v).astype(BF16)
            dq = dot_nt(act_b[rs, :], wd[...])
            gg = (dq * v * s * (1.0 + g * (1.0 - s))).astype(BF16)
            gv = (dq * sg_).astype(BF16)
            zi = pl.ds((r % 2) * zb, zb)
            for w, value in enumerate((q, gg, gv)):
                acts[2 * w + r // 2, zi] = value.reshape(zb, ny, dn, CHUNK)
            outv[rs, :] += dot(q, wd[...])

            @pl.when(r == 1)
            def _():
                pass_on(m + RELAY)

            dnv[rs, :] += dot_nt(gg, gate) + dot_nt(gv, up)

        @pl.when(m == 0)
        def _():
            arrived_shared(1)

        @pl.when(jnp.logical_and(m >= 1, m + 1 < steps))
        def _():
            arrived(m + 1)

        @pl.when(m + 1 < steps)
        def _():
            load(m + 1)

        weight_grads(slot, hid(1), hid(2))
        for h in range(nx):
            gd[slot, h] = dot_tn(hid(0), act_b[:, pl.ds(h * lanes, lanes)]).astype(BF16)

    def weight_grads(slot, first, second):
        group = n // 4

        @pl.loop(0, 4)
        def _(t):
            a = tr[span_of(t * TILE, TILE, TILE), :]
            for w, src in enumerate((first, second)):
                full = dot(a, src).astype(BF16).reshape(group, nx, dnx, CHUNK)
                for h in range(nx):
                    for k in range(group):
                        j = t * group + k
                        ggu[slot, w, h, j // ny, j % ny] = full[k, h]

    def has_rows(m):
        return m < chunks - 1

    def send_x(m):
        slot = m % slots
        for d in range(1, nx):
            xo = xp(d)
            remote(ggu.at[slot, :, xo], h0g.at[m, d - 1], sa_g.at[slot], ra_g.at[m], at(x=xo)).start()

            @pl.when(has_rows(m))
            def _():
                remote(gd.at[slot, xo], h0d.at[m, d - 1], sa_d.at[slot], ra_d.at[m], at(x=xo)).start()

    def fetch_x(m):
        landed(h0g.at[m], ra_g.at[m])
        local(h0g.at[m], vag, ld0.at[0]).start()

        @pl.when(has_rows(m))
        def _():
            landed(h0d.at[m], ra_d.at[m])
            local(h0d.at[m], vad, ld0.at[1]).start()

    def sum_x(m):
        slot = m % slots
        landed(h0g.at[m], sa_g.at[slot])
        landed(vag, ld0.at[0])

        @pl.loop(0, nz)
        def _(zi):
            for yi in range(ny):
                for w in range(2):
                    total = ggu[slot, w, x, zi, yi].astype(F32)
                    for d in range(1, nx):
                        total += vag[d - 1, w, zi, yi].astype(F32)
                    s1g[yi, w, zi] = total.astype(BF16)

        local(s1g, h1g.at[m], st1.at[0]).start()

        @pl.when(has_rows(m))
        def _():
            landed(h0d.at[m], sa_d.at[slot])
            landed(vad, ld0.at[1])
            total = gd[slot, x].astype(F32)
            for d in range(1, nx):
                total += vad[d - 1].astype(F32)
            s1d[...] = total.astype(BF16)
            copy = local(s1d, h1d.at[m], st1.at[1])
            copy.start()
            copy.wait()

        landed(s1g, st1.at[0])

    def send_y(m, _):
        for d in range(1, ny):
            yo = yp(d)
            remote(h1g.at[m, yo], hyg.at[m, d - 1], sy_g.at[m], ry_g.at[m], at(y=yo)).start()

        @pl.when(has_rows(m))
        def _():
            for q in range(pieces):
                _, yo, _ = grad_owner(m, q)
                part = pl.ds(q * gp, gp)

                @pl.when(yo != y)
                def _():
                    d = lax.rem(yo - y + ny, ny)
                    remote(h1d.at[m, part], hyd.at[m, d - 1, part], sy_d.at[m, q], ry_d.at[m, q], at(y=yo)).start()

    def y_copies(m, i):
        copies = [local(h1g.at[m, y], y1g.at[i], ld1.at[i, 0]), local(hyg.at[m], yrg.at[i], ld1.at[i, 1])]
        late = [local(h1d.at[m], y1d.at[i], ld1.at[i, 2]), local(hyd.at[m], yrd.at[i], ld1.at[i, 3])]
        return copies, late

    def fetch_y(m, i):
        landed(hyg.at[m], ry_g.at[m])
        copies, late = y_copies(m, i)
        for copy in copies:
            copy.start()

        @pl.when(m < chunks - 1)
        def _():
            for q in range(pieces):
                _, yo, _ = grad_owner(m, q)

                @pl.when(yo == y)
                def _():
                    landed(hyd.at[m, :, pl.ds(q * gp, gp)], ry_d.at[m, q])

            for copy in late:
                copy.start()

    def send_z(m, i):
        copies, late = y_copies(m, i)
        for copy in copies:
            copy.wait()
        for zi in range(nz):
            for w in range(2):
                total = y1g[i, w, zi].astype(F32)
                for d in range(1, ny):
                    total += yrg[i, d - 1, w, zi].astype(F32)
                s1g[0, w, zi] = total.astype(BF16)
        stores = [local(s1g.at[0], h2g.at[m], st2.at[0]), local(s1d, h2d.at[m], st2.at[1])]
        stores[0].start()

        @pl.when(m < chunks - 1)
        def _():
            for copy in late:
                copy.wait()
            total = y1d[i].astype(F32)
            for d in range(1, ny):
                total += yrd[i, d - 1].astype(F32)
            s1d[...] = total.astype(BF16)
            stores[1].start()
            stores[1].wait()

        stores[0].wait()
        for d in range(1, nz):
            zo = zp(d)
            remote(h2g.at[m, :, zo], hzg.at[m, d - 1], sz_g.at[m], rz_g.at[m], at(z=zo)).start()

        @pl.when(m < chunks - 1)
        def _():
            for q in range(pieces):
                zo, yo, _ = grad_owner(m, q)
                part = pl.ds(q * gp, gp)

                @pl.when(jnp.logical_and(yo == y, zo != z))
                def _():
                    d = lax.rem(zo - z + nz, nz)
                    remote(h2d.at[m, part], hzd.at[m, d - 1, part], sz_d.at[m, q], rz_d.at[m, q], at(z=zo)).start()

    def z_copies(m, i):
        copies = [local(h2g.at[m, :, z], z2g.at[i], ld2.at[i, 0]), local(hzg.at[m], zrg.at[i], ld2.at[i, 1])]
        late = [local(h2d.at[m], z2d.at[i], ld2.at[i, 2]), local(hzd.at[m], zrd.at[i], ld2.at[i, 3])]
        return copies, late

    def fetch_z(m, i):
        landed(hzg.at[m], rz_g.at[m])
        copies, late = z_copies(m, i)
        for copy in copies:
            copy.start()

        @pl.when(m < chunks - 1)
        def _():
            for q in range(pieces):
                zo, yo, _ = grad_owner(m, q)

                @pl.when(jnp.logical_and(yo == y, zo == z))
                def _():
                    landed(hzd.at[m, :, pl.ds(q * gp, gp)], rz_d.at[m, q])

            for copy in late:
                copy.start()

    def rep(p):
        d, e = reps[p]
        return at(x=xp(d), c=lax.rem(c + e, 2))

    direct_reps = [p for p, (d, e) in enumerate(reps) if d == 0 or e == 0]

    def spread(there, ssem, rsem):
        for p in direct_reps:
            remote(there, there, ssem.at[p], rsem.at[p], rep(p)).start()

    def own_gu(xs, cs):
        return gu_full.at[:, pl.ds(pl.multiple_of(xs * dnx, dnx), dnx), span_of(cs * half, half, BLOCK)]

    def own_in(xs, k):
        return in_full.at[
            pl.ds(pl.multiple_of(xs * dnx, dnx), dnx), span_of(k * width + c * chan, chan, chan)
        ]

    in_size = in_full.at[pl.ds(0, dnx), pl.ds(0, 3 * chan)]

    def own_lanes(ref, xs):
        return ref.at[:, span_of(xs * lanes, lanes, BLOCK)]

    def hand_over(mixer):
        for d in range(1, nx):
            p, q = reps.index((d, 0)), reps.index((d, 1))
            xs = lax.rem(x - d + nx, nx)
            sems = (fs_i, fr_i) if mixer else (fs_g, fr_g)
            landed(in_size if mixer else own_gu(xs, c), sems[1].at[p])
            for part in [own_in(xs, k) for k in range(3)] if mixer else [own_gu(xs, c)]:
                remote(part, part, sems[0].at[q], sems[1].at[q], at(c=1 - c)).start()

            @pl.when(in_half)
            def _():
                part = own_lanes(out_full if mixer else down_full, xs)
                landed(part, (fr_o if mixer else fr_d).at[p])
                remote(part, part, (fs_o if mixer else fs_d).at[q], (fr_o if mixer else fr_d).at[q], at(c=1 - c)).start()

    def finish(m, i):
        copies, late = z_copies(m, i)
        for copy in copies:
            copy.wait()
        for w in range(2):
            total = z2g[i, w].astype(F32)
            for d in range(1, nz):
                total += zrg[i, d - 1, w].astype(F32)
            fing[w] = total.astype(BF16)
        part_rows = pl.ds(pl.multiple_of(x * dnx, dnx), dnx)
        part_lanes = span_of(x * lanes, lanes, BLOCK)
        b = blocks(jnp.minimum(m, steps - 1))

        def gu_place(k):
            return gu_full.at[:, part_rows, span_of(c * half + b[k] * BLOCK, BLOCK, BLOCK)]

        def in_place(w):
            start = jnp.maximum(m - steps, 0) * width + c * chan + w * CHUNK
            return in_full.at[part_rows, span_of(start, CHUNK, CHUNK)]

        def owned_rows(do):
            @pl.when(m < chunks - 1)
            def _():
                for q in range(pieces):
                    zo, yo, row = grad_owner(m, q)

                    @pl.when(jnp.logical_and(yo == y, zo == z))
                    def _():
                        do(q, pl.ds(q * gp, gp), pl.ds(row, gp))

        @pl.when(m < steps)
        def _():
            for k in range(2):
                local(fing.at[:, :, pl.ds(k * BLOCK, BLOCK)], gu_place(k), st3.at[0]).start()

        @pl.when(m >= steps)
        def _():
            for w in range(2):
                local(fing.at[w], in_place(w), st3.at[0]).start()

        @pl.when(m < chunks - 1)
        def _():
            for copy in late:
                copy.wait()

        def add_rows(q, part, rows_at):
            total = z2d[i, part].astype(F32)
            for d in range(1, nz):
                total += zrd[i, d - 1, part].astype(F32)
            find[part] = total.astype(BF16)

            @pl.when(m < steps)
            def _():
                local(find.at[part], down_full.at[rows_at, part_lanes], st3.at[1 + q]).start()

            @pl.when(m >= steps)
            def _():
                local(find.at[part], out_full.at[rows_at, part_lanes], st3.at[1 + q]).start()

        def spread_rows(q, part, rows_at):
            landed(find.at[part], st3.at[1 + q])

            @pl.when(m < steps)
            def _():
                spread(down_full.at[rows_at, part_lanes], fs_d, fr_d)

            @pl.when(m >= steps)
            def _():
                spread(out_full.at[rows_at, part_lanes], fs_o, fr_o)

        owned_rows(add_rows)
        landed(fing, st3.at[0])

        @pl.when(m < steps)
        def _():
            for k in range(2):
                spread(gu_place(k), fs_g, fr_g)

        @pl.when(m >= steps)
        def _():
            for w in range(2):
                spread(in_place(w), fs_i, fr_i)

        owned_rows(spread_rows)

    def gone(m):
        return jnp.clip(jnp.minimum(m - 1, 2 * (m - HOLD)), 0, chunks)

    def two(m, do):
        for i in range(2):
            k = gone(m - 1) + i

            @pl.when(k < gone(m))
            def _():
                do(k, i)

    def own_rep():
        return x * 2 + c

    def sum_reps():
        local(sg, sg_all.at[own_rep()], sem_sum.at[0]).start()
        for p in range(len(reps)):
            remote(sg, sg_all.at[own_rep()], sem_sum.at[1], sem_sum.at[2], rep(p)).start()

    def sum_group():
        landed(sg, sem_sum.at[0])
        landed(sg_all.at[pl.ds(0, len(reps))], sem_sum.at[1])
        landed(sg_all.at[pl.ds(0, len(reps))], sem_sum.at[2])
        total = sg_all[0]
        for p in range(1, 2 * nx):
            total += sg_all[p]
        for j in range(n):
            sg_mine[j] = total[:, j * dn : (j + 1) * dn]
        local(sg_mine.at[me], sg_parts.at[me], sem_sum.at[3]).start()
        for d in range(1, n):
            j = lax.rem(me + d, n)
            remote(sg_mine.at[j], sg_parts.at[me], sem_sum.at[4], sem_sum.at[5], member(j)).start()

    def sum_last():
        landed(sg_mine.at[0], sem_sum.at[3])
        landed(sg_parts.at[pl.ds(0, n - 1)], sem_sum.at[4])
        landed(sg_parts.at[pl.ds(0, n - 1)], sem_sum.at[5])
        total = sg_parts[0]
        for j in range(1, n):
            total += sg_parts[j]
        smallv[0] = total
        local(smallv.at[0], small_out, sem_in.at[0]).start()

    def give_sums():
        @pl.loop(0, tiles)
        def _(t):
            rl = span_of(t * TILE, TILE, TILE)
            ro = span_of((1 - c) * rows + t * TILE, TILE, TILE)
            for i, src in enumerate((outv, dnv)):
                side = pl.ds(i * width, width)
                tr[rl, side] = src[ro, :].astype(BF16)
                remote(
                    tr.at[rl, side], take.at[i, rl], sem_sums.at[i, t], sem_sums.at[2 + i, t], at(c=1 - c)
                ).start()

        local(spill_h, outv.at[other], sem_spill.at[7]).start()
        local(tok_in, act_a.at[mine], sem_in.at[0]).start()
        local(spill_t, act_a.at[other], sem_spill.at[6]).start()

    def loaded(t, i):
        src = spill_p.at[i, span_of(t * TILE, TILE, TILE)]
        dst = dnv.at[span_of((1 - c) * rows + i * TILE, TILE, TILE), span_of((t % 2) * chan, chan, chan)]
        return local(src, dst, sem_spill.at[(t % 2) * 3 + i])

    def mixer_back():
        mixer_load()
        conv_acc[...] = jnp.zeros_like(conv_acc)
        sg[...] = jnp.zeros_like(sg)
        local(spill_h, outv.at[other], sem_spill.at[7]).wait()
        for i in range(3):
            loaded(0, i).start()

        @pl.loop(0, tiles)
        def _(t):
            rl = span_of(t * TILE, TILE, TILE)
            rs = span_of(c * rows + t * TILE, TILE, TILE)
            ro = span_of((1 - c) * rows + t * TILE, TILE, TILE)
            for i in range(2):
                landed(take.at[i, rl], sem_sums.at[2 + i, t])
                landed(take.at[i, rl], sem_sums.at[i, t])
            total = outv[rs, :] + take[0, rl, :].astype(F32)
            tr[rl, pl.ds(0, width)] = (total * live_in[rl, :]).astype(BF16)
            dn2 = dnv[rs, :] + take[1, rl, :].astype(F32)
            middle = outv[ro, :]
            scale = row_scale(middle)
            unit = middle * scale
            sg[1:2, :] += jnp.sum(dn2 * unit, axis=0, keepdims=True)
            d2 = dn2 * vec[1:2, :]
            back = scale * (d2 - unit * jnp.mean(d2 * unit, axis=-1, keepdims=True))
            back = act_b[rs, :].astype(F32) + back
            dnv[rs, :] = back
            act_b[rs, :] = back.astype(BF16)
            remote(act_b.at[rs], act_b.at[rs], sem_dm.at[0, t], sem_dm.at[1, t], at(c=1 - c)).start()

        out = local(tr.at[:, pl.ds(0, width)], y_out, sem_in.at[1])
        out.start()
        local(tok_in, act_a.at[mine], sem_in.at[0]).wait()
        local(spill_t, act_a.at[other], sem_spill.at[6]).wait()
        out.wait()

        @pl.loop(0, 2 * tiles)
        def _(t):
            rs = span_of(t * TILE, TILE, TILE)
            tr[:, rs] = normed(act_a[rs, :].astype(F32)).T

        @pl.loop(0, tiles)
        def _(t):
            landed(act_b.at[span_of(c * rows + t * TILE, TILE, TILE)], sem_dm.at[0, t])
            landed(act_b.at[span_of((1 - c) * rows + t * TILE, TILE, TILE)], sem_dm.at[1, t])

        for cc in range(2):

            @pl.loop(0, seqs)
            def _(s):
                head = act_b[span_of(cc * rows + s * span, EDGE, span), :].astype(F32)
                for k in range(2):
                    hf[k, pl.ds(s, 1), :] = head[k : k + 1, :]

            for k in range(2):
                own = slice(cc * seqs, (cc + 1) * seqs)
                ks[k, own, :] = dot_nt(hf[k].astype(BF16), wout[...]) * chd[k, own, :]

        @pl.when(me > 0)
        def _():
            remote(ks, kh, sem_kh.at[0], sem_kh.at[1], member(lax.rem(me + n - 1, n))).start()

        @pl.when(me == n - 1)
        def _():
            kh[...] = jnp.zeros_like(kh)

        for h in range(nx):
            side = pl.ds(h * lanes, lanes)
            gd[steps % slots, h] = dot_tn(zv[:, :CHUNK], act_b[:, side]).astype(BF16)
            og[h] = dot_tn(zv[:, CHUNK:], act_b[:, side]).astype(BF16)

        @pl.when(me < n - 1)
        def _():
            landed(kh, sem_kh.at[1])

        @pl.loop(0, 2 * tiles)
        def _(t):
            rs = span_of(t * TILE, TILE, TILE)
            first = t * tseq
            for i in range(3):
                loaded(t, i).wait()

            @pl.when(t + 1 < 2 * tiles)
            def _():
                for i in range(3):
                    loaded(t + 1, i).start()

            for h in range(2):
                hl = pl.ds(h * CHUNK, CHUNK)
                dz = dot_nt(act_b[rs, :], wout[hl, :]).reshape(tseq, span, CHUNK)
                b_gate, c_gate, x_value = (
                    dnv[
                        span_of((1 - c) * rows + i * TILE, TILE, TILE),
                        span_of((t % 2) * chan + h * CHUNK, CHUNK, CHUNK),
                    ].reshape(tseq, span, CHUNK)
                    for i in range(3)
                )
                *lags, conv = convolve((b_gate * x_value).reshape(TILE, CHUNK), first, h)
                dk = dz * c_gate
                for k in range(3):
                    conv_acc[k : k + 1, hl] += jnp.sum((dk * lags[k]).reshape(TILE, CHUNK), axis=0, keepdims=True)
                vb[:, :span, :] = dk
                for i in range(tseq):
                    for k in range(2):
                        vb[i, span + k : span + k + 1, :] = kh[k, pl.ds(first + i, 1), hl]
                du = tap(2, h) * dk + tap(1, h) * vb[:, 1 : 1 + span, :] + tap(0, h) * vb[:, 2 : 2 + span, :]
                act_a[rs, hl] = (du * x_value).astype(BF16).reshape(TILE, CHUNK)
                act_a[rs, pl.ds(chan + h * CHUNK, CHUNK)] = (dz * conv).astype(BF16).reshape(TILE, CHUNK)
                zv[rs, hl] = (du * b_gate).astype(BF16).reshape(TILE, CHUNK)

    def share_back():
        @pl.loop(0, 2 * tiles)
        def _(t):
            rs = span_of(tile_start(t), TILE, TILE)
            total = dot_nt(act_a[rs, :CHUNK], win(0))
            for b in range(1, 6):
                src = act_a[rs, b * CHUNK : (b + 1) * CHUNK] if b < 4 else zv[rs, (b - 4) * CHUNK : (b - 3) * CHUNK]
                total += dot_nt(src, win(b))

            @pl.when(t < tiles)
            def _():
                act_b[rs, :] = total.astype(BF16)

            @pl.when(t >= tiles)
            def _():
                outv[rs, :] = total

            @pl.when(t == tiles - 1)
            def _():
                remote(act_b.at[other], take.at[0], sem_pair.at[4], sem_pair.at[5], at(c=1 - c)).start()
                local(tok_in, act_b.at[mine], sem_in.at[0]).start()

    def finish_back():
        landed(take.at[0], sem_pair.at[5])
        local(tok_in, act_b.at[mine], sem_in.at[0]).wait()

        @pl.loop(0, tiles)
        def _(t):
            rl = span_of(t * TILE, TILE, TILE)
            rs = span_of(c * rows + t * TILE, TILE, TILE)
            tokens = act_b[rs, :].astype(F32)
            scale = row_scale(tokens)
            unit = tokens * scale
            dn1 = outv[rs, :] + take[0, rl, :].astype(F32)
            sg[0:1, :] += jnp.sum(dn1 * unit, axis=0, keepdims=True)
            d1 = dn1 * vec[0:1, :]
            back = dnv[rs, :] + scale * (d1 - unit * jnp.mean(d1 * unit, axis=-1, keepdims=True))
            take[1, rl, :] = (back * live_in[rl, :]).astype(BF16)

        local(take.at[1], dx_out, sem_in.at[1]).start()
        sg[2:5, span_of(c * chan, chan, chan)] = conv_acc[0:3, :]
        sum_reps()

    @pl.loop(0, chunks + 4)
    def _(m):
        @pl.when(m < steps)
        def _():
            compute(m)

        @pl.when(m == steps - 1)
        def _():
            give_sums()

        @pl.when(m == steps)
        def _():
            mixer_back()

        @pl.when(jnp.logical_and(m >= steps, m < chunks - 1))
        def _():
            b = (m - steps) * 2 * CHUNK
            weight_grads(
                m % slots, act_a[:, span_of(b, CHUNK, CHUNK)], act_a[:, span_of(b + CHUNK, CHUNK, CHUNK)]
            )

        @pl.when(m == steps + 1)
        def _():
            gd[(steps + 1) % slots] = og[...]

        @pl.when(m == chunks - 1)
        def _():
            weight_grads(m % slots, zv[:, :CHUNK], zv[:, CHUNK:])

        @pl.when(m < chunks)
        def _():
            send_x(m)

        @pl.when(jnp.logical_and(m >= 2, m < chunks + 2))
        def _():
            fetch_x(m - 2)

        two(m - 1, fetch_y)
        two(m - 2, fetch_z)
        pass_on_far(m + RELAY)

        @pl.when(jnp.logical_and(m >= 2, m < chunks + 2))
        def _():
            sum_x(m - 2)

        two(m, send_y)
        two(m - 1, send_z)
        two(m - 2, finish)

        @pl.when(m == steps + 1)
        def _():
            share_back()

        @pl.when(m == chunks - 1)
        def _():
            finish_back()

        @pl.when(m == chunks)
        def _():
            sum_group()

        @pl.when(m == chunks + 1)
        def _():
            sum_last()
            hand_over(False)

        @pl.when(m + 1 < steps)
        def _():
            loaded_weights()

    landed(take.at[1], sem_in.at[1])
    landed(smallv.at[0], sem_in.at[0])

    @pl.loop(0, chunks)
    def _(m):
        landed(hyg.at[m], sy_g.at[m])
        landed(hzg.at[m], sz_g.at[m])

        @pl.when(m < chunks - 1)
        def _():
            for q in range(pieces):
                zo, yo, _ = grad_owner(m, q)
                part = pl.ds(q * gp, gp)

                @pl.when(yo != y)
                def _():
                    landed(h1d.at[m, part], sy_d.at[m, q])

                @pl.when(jnp.logical_and(yo == y, zo != z))
                def _():
                    landed(h2d.at[m, part], sz_d.at[m, q])

    hand_over(True)
    for p in range(len(reps)):
        landed(own_gu(0, 0), fs_g.at[p])
        landed(in_size, fs_i.at[p])

        @pl.when(in_half)
        def _():
            landed(own_lanes(down_full, 0), fs_d.at[p])
            landed(own_lanes(out_full, 0), fs_o.at[p])
    landed(take.at[0], sem_pair.at[4])

    @pl.when(me > 0)
    def _():
        landed(ks, sem_kh.at[0])

    for p, (ax, d) in enumerate(ag_peers):
        direct = ax == 1 or off(zp(d)) < (nz - 1) ** 2

        @pl.when(direct)
        def _():
            landed(all_in.at[pl.ds(0, 3) if ax else pl.ds(0, 6), 0, 0], mg_send.at[p])
            landed(all_gu.at[pl.ds(0, steps - ax), :, 0, 0], ag_send.at[p])

        @pl.when(jnp.logical_and(direct, in_half))
        def _():
            landed(all_out.at[0], mg_osend.at[p])
            landed(all_down.at[:, pl.ds(0, gp)], ag_dsend.at[p])

    @pl.when(inner)
    def _():
        landed(all_in.at[:, 0, 0], ag_far.at[0])
        landed(all_gu.at[:, :, 0, 0], ag_far.at[2])

    @pl.when(z == jnp.where(c == 0, 2, 1))
    def _():
        landed(all_out.at[0], ag_far.at[1])
        landed(all_down.at[:, pl.ds(0, gp)], ag_far.at[3])

    for d in range(1, nz):
        for e in range(1, ny):
            landed(all_in.at[pl.ds(0, 3), 0, 0], mg_relay.at[d - 1, e - 1])
            landed(all_gu.at[pl.ds(0, steps - 1), :, 0, 0], ag_relay.at[d - 1, e - 1])
    for e in range(1, ny):
        landed(all_in.at[pl.ds(0, 3), :, 0], mg_cross.at[e - 1])
        landed(all_gu.at[0, :, :, 0], ag_cross.at[e - 1])
    for o in range(n // 2):
        zo, yo = out_owner(o)

        @pl.when(jnp.logical_and(zo != z, yo == y))
        def _():
            for e in range(1, ny):
                landed(all_out.at[0], mg_orelay.at[o, e - 1])

    for k in range(2):
        zo = (n // 2 * c) // ny + k

        @pl.when(zo != z)
        def _():
            for e in range(1, ny):
                landed(all_down.at[:, pl.ds(0, gp)], ag_drelay.at[zo % 2, e - 1])

    for p, (d, e) in enumerate(reps):
        if d == 0 or e == 1:
            landed(own_gu(0, 0), fr_g.at[p])
            landed(in_size, fr_i.at[p])

            @pl.when(jnp.logical_not(in_half))
            def _():
                landed(own_lanes(down_full, 0), fr_d.at[p])
                landed(own_lanes(out_full, 0), fr_o.at[p])


def block_call(sizes, *operands):
    nx, nz, ny, seqs, span, width, hidden = sizes
    n = nz * ny
    rows = seqs * span
    dn = width // n
    dnx = dn // nx
    half = hidden // 2
    chan = width // 2
    steps = half // CHUNK
    own_rows = hidden // n
    gp = min(BLOCK, own_rows & -own_rows)
    pieces = CHUNK // gp
    lanes = width // nx
    chunks = steps + 3
    tseq = TILE // span
    tiles = rows // TILE
    reps = 2 * nx - 1
    hops = nz + ny - 2
    dma = lambda *dims: pltpu.SemaphoreType.DMA(dims)
    bf = lambda *dims: pltpu.VMEM(dims, BF16)
    fl = lambda *dims: pltpu.VMEM(dims, F32)
    anywhere = pl.BlockSpec(memory_space=pl.ANY)
    shape = jax.ShapeDtypeStruct
    specs = [anywhere] * 10
    specs[3] = pl.BlockSpec(memory_space=pltpu.VMEM)
    return pl.pallas_call(
        functools.partial(block_kernel, sizes),
        out_shape=[
            shape((rows, width), BF16),
            shape((rows, width), BF16),
            shape((2, dn, hidden), BF16),
            shape((own_rows, width), BF16),
            shape((dn, 3 * width), BF16),
            shape((dn, width), BF16),
            shape((8, dn), F32),
            shape((steps, 2, nz, ny, dn, CHUNK), BF16),
            shape((steps, CHUNK, width), BF16),
            shape((6, nz, ny, dn, CHUNK), BF16),
            shape((n // 2, dn, width), BF16),
            shape((3, 2 * rows, chan), F32),
            shape((rows, width), F32),
            shape((rows, width), BF16),
            shape((chunks, nx - 1, 2, nz, ny, dnx, CHUNK), BF16),
            shape((chunks, nx - 1, CHUNK, lanes), BF16),
            shape((chunks, ny, 2, nz, dnx, CHUNK), BF16),
            shape((chunks, CHUNK, lanes), BF16),
            shape((chunks, ny - 1, 2, nz, dnx, CHUNK), BF16),
            shape((chunks, ny - 1, CHUNK, lanes), BF16),
            shape((chunks, 2, nz, dnx, CHUNK), BF16),
            shape((chunks, CHUNK, lanes), BF16),
            shape((chunks, nz - 1, 2, dnx, CHUNK), BF16),
            shape((chunks, nz - 1, CHUNK, lanes), BF16),
        ],
        in_specs=specs,
        out_specs=[anywhere] * 24,
        scratch_shapes=[
            bf(2 * rows, width),
            bf(2 * rows, width),
            bf(width, 2 * rows),
            bf(2, nz, ny, dn, CHUNK),
            bf(CHUNK, width),
            fl(2 * rows, width),
            fl(2 * rows, width),
            bf(6, nz, ny, dn, CHUNK),
            bf(chan, width),
            bf(2 * rows, chan),
            bf(2, rows, width),
            fl(tseq, span + EDGE, CHUNK),
            fl(tseq, span + EDGE, CHUNK),
            bf(2, 2, seqs, width),
            fl(2, 2 * seqs, chan),
            fl(2, 2 * seqs, chan),
            fl(2, 2 * seqs, chan),
            fl(2, 2 * seqs, chan),
            fl(2, seqs, width),
            fl(n, 8, dn),
            fl(8, width),
            fl(8, chan),
            fl(8, width),
            fl(2 * nx, 8, width),
            fl(n, 8, dn),
            fl(n, 8, dn),
            bf(3, 2, nx, nz, ny, dnx, CHUNK),
            bf(3, nx, CHUNK, lanes),
            bf(nx - 1, 2, nz, ny, dnx, CHUNK),
            bf(nx - 1, CHUNK, lanes),
            bf(ny, 2, nz, dnx, CHUNK),
            bf(CHUNK, lanes),
            bf(nx, CHUNK, lanes),
            bf(2, 2, nz, dnx, CHUNK),
            bf(2, CHUNK, lanes),
            bf(2, ny - 1, 2, nz, dnx, CHUNK),
            bf(2, ny - 1, CHUNK, lanes),
            bf(2, 2, dnx, CHUNK),
            bf(2, CHUNK, lanes),
            bf(2, nz - 1, 2, dnx, CHUNK),
            bf(2, nz - 1, CHUNK, lanes),
            bf(2, dnx, CHUNK),
            bf(CHUNK, lanes),
            dma(2),
            dma(2 + n // 2),
            dma(2, steps * pieces),
            dma(6),
            dma(2, tiles),
            dma(2, tiles),
            dma(4, tiles),
            dma(2, tiles),
            dma(3),
            dma(4),
            dma(2),
            dma(8),
            dma(ny - 1),
            dma(SHARED, ny - 1),
            dma(ny - 1),
            dma(6, ny - 1),
            dma(4),
            dma(steps, nz - 1),
            dma(steps, ny - 1),
            dma(steps, pieces),
            dma(steps, pieces),
            dma(hops),
            dma(nz - 1, ny - 1),
            dma(hops),
            dma(2, ny - 1),
            dma(2),
            dma(6, nz - 1),
            dma(6, ny - 1),
            dma(n // 2),
            dma(n // 2),
            dma(hops),
            dma(nz - 1, ny - 1),
            dma(hops),
            dma(n // 2, ny - 1),
            dma(chunks),
            dma(chunks),
            dma(3),
            dma(3),
            dma(2),
            dma(2),
            dma(chunks),
            dma(chunks, pieces),
            dma(chunks),
            dma(chunks, pieces),
            dma(2, 4),
            dma(2),
            dma(chunks),
            dma(chunks, pieces),
            dma(chunks),
            dma(chunks, pieces),
            dma(2, 4),
            dma(1 + pieces),
            dma(reps),
            dma(reps),
            dma(reps),
            dma(reps),
            dma(reps),
            dma(reps),
            dma(reps),
            dma(reps),
            dma(6),
        ],
        compiler_params=pltpu.CompilerParams(
            collective_id=0, has_side_effects=True, vmem_limit_bytes=63 << 20
        ),
        name="gated_block",
    )(*operands)[:7]


def live_mask(lengths, deal, span):
    slots = jnp.arange(deal.shape[1], dtype=jnp.int32)
    picked = deal[0][:, None] == slots[None, :]
    source_len = jnp.sum(jnp.where(picked, lengths[0][:, None], 0), axis=0)
    position = lax.axis_index(GROUP) * span + jnp.arange(span, dtype=jnp.int32)
    return (position[None, :] < source_len[:, None]).astype(F32).reshape(-1, 1)


def body(
    tokens,
    cotangent,
    lengths,
    deal,
    norm_gain,
    in_weight,
    conv_weight,
    out_weight,
    ffn_gain,
    gate_weight,
    up_weight,
    down_weight,
):
    seqs, span, width = tokens.shape
    hidden = gate_weight.shape[1]
    nx, nz, ny = (lax.axis_size(axis) for axis in ("x", "z", "y"))
    dn = width // (nz * ny)
    small = jnp.stack([norm_gain, ffn_gain, *(conv_weight[:, k] for k in range(3))]).astype(F32)
    small = jnp.pad(small, ((0, 3), (0, 0)))
    block_out, block_grad, gu, down, mixer_in, mixer_out, sums = block_call(
        (nx, nz, ny, seqs, span, width, hidden),
        tokens.reshape(-1, width),
        tokens[:, span - 2 :].transpose(1, 0, 2),
        cotangent.reshape(-1, width),
        live_mask(lengths, deal, span),
        small,
        in_weight,
        out_weight,
        gate_weight,
        up_weight,
        down_weight,
    )
    return (
        block_out.reshape(tokens.shape),
        block_grad.reshape(tokens.shape),
        sums[0],
        mixer_in.astype(F32),
        sums[2:5].T,
        mixer_out.astype(F32),
        sums[1],
        gu[0].astype(F32),
        gu[1].astype(F32),
        down.astype(F32),
    )


def solution(mesh):
    rep, fsdp = mesh.shape["rep"], mesh.shape["fsdp"]
    grid = (rep // 2, 2, 4, fsdp // 4)
    split = Mesh(mesh.devices.reshape(grid), ("x", "core", "z", "y"))
    copies = ("x", "core")
    rows = P(copies, GROUP, None)
    lists = P(copies, None)
    vector = P(GROUP)
    matrix = P(GROUP, None)
    return jax.shard_map(
        body,
        mesh=split,
        in_specs=(
            rows,
            rows,
            lists,
            lists,
            vector,
            matrix,
            matrix,
            matrix,
            vector,
            matrix,
            matrix,
            matrix,
        ),
        out_specs=(rows, rows, vector, matrix, matrix, matrix, vector, matrix, matrix, matrix),
        check_vma=False,
    )
```

```python
import functools
import jax
import jax.numpy as jnp
from jax import lax
from jax.experimental import pallas as pl
from jax.experimental.pallas import tpu as pltpu
from jax.sharding import Mesh, PartitionSpec as P

EPS = 1e-05
F32 = jnp.float32
BF16 = jnp.bfloat16
NT = (((1,), (1,)), ((), ()))
TN = (((0,), (0,)), ((), ()))
MESH = pl.DeviceIdType.MESH
GROUP = ("z", "y")
CHUNK = 256
BLOCK = 128
TILE = 256
EDGE = 8
AHEAD = 4
RELAY = 2
HOLD = 5
SHARED = 2


def dot(left, right):
    return jnp.dot(left, right, preferred_element_type=F32)


def dot_nt(left, right):
    return lax.dot_general(left, right, NT, preferred_element_type=F32)


def dot_tn(left, right):
    return lax.dot_general(left, right, TN, preferred_element_type=F32)


def row_scale(values):
    return lax.rsqrt(jnp.mean(values * values, axis=-1, keepdims=True) + EPS)


def block_kernel(
    sizes,
    tok_in, edge_in, cot_in, live_in, small_in, in_in, out_in, gate_in, up_in, down_in,
    y_out, dx_out, gu_full, down_full, in_full, out_full, small_out,
    all_gu, all_down, all_in, all_out, spill_p, spill_h, spill_t,
    h0g, h0d, h1g, h1d, hyg, hyd, h2g, h2d, hzg, hzd,
    act_a, act_b, tr, wgu, wd, outv, dnv, acts, wout, zv, take,
    ub, vb, hal, uh, kh, ks, chd, hf, smallv, vec, conv_acc, sg, sg_all, sg_mine, sg_parts,
    ggu, gd, vag, vad, s1g, s1d, og, y1g, y1d, yrg, yrd, z2g, z2d, zrg, zrd, fing, find,
    sem_in, sem_load, sem_own, sem_pair, sem_half, sem_n2, sem_sums, sem_dm, sem_small, sem_edge, sem_kh, sem_spill,
    ag_cross, ag_x, mg_cross, mg_x, ag_far, ag_z, ag_y, ag_dz, ag_dy, ag_send, ag_relay, ag_dsend, ag_drelay,
    mg_own, mg_z, mg_y, mg_oz, mg_oy, mg_send, mg_relay, mg_osend, mg_orelay,
    ra_g, ra_d, sa_g, sa_d, ld0, st1, ry_g, ry_d, sy_g, sy_d, ld1, st2, rz_g, rz_d, sz_g, sz_d, ld2, st3,
    fs_g, fs_i, fs_d, fs_o, fr_g, fr_i, fr_d, fr_o, sem_sum,
):
    nx, nz, ny, seqs, span, width, hidden = sizes
    n = nz * ny
    rows = seqs * span
    dn = width // n
    dnx = dn // nx
    half = hidden // 2
    chan = width // 2
    steps = half // CHUNK
    chunks = steps + 3
    per_half = half // BLOCK // 2
    own_rows = hidden // n
    gp = min(BLOCK, own_rows & -own_rows)
    pieces = CHUNK // gp
    lanes = width // nx
    slots = 3
    tiles = rows // TILE
    tseq = TILE // span
    x, c = lax.axis_index("x"), lax.axis_index("core")
    z, y = lax.axis_index("z"), lax.axis_index("y")
    me = z * ny + y
    in_half = me // (n // 2) == c

    def at(x=x, c=c, z=z, y=y):
        return (x, c, z, y)

    def member(j, c=c):
        return at(c=c, z=j // ny, y=j % ny)

    def zp(d):
        return lax.rem(z + d, nz)

    def yp(d):
        return lax.rem(y + d, ny)

    def xp(d):
        return lax.rem(x + d, nx)

    def remote(src, dst, ssem, rsem, dev):
        return pltpu.make_async_remote_copy(
            src_ref=src, dst_ref=dst, send_sem=ssem, recv_sem=rsem, device_id=dev, device_id_type=MESH
        )

    def local(src, dst, sem):
        return pltpu.make_async_copy(src, dst, sem)

    def landed(ref, sem):
        pltpu.make_async_copy(ref, ref, sem).wait()

    def span_of(start, size, align):
        return pl.ds(pl.multiple_of(start, align), size)

    mine = span_of(c * rows, rows, rows)
    other = span_of((1 - c) * rows, rows, rows)

    barrier = pltpu.get_barrier_semaphore()
    peers = [member(lax.rem(me + d, n)) for d in range(1, n)]
    reps = [(d, e) for d in range(nx) for e in range(2) if d + e > 0]
    peers += [at(x=xp(d), c=lax.rem(c + e, 2)) for d, e in reps]
    peers += [member(lax.rem(me + d, n), c=1 - c) for d in (1, n - 1)]
    for dev in peers:
        pl.semaphore_signal(barrier, inc=1, device_id=dev, device_id_type=MESH)
    pl.semaphore_wait(barrier, len(peers))

    local(small_in, smallv.at[me], sem_small.at[0]).start()
    for d in range(1, n):
        remote(small_in, smallv.at[me], sem_small.at[1], sem_small.at[2], member(lax.rem(me + d, n))).start()

    @pl.when(me < n - 1)
    def _():
        for e in range(2):
            dev = member(lax.rem(me + 1, n), c=lax.rem(c + e, 2))
            remote(edge_in, hal.at[c], sem_edge.at[e], sem_edge.at[2 + c], dev).start()

    local(tok_in, act_a.at[mine], sem_in.at[0]).start()
    local(cot_in, take.at[1], sem_in.at[1]).start()
    remote(tok_in, act_a.at[mine], sem_pair.at[0], sem_pair.at[1], at(c=1 - c)).start()

    ag_peers = [(0, d) for d in range(1, nz)] + [(1, d) for d in range(1, ny)]

    def toward(ax, d):
        return at(z=zp(d)) if ax == 0 else at(y=yp(d))

    def mixer_first_hop(b):
        here = in_in.at[:, span_of((b // 2) * width + c * chan + (b % 2) * CHUNK, CHUNK, CHUNK)]
        there = all_in.at[b, z, y]
        local(here, there, mg_own.at[0]).start()
        hops(here, there, mg_send, lambda d: mg_z.at[b, d - 1], lambda d: mg_y.at[b, d - 1], b % 2)

    def out_first_hop():
        @pl.when(in_half)
        def _():
            o = me - c * (n // 2)
            local(out_in, all_out.at[o], mg_own.at[1]).start()
            hops(out_in, all_out.at[o], mg_osend, lambda d: mg_oz.at[o], lambda d: mg_oy.at[o])

    def off(zs):
        return (zs - z) * (zs - z)

    inner = jnp.logical_and(z > 0, z < nz - 1)
    end = jnp.where(z == 1, 0, nz - 1)
    end_slot = jnp.where(z == 1, 0, nz - 2)

    plane = x % 2
    partner = x + 1 - 2 * plane

    def hops(here, there, send, recv_z, recv_y, only=None):
        for p, (ax, d) in enumerate(ag_peers):
            if ax == 1:

                @pl.when(True if only is None else plane == only)
                def _():
                    remote(here, there, send.at[p], recv_y(d), toward(ax, d)).start()
            elif d in (1, nz - 1):

                @pl.when(off(zp(d)) < (nz - 1) ** 2)
                def _():
                    remote(here, there, send.at[p], recv_z(d), toward(ax, d)).start()
            else:
                remote(here, there, send.at[p], recv_z(d), toward(ax, d)).start()

    def out_owner(o):
        j = c * (n // 2) + o
        return j // ny, j % ny

    def along_y(block, send, recv):
        for e in range(1, ny):
            remote(block, block, send.at[e - 1], recv(e), at(y=yp(e))).start()

    def along(block, part, wanted, d, near, arrived, far_send, far_recv, y_send, y_recv):
        if d in (1, nz - 1):
            this = off(lax.rem(z - d + nz, nz)) == (nz - 1) ** 2

            @pl.when(jnp.logical_not(this) if near else this)
            def _():
                landed(block, arrived)

                @pl.when(wanted)
                def _():
                    along_y(part, y_send, y_recv)
        elif near:
            landed(block, arrived)

            @pl.when(inner)
            def _():
                remote(block, block, far_send, far_recv, at(z=end)).start()

            @pl.when(wanted)
            def _():
                along_y(part, y_send, y_recv)

    def mixer_cross(b):
        @pl.when(plane == b % 2)
        def _():
            for e in range(1, ny):
                block = all_in.at[b, :, lax.rem(y - e + ny, ny)]
                landed(block, mg_y.at[b, e - 1])
                remote(block, block, mg_cross.at[e - 1], mg_x.at[b, e - 1], at(x=partner)).start()

    def mixer_hop(b, near):
        for d in range(1, nz):
            block = all_in.at[b, lax.rem(z - d + nz, nz), y]
            along(
                block, block, plane == b % 2, d, near, mg_z.at[b, d - 1], ag_far.at[0], mg_z.at[b, end_slot], mg_relay.at[d - 1], lambda e: mg_y.at[b, e - 1]
            )

    def owned(block, zo, near, arrived, far_send, y_send, y_recv):
        @pl.when(off(zo) < (nz - 1) ** 2 if near else off(zo) == (nz - 1) ** 2)
        def _():
            landed(block, arrived)

            @pl.when(jnp.logical_and(inner, off(zo) == 4))
            def _():
                remote(block, block, far_send, arrived, at(z=end)).start()

            along_y(block, y_send, y_recv)

    def out_hop(near):
        for o in range(n // 2):
            zo, yo = out_owner(o)

            @pl.when(jnp.logical_and(zo != z, yo == y))
            def _():
                owned(all_out.at[o], zo, near, mg_oz.at[o], ag_far.at[1], mg_orelay.at[o], lambda e: mg_oy.at[o])

    def mixer_arrived():
        for e in range(1, ny):
            for b in range(6):

                @pl.when(plane != b % 2)
                def _():
                    landed(all_in.at[b, :, lax.rem(y - e + ny, ny)], mg_x.at[b, e - 1])
        for o in range(n // 2):
            _, yo = out_owner(o)

            @pl.when(yo != y)
            def _():
                landed(all_out.at[o], mg_oy.at[o])

        landed(all_in.at[:, 0, 0], mg_own.at[0])

        @pl.when(in_half)
        def _():
            landed(all_out.at[0], mg_own.at[1])

    def mixer_load():
        copies = [local(all_in, acts, sem_load.at[0])]
        copies += [local(all_out.at[o], wout.at[pl.ds(o * dn, dn)], sem_load.at[2 + o]) for o in range(n // 2)]
        for copy in copies:
            copy.start()
        for copy in copies:
            copy.wait()

    def blocks(m):
        h, i = m % 2, m // 2
        first = per_half * h + i
        return first, per_half * h + per_half - 1 - i + per_half * (m // (2 * (per_half // 2)))

    def column(b):
        return pl.multiple_of(c * half + b * BLOCK, BLOCK)

    def owner(m, q):
        b = blocks(m)[q * gp // BLOCK]
        row = c * half + b * BLOCK + (q * gp) % BLOCK
        j = row // own_rows
        return j // ny, j % ny, pl.multiple_of(row - j * own_rows, gp)

    def grad_owner(m, q):
        zo, yo, row = owner(jnp.minimum(m, steps - 1), q)
        mixed = c * chan + jnp.maximum(m - steps, 0) * CHUNK + q * gp
        j = mixed // dn
        late = m >= steps
        return (
            jnp.where(late, j // ny, zo),
            jnp.where(late, j % ny, yo),
            pl.multiple_of(jnp.where(late, mixed - j * dn, row), gp),
        )

    def first_hop(m, shared=False):
        b = blocks(m)
        for k in range(2):
            for w, src in enumerate((gate_in, up_in)):
                here = src.at[:, pl.ds(column(b[k]), BLOCK)]
                there = all_gu.at[m, w, z, y, :, pl.ds(k * BLOCK, BLOCK)]
                local(here, there, sem_own.at[0, m]).start()
                hops(here, there, ag_send, lambda d: ag_z.at[m, d - 1], lambda d: ag_y.at[m, d - 1], k if shared else None)
        for q in range(pieces):
            zo, yo, row = owner(m, q)

            @pl.when(jnp.logical_and(zo == z, yo == y))
            def _():
                here = down_in.at[pl.ds(row, gp)]
                there = all_down.at[m, pl.ds(q * gp, gp)]
                local(here, there, sem_own.at[1, m * pieces + q]).start()
                hops(here, there, ag_dsend, lambda d: ag_dz.at[m, q], lambda d: ag_dy.at[m, q])

    def half_of(m, ys, side):
        return all_gu.at[m, :, :, ys, :, span_of(side * BLOCK, BLOCK, BLOCK)]

    def cross(m):
        for e in range(1, ny):
            block = half_of(m, lax.rem(y - e + ny, ny), plane)
            landed(block, ag_y.at[m, e - 1])
            remote(block, block, ag_cross.at[e - 1], ag_x.at[m, e - 1], at(x=partner)).start()

    def next_hop(m, near, shared=False):
        for d in range(1, nz):
            zs = lax.rem(z - d + nz, nz)
            block = all_gu.at[m, :, zs, y]
            part = all_gu.at[m, :, zs, y, :, span_of(plane * BLOCK, BLOCK, BLOCK)] if shared else block
            along(
                block, part, True, d, near, ag_z.at[m, d - 1], ag_far.at[2], ag_z.at[m, end_slot], ag_relay.at[d - 1], lambda e: ag_y.at[m, e - 1]
            )
        for q in range(pieces):
            zo, yo, _ = owner(m, q)

            @pl.when(jnp.logical_and(zo != z, yo == y))
            def _():
                block = all_down.at[m, pl.ds(q * gp, gp)]
                owned(block, zo, near, ag_dz.at[m, q], ag_far.at[3], ag_drelay.at[zo % 2], lambda e: ag_dy.at[m, q])

    def arrived_shared(m):
        for e in range(1, ny):
            landed(half_of(m, lax.rem(y - e + ny, ny), 1 - plane), ag_x.at[m, e - 1])

    def arrived(m):
        for e in range(1, ny):
            landed(all_gu.at[m, :, :, lax.rem(y - e + ny, ny)], ag_y.at[m, e - 1])

    def load(m):
        landed(all_gu.at[m, :, 0, 0], sem_own.at[0, m])
        for q in range(pieces):
            zo, yo, _ = owner(m, q)
            block = all_down.at[m, pl.ds(q * gp, gp)]

            @pl.when(jnp.logical_and(zo == z, yo == y))
            def _():
                landed(block, sem_own.at[1, m * pieces + q])

            @pl.when(yo != y)
            def _():
                landed(block, ag_dy.at[m, q])

        local(all_gu.at[m], wgu, sem_load.at[0]).start()
        local(all_down.at[m], wd, sem_load.at[1]).start()

    def loaded_weights():
        landed(wgu, sem_load.at[0])
        landed(wd, sem_load.at[1])

    def pass_on(m):
        @pl.when(m < steps)
        def _():
            next_hop(m, True)

    def pass_on_far(m):
        @pl.when(m < steps)
        def _():
            next_hop(m, False)

        @pl.when(m + AHEAD - RELAY < steps)
        def _():
            first_hop(m + AHEAD - RELAY)

    for b in range(3):
        mixer_first_hop(b)

    local(cot_in, take.at[1], sem_in.at[1]).wait()

    @pl.loop(0, tiles)
    def _(t):
        rl = span_of(t * TILE, TILE, TILE)
        rs = span_of(c * rows + t * TILE, TILE, TILE)
        act_b[rs, :] = (take[1, rl, :].astype(F32) * live_in[rl, :]).astype(BF16)

    remote(act_b.at[mine], act_b.at[mine], sem_pair.at[2], sem_pair.at[3], at(c=1 - c)).start()

    landed(small_in, sem_small.at[0])
    landed(smallv.at[pl.ds(0, n - 1)], sem_small.at[1])
    landed(smallv.at[pl.ds(0, n - 1)], sem_small.at[2])
    for j in range(n):
        vec[:, j * dn : (j + 1) * dn] = smallv[j]

    @pl.when(me < n - 1)
    def _():
        for e in range(2):
            landed(hal.at[0], sem_edge.at[e])

    @pl.when(me > 0)
    def _():
        for e in range(2):
            landed(hal.at[e], sem_edge.at[2 + e])

    @pl.when(me == 0)
    def _():
        hal[...] = jnp.zeros_like(hal)

    for b in range(8):
        if b < 6:
            mixer_hop(b, True)
        if 0 < b < 7:
            mixer_hop(b - 1, False)
        if b < 3:
            mixer_first_hop(b + 3)
        elif b == 3:
            out_first_hop()
        elif b > 5:
            out_hop(b == 6)
            first_hop(b - 6, True)
        if b > 1:
            mixer_cross(b - 2)
    local(tok_in, act_a.at[mine], sem_in.at[0]).wait()
    landed(act_a.at[mine], sem_pair.at[0])
    landed(act_a.at[other], sem_pair.at[1])
    local(act_a.at[other], spill_t, sem_spill.at[6]).start()
    mixer_arrived()
    mixer_load()

    def win(b):
        return acts[b].reshape(width, CHUNK)

    def tap(k, h):
        return vec[2 + k : 3 + k, span_of(c * chan + h * CHUNK, CHUNK, CHUNK)].reshape(1, 1, CHUNK)

    def normed(tokens):
        return (tokens * row_scale(tokens) * vec[0:1, :]).astype(BF16)

    for cc in range(2):
        for k in range(2):
            edge = normed(hal[cc, k].astype(F32))
            for h in range(2):
                hl = slice(h * CHUNK, (h + 1) * CHUNK)
                uh[k, cc * seqs : (cc + 1) * seqs, hl] = dot(edge, win(h)) * dot(edge, win(4 + h))

    def convolve(product, first, h):
        for i in range(tseq):
            for k in range(2):
                row = EDGE - 2 + k
                ub[i, row : row + 1, :] = uh[k, pl.ds(first + i, 1), h * CHUNK : (h + 1) * CHUNK]
        ub[:, EDGE:, :] = product.reshape(tseq, span, CHUNK)
        lag_two = ub[:, EDGE - 2 : EDGE - 2 + span, :]
        lag_one = ub[:, EDGE - 1 : EDGE - 1 + span, :]
        lag_none = ub[:, EDGE:, :]
        return lag_two, lag_one, lag_none, tap(0, h) * lag_two + tap(1, h) * lag_one + tap(2, h) * lag_none

    def spilled(t, i, rs):
        slot = t % 2
        src = dnv.at[span_of(slot * 3 * TILE + i * TILE, TILE, TILE), pl.ds(0, chan)]
        return local(src, spill_p.at[i, rs], sem_spill.at[slot * 3 + i])

    def tile_start(t):
        return lax.rem(t + (1 - c) * tiles, 2 * tiles) * TILE

    @pl.loop(0, 2 * tiles)
    def _(t):
        start = tile_start(t)
        rs = span_of(start, TILE, TILE)
        first = start // span
        tokens = act_a[rs, :].astype(F32)
        n1 = normed(tokens)

        @pl.when(t >= 2)
        def _():
            for i in range(3):
                spilled(t, i, rs).wait()

        for h in range(2):
            parts = [dot(n1, win(2 * i + h)) for i in range(3)]
            hl = pl.ds(h * CHUNK, CHUNK)
            for i in range(3):
                dnv[span_of((t % 2) * 3 * TILE + i * TILE, TILE, TILE), hl] = parts[i]
            for i in range(tseq):
                for k in range(2):
                    chd[k, pl.ds(first + i, 1), hl] = parts[1][i * span + k : i * span + k + 1, :]
            conv = convolve(parts[0] * parts[2], first, h)[3].reshape(TILE, CHUNK)
            zv[rs, hl] = (parts[1] * conv).astype(BF16)
        for i in range(3):
            spilled(t, i, rs).start()
        mixed = dot(zv[rs, :], wout[...])

        i = lax.rem(t, tiles)
        half_rows = span_of(i * TILE, TILE, TILE)

        @pl.when(t == 0)
        def _():
            landed(act_a.at[other], sem_spill.at[6])

        @pl.when(t < tiles)
        def _():
            tr[half_rows, other] = mixed.astype(BF16)
            remote(
                tr.at[half_rows, other], take.at[0, half_rows], sem_half.at[0, i], sem_half.at[1, i], at(c=1 - c)
            ).start()
            outv[rs, :] = jnp.zeros((TILE, width), F32)

        @pl.when(t >= tiles)
        def _():
            landed(take.at[0, half_rows], sem_half.at[1, i])
            middle = act_a[rs, :].astype(F32) + mixed + take[0, half_rows, :].astype(F32)
            outv[rs, :] = middle
            n2 = (middle * row_scale(middle) * vec[1:2, :]).astype(BF16)
            act_a[rs, :] = n2
            remote(act_a.at[rs], act_a.at[rs], sem_n2.at[0, i], sem_n2.at[1, i], at(c=1 - c)).start()
            tr[:, rs] = n2.T

        @pl.when(lax.rem(t, tiles) == 1)
        def _():
            next_hop(t // tiles, True, True)

        @pl.when(t == tiles + 1)
        def _():
            cross(0)

        @pl.when(lax.rem(t, tiles) == tiles - 1)
        def _():
            next_hop(t // tiles, False, True)
            first_hop(t // tiles + 2)


    for slot in range(2):
        for i in range(3):
            spilled(slot, i, pl.ds(0, TILE)).wait()
    local(outv.at[mine], spill_h, sem_spill.at[7]).start()
    cross(1)

    @pl.loop(0, tiles)
    def _(t):
        half_rows = span_of(t * TILE, TILE, TILE)
        rs = span_of(c * rows + t * TILE, TILE, TILE)
        ro = span_of((1 - c) * rows + t * TILE, TILE, TILE)
        dnv[ro, :] = jnp.zeros((TILE, width), F32)
        dnv[rs, :] = jnp.zeros((TILE, width), F32)
        landed(tr.at[half_rows, other], sem_half.at[0, t])

    @pl.loop(0, tiles)
    def _(t):
        rs = span_of(c * rows + t * TILE, TILE, TILE)
        ro = span_of((1 - c) * rows + t * TILE, TILE, TILE)
        landed(act_a.at[rs], sem_n2.at[0, t])
        landed(act_a.at[ro], sem_n2.at[1, t])
        tr[:, ro] = act_a[ro, :].T

    landed(act_b.at[other], sem_pair.at[3])
    landed(act_b.at[mine], sem_pair.at[2])
    local(outv.at[mine], spill_h, sem_spill.at[7]).wait()
    arrived_shared(0)
    load(0)
    loaded_weights()

    big = 512
    zb = big // (ny * dn)

    def hid(w):
        return acts[2 * w : 2 * w + 2].reshape(2 * rows, CHUNK)

    def compute(m):
        slot = m % slots

        @pl.loop(0, 2 * rows // big)
        def _(r):
            rs = span_of(r * big, big, big)
            gate = wgu[0].reshape(width, CHUNK)
            up = wgu[1].reshape(width, CHUNK)
            n2r = act_a[rs, :]
            g = dot(n2r, gate)
            v = dot(n2r, up)
            s = jax.nn.sigmoid(g)
            sg_ = g * s
            q = (sg_ * v).astype(BF16)
            dq = dot_nt(act_b[rs, :], wd[...])
            gg = (dq * v * s * (1.0 + g * (1.0 - s))).astype(BF16)
            gv = (dq * sg_).astype(BF16)
            zi = pl.ds((r % 2) * zb, zb)
            for w, value in enumerate((q, gg, gv)):
                acts[2 * w + r // 2, zi] = value.reshape(zb, ny, dn, CHUNK)
            outv[rs, :] += dot(q, wd[...])

            @pl.when(r == 1)
            def _():
                pass_on(m + RELAY)

            dnv[rs, :] += dot_nt(gg, gate) + dot_nt(gv, up)

        @pl.when(m == 0)
        def _():
            arrived_shared(1)

        @pl.when(jnp.logical_and(m >= 1, m + 1 < steps))
        def _():
            arrived(m + 1)

        @pl.when(m + 1 < steps)
        def _():
            load(m + 1)

        weight_grads(slot, hid(1), hid(2))
        for h in range(nx):
            gd[slot, h] = dot_tn(hid(0), act_b[:, pl.ds(h * lanes, lanes)]).astype(BF16)

    def weight_grads(slot, first, second):
        group = n // 2
        depth = width // 2

        @pl.loop(0, 2)
        def _(t):
            a = tr[span_of(t * depth, depth, depth), :]
            for w, src in enumerate((first, second)):
                full = dot(a, src).astype(BF16).reshape(group, nx, dnx, CHUNK)
                for h in range(nx):
                    for k in range(group):
                        j = t * group + k
                        ggu[slot, w, h, j // ny, j % ny] = full[k, h]

    def has_rows(m):
        return m < chunks - 1

    def send_x(m):
        slot = m % slots
        for d in range(1, nx):
            xo = xp(d)
            remote(ggu.at[slot, :, xo], h0g.at[m, d - 1], sa_g.at[slot], ra_g.at[m], at(x=xo)).start()

            @pl.when(has_rows(m))
            def _():
                remote(gd.at[slot, xo], h0d.at[m, d - 1], sa_d.at[slot], ra_d.at[m], at(x=xo)).start()

    def fetch_x(m):
        landed(h0g.at[m], ra_g.at[m])
        local(h0g.at[m], vag, ld0.at[0]).start()

        @pl.when(has_rows(m))
        def _():
            landed(h0d.at[m], ra_d.at[m])
            local(h0d.at[m], vad, ld0.at[1]).start()

    def sum_x(m):
        slot = m % slots
        landed(h0g.at[m], sa_g.at[slot])
        landed(vag, ld0.at[0])

        @pl.loop(0, nz)
        def _(zi):
            for yi in range(ny):
                for w in range(2):
                    total = ggu[slot, w, x, zi, yi].astype(F32)
                    for d in range(1, nx):
                        total += vag[d - 1, w, zi, yi].astype(F32)
                    s1g[yi, w, zi] = total.astype(BF16)

        local(s1g, h1g.at[m], st1.at[0]).start()

        @pl.when(has_rows(m))
        def _():
            landed(h0d.at[m], sa_d.at[slot])
            landed(vad, ld0.at[1])
            total = gd[slot, x].astype(F32)
            for d in range(1, nx):
                total += vad[d - 1].astype(F32)
            s1d[...] = total.astype(BF16)
            copy = local(s1d, h1d.at[m], st1.at[1])
            copy.start()
            copy.wait()

        landed(s1g, st1.at[0])

    def send_y(m, _):
        for d in range(1, ny):
            yo = yp(d)
            remote(h1g.at[m, yo], hyg.at[m, d - 1], sy_g.at[m], ry_g.at[m], at(y=yo)).start()

        @pl.when(has_rows(m))
        def _():
            for q in range(pieces):
                _, yo, _ = grad_owner(m, q)
                part = pl.ds(q * gp, gp)

                @pl.when(yo != y)
                def _():
                    d = lax.rem(yo - y + ny, ny)
                    remote(h1d.at[m, part], hyd.at[m, d - 1, part], sy_d.at[m, q], ry_d.at[m, q], at(y=yo)).start()

    def y_copies(m, i):
        copies = [local(h1g.at[m, y], y1g.at[i], ld1.at[i, 0]), local(hyg.at[m], yrg.at[i], ld1.at[i, 1])]
        late = [local(h1d.at[m], y1d.at[i], ld1.at[i, 2]), local(hyd.at[m], yrd.at[i], ld1.at[i, 3])]
        return copies, late

    def fetch_y(m, i):
        landed(hyg.at[m], ry_g.at[m])
        copies, late = y_copies(m, i)
        for copy in copies:
            copy.start()

        @pl.when(m < chunks - 1)
        def _():
            for q in range(pieces):
                _, yo, _ = grad_owner(m, q)

                @pl.when(yo == y)
                def _():
                    landed(hyd.at[m, :, pl.ds(q * gp, gp)], ry_d.at[m, q])

            for copy in late:
                copy.start()

    def send_z(m, i):
        copies, late = y_copies(m, i)
        for copy in copies:
            copy.wait()
        for zi in range(nz):
            for w in range(2):
                total = y1g[i, w, zi].astype(F32)
                for d in range(1, ny):
                    total += yrg[i, d - 1, w, zi].astype(F32)
                s1g[0, w, zi] = total.astype(BF16)
        stores = [local(s1g.at[0], h2g.at[m], st2.at[0]), local(s1d, h2d.at[m], st2.at[1])]
        stores[0].start()

        @pl.when(m < chunks - 1)
        def _():
            for copy in late:
                copy.wait()
            total = y1d[i].astype(F32)
            for d in range(1, ny):
                total += yrd[i, d - 1].astype(F32)
            s1d[...] = total.astype(BF16)
            stores[1].start()
            stores[1].wait()

        stores[0].wait()
        for d in range(1, nz):
            zo = zp(d)
            remote(h2g.at[m, :, zo], hzg.at[m, d - 1], sz_g.at[m], rz_g.at[m], at(z=zo)).start()

        @pl.when(m < chunks - 1)
        def _():
            for q in range(pieces):
                zo, yo, _ = grad_owner(m, q)
                part = pl.ds(q * gp, gp)

                @pl.when(jnp.logical_and(yo == y, zo != z))
                def _():
                    d = lax.rem(zo - z + nz, nz)
                    remote(h2d.at[m, part], hzd.at[m, d - 1, part], sz_d.at[m, q], rz_d.at[m, q], at(z=zo)).start()

    def z_copies(m, i):
        copies = [local(h2g.at[m, :, z], z2g.at[i], ld2.at[i, 0]), local(hzg.at[m], zrg.at[i], ld2.at[i, 1])]
        late = [local(h2d.at[m], z2d.at[i], ld2.at[i, 2]), local(hzd.at[m], zrd.at[i], ld2.at[i, 3])]
        return copies, late

    def fetch_z(m, i):
        landed(hzg.at[m], rz_g.at[m])
        copies, late = z_copies(m, i)
        for copy in copies:
            copy.start()

        @pl.when(m < chunks - 1)
        def _():
            for q in range(pieces):
                zo, yo, _ = grad_owner(m, q)

                @pl.when(jnp.logical_and(yo == y, zo == z))
                def _():
                    landed(hzd.at[m, :, pl.ds(q * gp, gp)], rz_d.at[m, q])

            for copy in late:
                copy.start()

    def rep(p):
        d, e = reps[p]
        return at(x=xp(d), c=lax.rem(c + e, 2))

    direct_reps = [p for p, (d, e) in enumerate(reps) if d == 0 or e == 0]

    def spread(there, ssem, rsem):
        for p in direct_reps:
            remote(there, there, ssem.at[p], rsem.at[p], rep(p)).start()

    def own_gu(xs, cs):
        return gu_full.at[:, pl.ds(pl.multiple_of(xs * dnx, dnx), dnx), span_of(cs * half, half, BLOCK)]

    def own_in(xs, k):
        return in_full.at[
            pl.ds(pl.multiple_of(xs * dnx, dnx), dnx), span_of(k * width + c * chan, chan, chan)
        ]

    in_size = in_full.at[pl.ds(0, dnx), pl.ds(0, 3 * chan)]

    def own_lanes(ref, xs):
        return ref.at[:, span_of(xs * lanes, lanes, BLOCK)]

    def hand_over(mixer):
        for d in range(1, nx):
            p, q = reps.index((d, 0)), reps.index((d, 1))
            xs = lax.rem(x - d + nx, nx)
            sems = (fs_i, fr_i) if mixer else (fs_g, fr_g)
            landed(in_size if mixer else own_gu(xs, c), sems[1].at[p])
            for part in [own_in(xs, k) for k in range(3)] if mixer else [own_gu(xs, c)]:
                remote(part, part, sems[0].at[q], sems[1].at[q], at(c=1 - c)).start()

            @pl.when(in_half)
            def _():
                part = own_lanes(out_full if mixer else down_full, xs)
                landed(part, (fr_o if mixer else fr_d).at[p])
                remote(part, part, (fs_o if mixer else fs_d).at[q], (fr_o if mixer else fr_d).at[q], at(c=1 - c)).start()

    def finish(m, i):
        copies, late = z_copies(m, i)
        for copy in copies:
            copy.wait()
        for w in range(2):
            total = z2g[i, w].astype(F32)
            for d in range(1, nz):
                total += zrg[i, d - 1, w].astype(F32)
            fing[w] = total.astype(BF16)
        part_rows = pl.ds(pl.multiple_of(x * dnx, dnx), dnx)
        part_lanes = span_of(x * lanes, lanes, BLOCK)
        b = blocks(jnp.minimum(m, steps - 1))

        def gu_place(k):
            return gu_full.at[:, part_rows, span_of(c * half + b[k] * BLOCK, BLOCK, BLOCK)]

        def in_place(w):
            start = jnp.maximum(m - steps, 0) * width + c * chan + w * CHUNK
            return in_full.at[part_rows, span_of(start, CHUNK, CHUNK)]

        def owned_rows(do):
            @pl.when(m < chunks - 1)
            def _():
                for q in range(pieces):
                    zo, yo, row = grad_owner(m, q)

                    @pl.when(jnp.logical_and(yo == y, zo == z))
                    def _():
                        do(q, pl.ds(q * gp, gp), pl.ds(row, gp))

        @pl.when(m < steps)
        def _():
            for k in range(2):
                local(fing.at[:, :, pl.ds(k * BLOCK, BLOCK)], gu_place(k), st3.at[0]).start()

        @pl.when(m >= steps)
        def _():
            for w in range(2):
                local(fing.at[w], in_place(w), st3.at[0]).start()

        @pl.when(m < chunks - 1)
        def _():
            for copy in late:
                copy.wait()

        def add_rows(q, part, rows_at):
            total = z2d[i, part].astype(F32)
            for d in range(1, nz):
                total += zrd[i, d - 1, part].astype(F32)
            find[part] = total.astype(BF16)

            @pl.when(m < steps)
            def _():
                local(find.at[part], down_full.at[rows_at, part_lanes], st3.at[1 + q]).start()

            @pl.when(m >= steps)
            def _():
                local(find.at[part], out_full.at[rows_at, part_lanes], st3.at[1 + q]).start()

        def spread_rows(q, part, rows_at):
            landed(find.at[part], st3.at[1 + q])

            @pl.when(m < steps)
            def _():
                spread(down_full.at[rows_at, part_lanes], fs_d, fr_d)

            @pl.when(m >= steps)
            def _():
                spread(out_full.at[rows_at, part_lanes], fs_o, fr_o)

        owned_rows(add_rows)
        landed(fing, st3.at[0])

        @pl.when(m < steps)
        def _():
            for k in range(2):
                spread(gu_place(k), fs_g, fr_g)

        @pl.when(m >= steps)
        def _():
            for w in range(2):
                spread(in_place(w), fs_i, fr_i)

        owned_rows(spread_rows)

    def gone(m):
        return jnp.clip(jnp.minimum(m - 1, 2 * (m - HOLD)), 0, chunks)

    def two(m, do):
        for i in range(2):
            k = gone(m - 1) + i

            @pl.when(k < gone(m))
            def _():
                do(k, i)

    def own_rep():
        return x * 2 + c

    def sum_reps():
        local(sg, sg_all.at[own_rep()], sem_sum.at[0]).start()
        for p in range(len(reps)):
            remote(sg, sg_all.at[own_rep()], sem_sum.at[1], sem_sum.at[2], rep(p)).start()

    def sum_group():
        landed(sg, sem_sum.at[0])
        landed(sg_all.at[pl.ds(0, len(reps))], sem_sum.at[1])
        landed(sg_all.at[pl.ds(0, len(reps))], sem_sum.at[2])
        total = sg_all[0]
        for p in range(1, 2 * nx):
            total += sg_all[p]
        for j in range(n):
            sg_mine[j] = total[:, j * dn : (j + 1) * dn]
        local(sg_mine.at[me], sg_parts.at[me], sem_sum.at[3]).start()
        for d in range(1, n):
            j = lax.rem(me + d, n)
            remote(sg_mine.at[j], sg_parts.at[me], sem_sum.at[4], sem_sum.at[5], member(j)).start()

    def sum_last():
        landed(sg_mine.at[0], sem_sum.at[3])
        landed(sg_parts.at[pl.ds(0, n - 1)], sem_sum.at[4])
        landed(sg_parts.at[pl.ds(0, n - 1)], sem_sum.at[5])
        total = sg_parts[0]
        for j in range(1, n):
            total += sg_parts[j]
        smallv[0] = total
        local(smallv.at[0], small_out, sem_in.at[0]).start()

    def give_sums():
        @pl.loop(0, tiles)
        def _(t):
            rl = span_of(t * TILE, TILE, TILE)
            ro = span_of((1 - c) * rows + t * TILE, TILE, TILE)
            for i, src in enumerate((outv, dnv)):
                side = pl.ds(i * width, width)
                tr[rl, side] = src[ro, :].astype(BF16)
                remote(
                    tr.at[rl, side], take.at[i, rl], sem_sums.at[i, t], sem_sums.at[2 + i, t], at(c=1 - c)
                ).start()

        local(spill_h, outv.at[other], sem_spill.at[7]).start()
        local(tok_in, act_a.at[mine], sem_in.at[0]).start()
        local(spill_t, act_a.at[other], sem_spill.at[6]).start()

    def loaded(t, i):
        src = spill_p.at[i, span_of(t * TILE, TILE, TILE)]
        dst = dnv.at[span_of((1 - c) * rows + i * TILE, TILE, TILE), span_of((t % 2) * chan, chan, chan)]
        return local(src, dst, sem_spill.at[(t % 2) * 3 + i])

    def mixer_back():
        mixer_load()
        conv_acc[...] = jnp.zeros_like(conv_acc)
        sg[...] = jnp.zeros_like(sg)
        local(spill_h, outv.at[other], sem_spill.at[7]).wait()
        for i in range(3):
            loaded(0, i).start()

        @pl.loop(0, tiles)
        def _(t):
            rl = span_of(t * TILE, TILE, TILE)
            rs = span_of(c * rows + t * TILE, TILE, TILE)
            ro = span_of((1 - c) * rows + t * TILE, TILE, TILE)
            for i in range(2):
                landed(take.at[i, rl], sem_sums.at[2 + i, t])
                landed(take.at[i, rl], sem_sums.at[i, t])
            total = outv[rs, :] + take[0, rl, :].astype(F32)
            tr[rl, pl.ds(0, width)] = (total * live_in[rl, :]).astype(BF16)
            dn2 = dnv[rs, :] + take[1, rl, :].astype(F32)
            middle = outv[ro, :]
            scale = row_scale(middle)
            unit = middle * scale
            sg[1:2, :] += jnp.sum(dn2 * unit, axis=0, keepdims=True)
            d2 = dn2 * vec[1:2, :]
            back = scale * (d2 - unit * jnp.mean(d2 * unit, axis=-1, keepdims=True))
            back = act_b[rs, :].astype(F32) + back
            dnv[rs, :] = back
            act_b[rs, :] = back.astype(BF16)
            remote(act_b.at[rs], act_b.at[rs], sem_dm.at[0, t], sem_dm.at[1, t], at(c=1 - c)).start()

        out = local(tr.at[:, pl.ds(0, width)], y_out, sem_in.at[1])
        out.start()
        local(tok_in, act_a.at[mine], sem_in.at[0]).wait()
        local(spill_t, act_a.at[other], sem_spill.at[6]).wait()
        out.wait()

        @pl.loop(0, 2 * tiles)
        def _(t):
            rs = span_of(t * TILE, TILE, TILE)
            tr[:, rs] = normed(act_a[rs, :].astype(F32)).T

        @pl.loop(0, tiles)
        def _(t):
            landed(act_b.at[span_of(c * rows + t * TILE, TILE, TILE)], sem_dm.at[0, t])
            landed(act_b.at[span_of((1 - c) * rows + t * TILE, TILE, TILE)], sem_dm.at[1, t])

        for cc in range(2):

            @pl.loop(0, seqs)
            def _(s):
                head = act_b[span_of(cc * rows + s * span, EDGE, span), :].astype(F32)
                for k in range(2):
                    hf[k, pl.ds(s, 1), :] = head[k : k + 1, :]

            for k in range(2):
                own = slice(cc * seqs, (cc + 1) * seqs)
                ks[k, own, :] = dot_nt(hf[k].astype(BF16), wout[...]) * chd[k, own, :]

        @pl.when(me > 0)
        def _():
            remote(ks, kh, sem_kh.at[0], sem_kh.at[1], member(lax.rem(me + n - 1, n))).start()

        @pl.when(me == n - 1)
        def _():
            kh[...] = jnp.zeros_like(kh)

        for h in range(nx):
            side = pl.ds(h * lanes, lanes)
            gd[steps % slots, h] = dot_tn(zv[:, :CHUNK], act_b[:, side]).astype(BF16)
            og[h] = dot_tn(zv[:, CHUNK:], act_b[:, side]).astype(BF16)

        @pl.when(me < n - 1)
        def _():
            landed(kh, sem_kh.at[1])

        @pl.loop(0, 2 * tiles)
        def _(t):
            rs = span_of(t * TILE, TILE, TILE)
            first = t * tseq
            for i in range(3):
                loaded(t, i).wait()

            @pl.when(t + 1 < 2 * tiles)
            def _():
                for i in range(3):
                    loaded(t + 1, i).start()

            for h in range(2):
                hl = pl.ds(h * CHUNK, CHUNK)
                dz = dot_nt(act_b[rs, :], wout[hl, :]).reshape(tseq, span, CHUNK)
                b_gate, c_gate, x_value = (
                    dnv[
                        span_of((1 - c) * rows + i * TILE, TILE, TILE),
                        span_of((t % 2) * chan + h * CHUNK, CHUNK, CHUNK),
                    ].reshape(tseq, span, CHUNK)
                    for i in range(3)
                )
                *lags, conv = convolve((b_gate * x_value).reshape(TILE, CHUNK), first, h)
                dk = dz * c_gate
                for k in range(3):
                    conv_acc[k : k + 1, hl] += jnp.sum((dk * lags[k]).reshape(TILE, CHUNK), axis=0, keepdims=True)
                vb[:, :span, :] = dk
                for i in range(tseq):
                    for k in range(2):
                        vb[i, span + k : span + k + 1, :] = kh[k, pl.ds(first + i, 1), hl]
                du = tap(2, h) * dk + tap(1, h) * vb[:, 1 : 1 + span, :] + tap(0, h) * vb[:, 2 : 2 + span, :]
                act_a[rs, hl] = (du * x_value).astype(BF16).reshape(TILE, CHUNK)
                act_a[rs, pl.ds(chan + h * CHUNK, CHUNK)] = (dz * conv).astype(BF16).reshape(TILE, CHUNK)
                zv[rs, hl] = (du * b_gate).astype(BF16).reshape(TILE, CHUNK)

    def share_back():
        @pl.loop(0, 2 * tiles)
        def _(t):
            rs = span_of(tile_start(t), TILE, TILE)
            total = dot_nt(act_a[rs, :CHUNK], win(0))
            for b in range(1, 6):
                src = act_a[rs, b * CHUNK : (b + 1) * CHUNK] if b < 4 else zv[rs, (b - 4) * CHUNK : (b - 3) * CHUNK]
                total += dot_nt(src, win(b))

            @pl.when(t < tiles)
            def _():
                act_b[rs, :] = total.astype(BF16)

            @pl.when(t >= tiles)
            def _():
                outv[rs, :] = total

            @pl.when(t == tiles - 1)
            def _():
                remote(act_b.at[other], take.at[0], sem_pair.at[4], sem_pair.at[5], at(c=1 - c)).start()
                local(tok_in, act_b.at[mine], sem_in.at[0]).start()

    def finish_back():
        landed(take.at[0], sem_pair.at[5])
        local(tok_in, act_b.at[mine], sem_in.at[0]).wait()

        @pl.loop(0, tiles)
        def _(t):
            rl = span_of(t * TILE, TILE, TILE)
            rs = span_of(c * rows + t * TILE, TILE, TILE)
            tokens = act_b[rs, :].astype(F32)
            scale = row_scale(tokens)
            unit = tokens * scale
            dn1 = outv[rs, :] + take[0, rl, :].astype(F32)
            sg[0:1, :] += jnp.sum(dn1 * unit, axis=0, keepdims=True)
            d1 = dn1 * vec[0:1, :]
            back = dnv[rs, :] + scale * (d1 - unit * jnp.mean(d1 * unit, axis=-1, keepdims=True))
            take[1, rl, :] = (back * live_in[rl, :]).astype(BF16)

        local(take.at[1], dx_out, sem_in.at[1]).start()
        sg[2:5, span_of(c * chan, chan, chan)] = conv_acc[0:3, :]
        sum_reps()

    @pl.loop(0, chunks + 4)
    def _(m):
        @pl.when(m < steps)
        def _():
            compute(m)

        @pl.when(m == steps - 1)
        def _():
            give_sums()

        @pl.when(m == steps)
        def _():
            mixer_back()

        @pl.when(jnp.logical_and(m >= steps, m < chunks - 1))
        def _():
            b = (m - steps) * 2 * CHUNK
            weight_grads(
                m % slots, act_a[:, span_of(b, CHUNK, CHUNK)], act_a[:, span_of(b + CHUNK, CHUNK, CHUNK)]
            )

        @pl.when(m == steps + 1)
        def _():
            gd[(steps + 1) % slots] = og[...]

        @pl.when(m == chunks - 1)
        def _():
            weight_grads(m % slots, zv[:, :CHUNK], zv[:, CHUNK:])

        @pl.when(m < chunks)
        def _():
            send_x(m)

        @pl.when(jnp.logical_and(m >= 2, m < chunks + 2))
        def _():
            fetch_x(m - 2)

        two(m - 1, fetch_y)
        two(m - 2, fetch_z)
        pass_on_far(m + RELAY)

        @pl.when(jnp.logical_and(m >= 2, m < chunks + 2))
        def _():
            sum_x(m - 2)

        two(m, send_y)
        two(m - 1, send_z)
        two(m - 2, finish)

        @pl.when(m == steps + 1)
        def _():
            share_back()

        @pl.when(m == chunks - 1)
        def _():
            finish_back()

        @pl.when(m == chunks)
        def _():
            sum_group()

        @pl.when(m == chunks + 1)
        def _():
            sum_last()
            hand_over(False)

        @pl.when(m + 1 < steps)
        def _():
            loaded_weights()

    landed(take.at[1], sem_in.at[1])
    landed(smallv.at[0], sem_in.at[0])

    @pl.loop(0, chunks)
    def _(m):
        landed(hyg.at[m], sy_g.at[m])
        landed(hzg.at[m], sz_g.at[m])

        @pl.when(m < chunks - 1)
        def _():
            for q in range(pieces):
                zo, yo, _ = grad_owner(m, q)
                part = pl.ds(q * gp, gp)

                @pl.when(yo != y)
                def _():
                    landed(h1d.at[m, part], sy_d.at[m, q])

                @pl.when(jnp.logical_and(yo == y, zo != z))
                def _():
                    landed(h2d.at[m, part], sz_d.at[m, q])

    hand_over(True)
    for p in range(len(reps)):
        landed(own_gu(0, 0), fs_g.at[p])
        landed(in_size, fs_i.at[p])

        @pl.when(in_half)
        def _():
            landed(own_lanes(down_full, 0), fs_d.at[p])
            landed(own_lanes(out_full, 0), fs_o.at[p])
    landed(take.at[0], sem_pair.at[4])

    @pl.when(me > 0)
    def _():
        landed(ks, sem_kh.at[0])

    for p, (ax, d) in enumerate(ag_peers):
        direct = ax == 1 or off(zp(d)) < (nz - 1) ** 2

        @pl.when(direct)
        def _():
            landed(all_in.at[pl.ds(0, 3) if ax else pl.ds(0, 6), 0, 0], mg_send.at[p])
            landed(all_gu.at[pl.ds(0, steps - ax), :, 0, 0], ag_send.at[p])

        @pl.when(jnp.logical_and(direct, in_half))
        def _():
            landed(all_out.at[0], mg_osend.at[p])
            landed(all_down.at[:, pl.ds(0, gp)], ag_dsend.at[p])

    @pl.when(inner)
    def _():
        landed(all_in.at[:, 0, 0], ag_far.at[0])
        landed(all_gu.at[:, :, 0, 0], ag_far.at[2])

    @pl.when(z == jnp.where(c == 0, 2, 1))
    def _():
        landed(all_out.at[0], ag_far.at[1])
        landed(all_down.at[:, pl.ds(0, gp)], ag_far.at[3])

    for d in range(1, nz):
        for e in range(1, ny):
            landed(all_in.at[pl.ds(0, 3), 0, 0], mg_relay.at[d - 1, e - 1])
            landed(all_gu.at[pl.ds(0, steps - 1), :, 0, 0], ag_relay.at[d - 1, e - 1])
    for e in range(1, ny):
        landed(all_in.at[pl.ds(0, 3), :, 0], mg_cross.at[e - 1])
        landed(all_gu.at[0, :, :, 0], ag_cross.at[e - 1])
    for o in range(n // 2):
        zo, yo = out_owner(o)

        @pl.when(jnp.logical_and(zo != z, yo == y))
        def _():
            for e in range(1, ny):
                landed(all_out.at[0], mg_orelay.at[o, e - 1])

    for k in range(2):
        zo = (n // 2 * c) // ny + k

        @pl.when(zo != z)
        def _():
            for e in range(1, ny):
                landed(all_down.at[:, pl.ds(0, gp)], ag_drelay.at[zo % 2, e - 1])

    for p, (d, e) in enumerate(reps):
        if d == 0 or e == 1:
            landed(own_gu(0, 0), fr_g.at[p])
            landed(in_size, fr_i.at[p])

            @pl.when(jnp.logical_not(in_half))
            def _():
                landed(own_lanes(down_full, 0), fr_d.at[p])
                landed(own_lanes(out_full, 0), fr_o.at[p])


def block_call(sizes, *operands):
    nx, nz, ny, seqs, span, width, hidden = sizes
    n = nz * ny
    rows = seqs * span
    dn = width // n
    dnx = dn // nx
    half = hidden // 2
    chan = width // 2
    steps = half // CHUNK
    own_rows = hidden // n
    gp = min(BLOCK, own_rows & -own_rows)
    pieces = CHUNK // gp
    lanes = width // nx
    chunks = steps + 3
    tseq = TILE // span
    tiles = rows // TILE
    reps = 2 * nx - 1
    hops = nz + ny - 2
    dma = lambda *dims: pltpu.SemaphoreType.DMA(dims)
    bf = lambda *dims: pltpu.VMEM(dims, BF16)
    fl = lambda *dims: pltpu.VMEM(dims, F32)
    anywhere = pl.BlockSpec(memory_space=pl.ANY)
    shape = jax.ShapeDtypeStruct
    specs = [anywhere] * 10
    specs[3] = pl.BlockSpec(memory_space=pltpu.VMEM)
    return pl.pallas_call(
        functools.partial(block_kernel, sizes),
        out_shape=[
            shape((rows, width), BF16),
            shape((rows, width), BF16),
            shape((2, dn, hidden), BF16),
            shape((own_rows, width), BF16),
            shape((dn, 3 * width), BF16),
            shape((dn, width), BF16),
            shape((8, dn), F32),
            shape((steps, 2, nz, ny, dn, CHUNK), BF16),
            shape((steps, CHUNK, width), BF16),
            shape((6, nz, ny, dn, CHUNK), BF16),
            shape((n // 2, dn, width), BF16),
            shape((3, 2 * rows, chan), F32),
            shape((rows, width), F32),
            shape((rows, width), BF16),
            shape((chunks, nx - 1, 2, nz, ny, dnx, CHUNK), BF16),
            shape((chunks, nx - 1, CHUNK, lanes), BF16),
            shape((chunks, ny, 2, nz, dnx, CHUNK), BF16),
            shape((chunks, CHUNK, lanes), BF16),
            shape((chunks, ny - 1, 2, nz, dnx, CHUNK), BF16),
            shape((chunks, ny - 1, CHUNK, lanes), BF16),
            shape((chunks, 2, nz, dnx, CHUNK), BF16),
            shape((chunks, CHUNK, lanes), BF16),
            shape((chunks, nz - 1, 2, dnx, CHUNK), BF16),
            shape((chunks, nz - 1, CHUNK, lanes), BF16),
        ],
        in_specs=specs,
        out_specs=[anywhere] * 24,
        scratch_shapes=[
            bf(2 * rows, width),
            bf(2 * rows, width),
            bf(width, 2 * rows),
            bf(2, nz, ny, dn, CHUNK),
            bf(CHUNK, width),
            fl(2 * rows, width),
            fl(2 * rows, width),
            bf(6, nz, ny, dn, CHUNK),
            bf(chan, width),
            bf(2 * rows, chan),
            bf(2, rows, width),
            fl(tseq, span + EDGE, CHUNK),
            fl(tseq, span + EDGE, CHUNK),
            bf(2, 2, seqs, width),
            fl(2, 2 * seqs, chan),
            fl(2, 2 * seqs, chan),
            fl(2, 2 * seqs, chan),
            fl(2, 2 * seqs, chan),
            fl(2, seqs, width),
            fl(n, 8, dn),
            fl(8, width),
            fl(8, chan),
            fl(8, width),
            fl(2 * nx, 8, width),
            fl(n, 8, dn),
            fl(n, 8, dn),
            bf(3, 2, nx, nz, ny, dnx, CHUNK),
            bf(3, nx, CHUNK, lanes),
            bf(nx - 1, 2, nz, ny, dnx, CHUNK),
            bf(nx - 1, CHUNK, lanes),
            bf(ny, 2, nz, dnx, CHUNK),
            bf(CHUNK, lanes),
            bf(nx, CHUNK, lanes),
            bf(2, 2, nz, dnx, CHUNK),
            bf(2, CHUNK, lanes),
            bf(2, ny - 1, 2, nz, dnx, CHUNK),
            bf(2, ny - 1, CHUNK, lanes),
            bf(2, 2, dnx, CHUNK),
            bf(2, CHUNK, lanes),
            bf(2, nz - 1, 2, dnx, CHUNK),
            bf(2, nz - 1, CHUNK, lanes),
            bf(2, dnx, CHUNK),
            bf(CHUNK, lanes),
            dma(2),
            dma(2 + n // 2),
            dma(2, steps * pieces),
            dma(6),
            dma(2, tiles),
            dma(2, tiles),
            dma(4, tiles),
            dma(2, tiles),
            dma(3),
            dma(4),
            dma(2),
            dma(8),
            dma(ny - 1),
            dma(SHARED, ny - 1),
            dma(ny - 1),
            dma(6, ny - 1),
            dma(4),
            dma(steps, nz - 1),
            dma(steps, ny - 1),
            dma(steps, pieces),
            dma(steps, pieces),
            dma(hops),
            dma(nz - 1, ny - 1),
            dma(hops),
            dma(2, ny - 1),
            dma(2),
            dma(6, nz - 1),
            dma(6, ny - 1),
            dma(n // 2),
            dma(n // 2),
            dma(hops),
            dma(nz - 1, ny - 1),
            dma(hops),
            dma(n // 2, ny - 1),
            dma(chunks),
            dma(chunks),
            dma(3),
            dma(3),
            dma(2),
            dma(2),
            dma(chunks),
            dma(chunks, pieces),
            dma(chunks),
            dma(chunks, pieces),
            dma(2, 4),
            dma(2),
            dma(chunks),
            dma(chunks, pieces),
            dma(chunks),
            dma(chunks, pieces),
            dma(2, 4),
            dma(1 + pieces),
            dma(reps),
            dma(reps),
            dma(reps),
            dma(reps),
            dma(reps),
            dma(reps),
            dma(reps),
            dma(reps),
            dma(6),
        ],
        compiler_params=pltpu.CompilerParams(
            collective_id=0, has_side_effects=True, vmem_limit_bytes=63 << 20
        ),
        name="gated_block",
    )(*operands)[:7]


def live_mask(lengths, deal, span):
    slots = jnp.arange(deal.shape[1], dtype=jnp.int32)
    picked = deal[0][:, None] == slots[None, :]
    source_len = jnp.sum(jnp.where(picked, lengths[0][:, None], 0), axis=0)
    position = lax.axis_index(GROUP) * span + jnp.arange(span, dtype=jnp.int32)
    return (position[None, :] < source_len[:, None]).astype(F32).reshape(-1, 1)


def body(
    tokens,
    cotangent,
    lengths,
    deal,
    norm_gain,
    in_weight,
    conv_weight,
    out_weight,
    ffn_gain,
    gate_weight,
    up_weight,
    down_weight,
):
    seqs, span, width = tokens.shape
    hidden = gate_weight.shape[1]
    nx, nz, ny = (lax.axis_size(axis) for axis in ("x", "z", "y"))
    dn = width // (nz * ny)
    small = jnp.stack([norm_gain, ffn_gain, *(conv_weight[:, k] for k in range(3))]).astype(F32)
    small = jnp.pad(small, ((0, 3), (0, 0)))
    block_out, block_grad, gu, down, mixer_in, mixer_out, sums = block_call(
        (nx, nz, ny, seqs, span, width, hidden),
        tokens.reshape(-1, width),
        tokens[:, span - 2 :].transpose(1, 0, 2),
        cotangent.reshape(-1, width),
        live_mask(lengths, deal, span),
        small,
        in_weight,
        out_weight,
        gate_weight,
        up_weight,
        down_weight,
    )
    return (
        block_out.reshape(tokens.shape),
        block_grad.reshape(tokens.shape),
        sums[0],
        mixer_in.astype(F32),
        sums[2:5].T,
        mixer_out.astype(F32),
        sums[1],
        gu[0].astype(F32),
        gu[1].astype(F32),
        down.astype(F32),
    )


def solution(mesh):
    rep, fsdp = mesh.shape["rep"], mesh.shape["fsdp"]
    grid = (rep // 2, 2, 4, fsdp // 4)
    split = Mesh(mesh.devices.reshape(grid), ("x", "core", "z", "y"))
    copies = ("x", "core")
    rows = P(copies, GROUP, None)
    lists = P(copies, None)
    vector = P(GROUP)
    matrix = P(GROUP, None)
    return jax.shard_map(
        body,
        mesh=split,
        in_specs=(
            rows,
            rows,
            lists,
            lists,
            vector,
            matrix,
            matrix,
            matrix,
            vector,
            matrix,
            matrix,
            matrix,
        ),
        out_specs=(rows, rows, vector, matrix, matrix, matrix, vector, matrix, matrix, matrix),
        check_vma=False,
    )
```
